32 devices in a mesh: groups: 1, rows: 16 (over z, y, core), cols: 2 (over x), sub: 1.
Axes of the slice: x: 2, y: 2, z: 4, core: 2. Of those that a mesh axis runs over, the one named last changes fastest.
Arguments:
- activations: bfloat16 [4096, 5376], P(('groups', 'rows'), ('cols', 'sub')), may hold values from -40 to 40
- positions: int32 [4096], P('groups'), may hold values from 0 to 6143, as said below
- query_weight: bfloat16 [5376, 4096], P('rows', ('cols', 'sub')), may hold values from -0.078125 to 0.078125
- key_weight: bfloat16 [5376, 2048], P('rows', ('cols', 'sub')), may hold values from -0.078125 to 0.078125
- value_weight: bfloat16 [5376, 2048], P('rows', ('cols', 'sub')), may hold values from -0.078125 to 0.078125
- output_weight: bfloat16 [4096, 5376], P(('cols', 'sub'), 'rows'), may hold values from -0.09375 to 0.09375
- input_gain: float32 [5376], replicated, may hold values from 0.1 to 1.9
- query_gain: float32 [128], replicated, may hold values from 0.1 to 1.9
- key_gain: float32 [128], replicated, may hold values from 0.1 to 1.9
Outputs:
- attended: bfloat16 [4096, 5376], P(('groups', 'rows'), ('cols', 'sub'))
The draws below stay inside these ranges and needn't reach their ends.
Inputs may be any that keep to these rules, and one draw needn't show every extreme that they name: `positions`: position of each token in its document: it rises by one from token to token, or falls to 0 where a new document begins; the first document may begin at any position.
All inputs are finite; a program needn't handle non-finite values.
Results may differ from the reference program's by a relative error of at most 0.0065.
Values may be sent and summed in bfloat16 or wider, within the bound.
No kernel may reach another device: no remote copies, remote signals or barrier semaphores. Data moves between devices by JAX's collectives and lax.ppermute only.
A program may use at most 128 MiB of HBM per device.

```python
import math
import jax
import jax.numpy as jnp
from jax import lax

D = 5376
HQ = 32
HK = 16
HD = 128
WINDOW = 1024
QUERY_SCALAR = 168
ROW_TOK = 256
SEQ = 4096
N_ROWS = 16
N_COLS = 2
N_SUB = 1


def draw_activations(key, part):
    data_key, row_key, column_key = jax.random.split(key, 3)
    values = jax.random.truncated_normal(data_key, -4.0, 4.0, (SEQ, D), jnp.float32)
    spread = 0.5
    row_scale = 10.0 ** jax.random.uniform(row_key, (SEQ, 1), jnp.float32, -spread, spread)
    column_scale = 10.0 ** jax.random.uniform(column_key, (1, D), jnp.float32, -0.5, 0.5)
    return (values * row_scale * column_scale).astype(jnp.bfloat16)


def draw_positions(key, part):
    mark_key, forced_key = jax.random.split(key, 2)
    indices = jnp.arange(SEQ, dtype=jnp.int32)
    marks = jax.random.randint(mark_key, (SEQ,), 0, 4 * WINDOW) == 0
    forced = jax.random.randint(forced_key, (), 1, SEQ)
    marks = (marks | (indices == forced)) & (indices > 0)
    latest = lax.cummax(jnp.where(marks, indices, 0), axis=0)
    first_mark = jnp.min(jnp.where(marks, indices, SEQ))
    offset = SEQ + 2 * WINDOW - first_mark
    return jnp.where(latest > 0, indices - latest, indices + offset).astype(jnp.int32)


def block_scale(stream_key, shape, shards, smallest, top_value):
    level, own = 1.0, jax.random.fold_in(stream_key, 6)
    for axis_at, parts in shards:
        steps = jnp.exp(jax.random.uniform(jax.random.fold_in(own, axis_at), (parts,), jnp.float32, smallest / len(shards), top_value / len(shards)))
        level = level * jnp.repeat(steps, shape[axis_at] // parts).reshape([-1 if axis == axis_at else 1 for axis in range(len(shape))])
    return level


def centred(stream_key, shape, deviation, reach, cuts=(), held_as=jnp.bfloat16):
    array = deviation * jax.random.normal(stream_key, shape, jnp.float32)
    if cuts:
        array = array * block_scale(stream_key, shape, cuts, -0.22, 0.18)
    return jnp.clip(array, -reach, reach).astype(held_as)


def setup_inputs(seed: int = 0, part: int = 0) -> dict:
    key_list = jax.random.split(jax.random.key(seed), 10)
    own_keys = jax.random.split(jax.random.fold_in(key_list[9], part), 10)
    return {
        "activations": draw_activations(jax.random.fold_in(jax.random.fold_in(key_list[9], part), 71), part),
        "positions": draw_positions(jax.random.fold_in(jax.random.fold_in(key_list[9], part), 71), part),
        "query_weight": centred(key_list[2], (D, HQ * HD), D ** -0.5, 0.078125, ((0, 16), (1, 2))),
        "key_weight": centred(key_list[3], (D, HK * HD), D ** -0.5, 0.078125, ((0, 16), (1, 2))),
        "value_weight": centred(key_list[4], (D, HK * HD), D ** -0.5, 0.078125, ((0, 16), (1, 2))),
        "output_weight": centred(key_list[5], (HQ * HD, D), (HQ * HD) ** -0.5, 0.09375, ((0, 2), (1, 16))),
        "input_gain": jnp.clip(1.0 + 0.18 * jax.random.normal(key_list[6], (D,), jnp.float32), 0.1, 1.9),
        "query_gain": jnp.clip(1.0 + 0.18 * jax.random.normal(key_list[7], (HD,), jnp.float32), 0.1, 1.9),
        "key_gain": jnp.clip(1.0 + 0.18 * jax.random.normal(key_list[8], (HD,), jnp.float32), 0.1, 1.9),
    }


def head_norm(tensor, gain_vector):
    return tensor * lax.rsqrt(lax.optimization_barrier(jnp.mean(tensor * tensor, axis=-1, keepdims=True)) + 1e-06) * gain_vector

def rotate(tensor, token_positions):
    half_width = tensor.shape[-1] // 2
    frequency = 10000.0 ** (-(jnp.arange(half_width, dtype=jnp.float32) * 2.0 / tensor.shape[-1]))
    angles = token_positions.astype(jnp.float32)[:, None] * frequency[None, :]
    cosine = jnp.cos(angles)[:, None, :]
    sine_part = jnp.sin(angles)[:, None, :]
    first_half = tensor[..., :half_width]
    second_half = tensor[..., half_width:]
    return jnp.concatenate([first_half * cosine - second_half * sine_part, second_half * cosine + first_half * sine_part], axis=-1)

def attend(queries, key_rows, value_rows, query_index, key_index, query_pos, key_pos):
    row_count = queries.shape[0]
    key_count = key_rows.shape[0]
    kv_heads = key_rows.shape[1] // HD
    group_size = queries.shape[1] // key_rows.shape[1]
    query_four = queries.astype(jnp.float32).reshape(row_count, kv_heads, group_size, HD)
    key_three = key_rows.astype(jnp.float32).reshape(key_count, kv_heads, HD)
    value_three = value_rows.astype(jnp.float32).reshape(key_count, kv_heads, HD)
    score_scale = 1.0 / math.sqrt(QUERY_SCALAR)
    scores = jnp.einsum('qgrd,kgd->grqk', query_four, key_three) * score_scale
    distance = query_index[:, None] - key_index[None, :]
    visible = (key_index[None, :] >= 0) & (distance >= 0) & (distance < WINDOW) & (query_pos[:, None] - key_pos[None, :] == distance)
    weights = jnp.where(visible[None, None], jnp.exp(scores), 0.0)
    totals = lax.optimization_barrier(jnp.sum(weights, axis=-1))
    rounded = lax.optimization_barrier(weights.astype(jnp.bfloat16))
    mixed_heads = jnp.einsum('grqk,kgd->qgrd', rounded.astype(jnp.float32), value_three)
    mixed_heads = mixed_heads / jnp.transpose(totals, (2, 0, 1))[..., None]
    return mixed_heads.astype(jnp.bfloat16).reshape(row_count, kv_heads * group_size * HD)

def reference(activations, positions, query_weight, key_weight, value_weight, output_weight, input_gain, query_gain, key_gain):
    widened = activations.astype(jnp.float32)
    inverse = lax.rsqrt(lax.optimization_barrier(jnp.mean(widened * widened, axis=-1, keepdims=True)) + 1e-06)
    normed = (widened * inverse * input_gain).astype(jnp.bfloat16)
    query_raw = jnp.dot(normed, query_weight, preferred_element_type=jnp.float32)
    key_raw = jnp.dot(normed, key_weight, preferred_element_type=jnp.float32)
    value_rows = jnp.dot(normed, value_weight, preferred_element_type=jnp.float32).astype(jnp.bfloat16)
    queries = rotate(head_norm(query_raw.reshape(SEQ, HQ, HD), query_gain), positions).astype(jnp.bfloat16).reshape(SEQ, HQ * HD)
    key_rows = rotate(head_norm(key_raw.reshape(SEQ, HK, HD), key_gain), positions).astype(jnp.bfloat16).reshape(SEQ, HK * HD)
    reach_rows = -(-WINDOW // ROW_TOK)
    margin = reach_rows * ROW_TOK
    key_padded = jnp.concatenate([jnp.zeros((margin, HK * HD), jnp.bfloat16), key_rows], axis=0)
    value_padded = jnp.concatenate([jnp.zeros((margin, HK * HD), jnp.bfloat16), value_rows], axis=0)
    position_padded = jnp.concatenate([jnp.zeros((margin,), jnp.int32), positions.astype(jnp.int32)], axis=0)

    def one_block(block_index):
        first_row = (block_index * ROW_TOK).astype(jnp.int32)
        query_block = lax.dynamic_slice_in_dim(queries, first_row, ROW_TOK, 0)
        key_block = lax.dynamic_slice_in_dim(key_padded, first_row, ROW_TOK + margin, 0)
        value_block = lax.dynamic_slice_in_dim(value_padded, first_row, ROW_TOK + margin, 0)
        query_pos = lax.dynamic_slice_in_dim(positions.astype(jnp.int32), first_row, ROW_TOK, 0)
        key_pos = lax.dynamic_slice_in_dim(position_padded, first_row, ROW_TOK + margin, 0)
        query_index = first_row + jnp.arange(ROW_TOK, dtype=jnp.int32)
        key_index = first_row - margin + jnp.arange(ROW_TOK + margin, dtype=jnp.int32)
        return attend(query_block, key_block, value_block, query_index, key_index, query_pos, key_pos)
    context = lax.map(one_block, jnp.arange(N_ROWS, dtype=jnp.int32)).reshape(SEQ, HQ * HD)
    groups_count = N_COLS * N_SUB
    group_width = HQ * HD // groups_count
    summed = widened
    for group in range(groups_count):
        lower = group * group_width
        upper = lower + group_width
        partial_sum = jnp.dot(context[:, lower:upper], output_weight[lower:upper], preferred_element_type=jnp.float32).astype(jnp.bfloat16)
        partial_sum = lax.optimization_barrier(partial_sum)
        summed = summed + partial_sum.astype(jnp.float32)
    return summed.astype(jnp.bfloat16)
```

```python
import functools
import math

import jax
import jax.numpy as jnp
from jax import lax
from jax.experimental import pallas as pl
from jax.experimental.pallas import tpu as pltpu
from jax.sharding import PartitionSpec as P

HD = 128
WINDOW = 1024
QUERY_SCALAR = 168
VMEM_BYTES = 67_000_000
AXES = ("rows", "cols", "sub")
ANY = pl.BlockSpec(memory_space=pl.ANY)
VMEM = pl.BlockSpec(memory_space=pltpu.VMEM)
SMEM = pl.BlockSpec(memory_space=pltpu.SMEM)


def passed_along(value, axis, by):
    peers = lax.axis_size(axis)
    pairs = [(i, i + by) for i in range(peers) if 0 <= i + by < peers]
    return lax.ppermute(value, axis, pairs)


def head_norm(tensor, gain_vector):
    return (
        tensor * lax.rsqrt(jnp.mean(tensor * tensor, axis=-1, keepdims=True) + 1e-06) * gain_vector
    )


def rotate(tensor, token_positions):
    half_width = tensor.shape[-1] // 2
    frequency = 10000.0 ** (-(jnp.arange(half_width, dtype=jnp.float32) * 2.0 / tensor.shape[-1]))
    angles = token_positions.astype(jnp.float32)[:, None] * frequency[None, :]
    cosine = jnp.cos(angles)[:, None, :]
    sine_part = jnp.sin(angles)[:, None, :]
    first_half = tensor[..., :half_width]
    second_half = tensor[..., half_width:]
    return jnp.concatenate(
        [
            first_half * cosine - second_half * sine_part,
            second_half * cosine + first_half * sine_part,
        ],
        axis=-1,
    )


def attend(queries, key_rows, value_rows, query_index, key_index, query_pos, key_pos):
    row_count = queries.shape[0]
    key_count = key_rows.shape[0]
    kv_heads = key_rows.shape[1] // HD
    group_size = queries.shape[1] // key_rows.shape[1]
    query_four = queries.reshape(row_count, kv_heads, group_size, HD)
    key_three = key_rows.reshape(key_count, kv_heads, HD)
    value_three = value_rows.reshape(key_count, kv_heads, HD)
    score_scale = 1.0 / math.sqrt(QUERY_SCALAR)
    scores = (
        jnp.einsum("qgrd,kgd->grqk", query_four, key_three, preferred_element_type=jnp.float32)
        * score_scale
    )
    distance = query_index[:, None] - key_index[None, :]
    visible = (
        (key_index[None, :] >= 0)
        & (distance >= 0)
        & (distance < WINDOW)
        & (query_pos[:, None] - key_pos[None, :] == distance)
    )
    weights = jnp.where(visible[None, None], jnp.exp(scores), 0.0)
    totals = jnp.sum(weights, axis=-1)
    rounded = weights.astype(jnp.bfloat16)
    mixed_heads = jnp.einsum(
        "grqk,kgd->qgrd", rounded, value_three, preferred_element_type=jnp.float32
    )
    mixed_heads = mixed_heads / jnp.transpose(totals, (2, 0, 1))[..., None]
    return mixed_heads.astype(jnp.bfloat16).reshape(row_count, kv_heads * group_size * HD)


def reach_back(key_rows, value_rows, reach_rows):
    pieces = []
    carried = (key_rows, value_rows)
    for distance in range(reach_rows):
        carried = passed_along((carried[0], carried[1]), "rows", 1)
        pieces.append(carried)
    ordered = pieces[::-1] + [(key_rows, value_rows)]
    all_keys = jnp.concatenate([member[0] for member in ordered], axis=0)
    all_values = jnp.concatenate([member[1] for member in ordered], axis=0)
    return (all_keys, all_values)


def gathered_body(
    activations,
    positions,
    query_weight,
    key_weight,
    value_weight,
    output_weight,
    input_gain,
    query_gain,
    key_gain,
):
    rows_here = activations.shape[0]
    row_panel = lax.all_gather(activations, ("cols", "sub"), axis=1, tiled=True)
    panel_wide = row_panel.astype(jnp.float32)
    inverse = lax.rsqrt(jnp.mean(panel_wide * panel_wide, axis=-1, keepdims=True) + 1e-06)
    normed = (panel_wide * inverse * input_gain).astype(jnp.bfloat16)
    row_index = lax.axis_index("rows")
    own_positions = lax.dynamic_slice_in_dim(positions, row_index * rows_here, rows_here, 0)
    reach_rows = min(-(-WINDOW // rows_here), lax.axis_size("rows") - 1)

    def add_rows(weight_piece):
        return jnp.dot(normed, weight_piece, preferred_element_type=jnp.float32)

    query_raw = add_rows(lax.all_gather(query_weight, "rows", axis=0, tiled=True))
    key_raw = add_rows(lax.all_gather(key_weight, "rows", axis=0, tiled=True))
    value_raw = add_rows(lax.all_gather(value_weight, "rows", axis=0, tiled=True))
    key_rows = rotate(head_norm(key_raw.reshape(rows_here, -1, HD), key_gain), own_positions)
    key_rows, value_rows = (
        key_rows.astype(jnp.bfloat16).reshape(rows_here, -1),
        value_raw.astype(jnp.bfloat16),
    )
    all_keys, all_values = reach_back(key_rows, value_rows, reach_rows)
    queries = rotate(head_norm(query_raw.reshape(rows_here, -1, HD), query_gain), own_positions)
    queries = queries.astype(jnp.bfloat16).reshape(rows_here, -1)
    key_count = all_keys.shape[0]
    query_index = row_index * rows_here + jnp.arange(rows_here, dtype=jnp.int32)
    key_index = (row_index - reach_rows) * rows_here + jnp.arange(key_count, dtype=jnp.int32)
    padded = jnp.concatenate([jnp.zeros((reach_rows * rows_here,), jnp.int32), positions], axis=0)
    key_positions = lax.dynamic_slice_in_dim(padded, row_index * rows_here, key_count, 0)
    context = attend(
        queries, all_keys, all_values, query_index, key_index, own_positions, key_positions
    )
    partial_terms = jnp.dot(
        context,
        lax.all_gather(output_weight, "rows", axis=1, tiled=True),
        preferred_element_type=jnp.float32,
    )
    summed = lax.psum_scatter(
        partial_terms.astype(jnp.bfloat16), ("cols", "sub"), scatter_dimension=1, tiled=True
    ).astype(jnp.float32)
    return (activations.astype(jnp.float32) + summed).astype(jnp.bfloat16)


def swapped(value, place=0, col=0, name="swap"):
    rows, cols = lax.axis_size("rows"), lax.axis_size("cols")
    pairs = [
        (r * cols + c, (r ^ place) * cols + (c ^ col)) for r in range(rows) for c in range(cols)
    ]
    with jax.named_scope(name):
        return lax.ppermute(value, AXES, pairs)


def run(kernel, out_shape, in_specs, out_specs, scratch, flops, bytes_moved, name):
    return pl.pallas_call(
        kernel,
        out_shape=out_shape,
        in_specs=in_specs,
        out_specs=out_specs,
        scratch_shapes=scratch,
        compiler_params=pltpu.CompilerParams(vmem_limit_bytes=VMEM_BYTES),
        cost_estimate=pl.CostEstimate(
            flops=int(flops), bytes_accessed=int(bytes_moved), transcendentals=0
        ),
        name=name,
    )


def cut_kernel(n, meta, wq, wk, wv, *outs):
    place = meta[0]
    wide_q = wq.shape[1] // n
    wide_k = wk.shape[1] // n
    for m in range(n):
        at = lax.bitwise_xor(place, m)
        cols_k = pl.ds(pl.multiple_of(at * wide_k, 128), wide_k)
        cols_q = pl.ds(pl.multiple_of(at * wide_q, 128), wide_q)
        outs[m][:, :wide_k] = wk[:, cols_k]
        outs[m][:, wide_k:] = wv[:, cols_k]
        outs[n + m][...] = wq[:, cols_q]


def load_all(n, meta, blocks, weights, block_mem, weight_mem, block_sem, weight_sem):
    place, half, col = meta[0], meta[1], meta[2]
    deep = weights[0].shape[0]
    copies = []
    for m in range(n):
        for far in range(2):
            owner = lax.bitwise_xor(place, m)
            rows = pl.ds(pl.multiple_of(owner * deep, 16), deep)
            copies.append(
                pltpu.make_async_copy(
                    weights[m * 2 + far],
                    weight_mem.at[lax.bitwise_xor(half, far), rows, :],
                    weight_sem.at[m * 2 + far],
                )
            )
    for copy in copies:
        copy.start()
    for m in range(n):
        for side in range(2):
            pltpu.make_async_copy(
                blocks[m * 2 + side], block_mem.at[m, side], block_sem.at[m, side]
            ).start()
    return copies


def project(m, meta, blocks, block_mem, weight_mem, block_sem):
    col = meta[2]
    for side in range(2):
        pltpu.make_async_copy(blocks[side], block_mem.at[m, side], block_sem.at[m, side]).wait()
    return jnp.dot(
        block_mem[m, 0], weight_mem[col], preferred_element_type=jnp.float32
    ) + jnp.dot(
        block_mem[m, 1], weight_mem[lax.bitwise_xor(col, 1)], preferred_element_type=jnp.float32
    )


def normed_rotated(raw, gain, cosine, sine):
    scaled = raw * lax.rsqrt(jnp.mean(raw * raw, axis=-1, keepdims=True) + 1e-06) * gain
    return scaled * cosine + pltpu.roll(scaled, HD // 2, 1) * sine


def key_kernel(n, reach, meta, cosine, sine, gain, *refs):
    blocks, weights = refs[: 2 * n], refs[2 * n : 4 * n]
    kv_out, tail_out, block_mem, weight_mem, block_sem, weight_sem = refs[4 * n :]
    copies = load_all(n, meta, blocks, weights, block_mem, weight_mem, block_sem, weight_sem)
    for copy in copies:
        copy.wait()
    place = meta[0]

    @pl.loop(0, n)
    def _(m):
        at = lax.bitwise_xor(place, m)
        raw = project(m, meta, blocks, block_mem, weight_mem, block_sem)
        keys = normed_rotated(raw[:, :HD], gain[...], cosine[at], sine[at]).astype(jnp.bfloat16)
        values = raw[:, HD:].astype(jnp.bfloat16)
        kv_out[m, :, :HD] = keys
        kv_out[m, :, HD:] = values

        @pl.when(at >= n - reach)
        def _():
            tail_out[at - (n - reach), :, :HD] = keys
            tail_out[at - (n - reach), :, HD:] = values


def attend_kernel(n, reach, heads, meta, cosine, sine, gain, q_doc, k_doc, kv_own, kv_back, *refs):
    blocks, weights = refs[: 2 * n], refs[2 * n : 4 * n]
    keep_out, send_out = refs[4 * n : 4 * n + 2]
    block_mem, weight_mem, kv_mem, block_sem, weight_sem, kv_sem = refs[4 * n + 2 :]
    place, col = meta[0], meta[2]
    tokens = block_mem.shape[2]
    part = tokens // 2
    copies = load_all(n, meta, blocks, weights, block_mem, weight_mem, block_sem, weight_sem)
    more = [pltpu.make_async_copy(kv_back, kv_mem.at[pl.ds(0, reach)], kv_sem.at[n])]
    for m in range(n):
        more.append(
            pltpu.make_async_copy(
                kv_own.at[m], kv_mem.at[reach + lax.bitwise_xor(place, m)], kv_sem.at[m]
            )
        )
    for copy in more:
        copy.start()
    for copy in copies + more:
        copy.wait()
    scale = 1.0 / math.sqrt(QUERY_SCALAR)
    row_at = lax.broadcasted_iota(jnp.int32, (tokens, tokens), 0)
    col_at = lax.broadcasted_iota(jnp.int32, (tokens, tokens), 1)

    @pl.loop(0, n)
    def _(m):
        at = lax.bitwise_xor(place, m)
        raw = project(m, meta, blocks, block_mem, weight_mem, block_sem)
        cosine_here, sine_here = cosine[at], sine[at]
        queries = [
            normed_rotated(
                raw[:, h * HD : (h + 1) * HD], gain[...], cosine_here, sine_here
            ).astype(jnp.bfloat16)
            for h in range(heads)
        ]
        doc = q_doc[at]
        totals = [jnp.zeros((tokens, 1), jnp.float32) for _ in range(heads)]
        mixed = [jnp.zeros((tokens, HD), jnp.float32) for _ in range(heads)]
        for step in range(reach + 1):
            pair = kv_mem[at + step]
            visible = doc == k_doc[at + step]
            if step == 0:
                visible = visible & (row_at < col_at)
            if step == reach:
                visible = visible & (row_at >= col_at)
            for h in range(heads):
                scores = lax.dot_general(
                    queries[h],
                    pair[:, :HD],
                    (((1,), (1,)), ((), ())),
                    preferred_element_type=jnp.float32,
                )
                weights_here = jnp.where(visible, jnp.exp(scores * scale), 0.0)
                totals[h] = totals[h] + jnp.sum(weights_here, axis=-1, keepdims=True)
                mixed[h] = mixed[h] + jnp.dot(
                    weights_here.astype(jnp.bfloat16),
                    pair[:, HD:],
                    preferred_element_type=jnp.float32,
                )
        for h in range(heads):
            done = (mixed[h] / totals[h]).astype(jnp.bfloat16)
            top, bottom = done[:part], done[part:]
            keep_out[at, :, h * HD : (h + 1) * HD] = jnp.where(col == 0, top, bottom)
            send_out[at, :, h * HD : (h + 1) * HD] = jnp.where(col == 0, bottom, top)


def output_kernel(n, meta, *refs):
    contexts, weights = refs[: 2 * n], refs[2 * n : 2 * n + 4]
    outs = refs[2 * n + 4 : 4 * n + 4]
    context_mem, weight_mem, result_mem, context_sem, weight_sem = refs[4 * n + 4 :]
    place, half, col = meta[0], meta[1], meta[2]
    deep = weights[0].shape[0]
    wide = contexts[0].shape[2]
    part = contexts[0].shape[1]
    copies = []
    for far in range(2):
        for side in range(2):
            rows = pl.ds(pl.multiple_of(lax.bitwise_xor(col, side) * deep, 16), deep)
            copies.append(
                pltpu.make_async_copy(
                    weights[far * 2 + side],
                    weight_mem.at[lax.bitwise_xor(half, far), rows, :],
                    weight_sem.at[far * 2 + side],
                )
            )
    for m in range(n):
        for side in range(2):
            first = lax.bitwise_xor(col, side) * deep + lax.bitwise_xor(place, m) * wide
            copies.append(
                pltpu.make_async_copy(
                    contexts[m * 2 + side],
                    context_mem.at[:, :, pl.ds(pl.multiple_of(first, 128), wide)],
                    context_sem.at[m * 2 + side],
                )
            )
    for copy in copies:
        copy.start()
    for copy in copies:
        copy.wait()

    @pl.loop(0, n // 2)
    def _(t):
        left = context_mem[pl.ds(2 * t, 2)].reshape(2 * part, 2 * deep)
        for block in range(2):
            result = jnp.dot(left, weight_mem[block], preferred_element_type=jnp.float32)
            result_mem[block, pl.ds(2 * t, 2)] = result.astype(jnp.bfloat16).reshape(2, part, -1)

    for m in range(n):
        for side in range(2):
            outs[m * 2 + side][...] = result_mem[
                lax.bitwise_xor(col, side), lax.bitwise_xor(place, m)
            ]


def split_body(
    activations,
    positions,
    query_weight,
    key_weight,
    value_weight,
    output_weight,
    input_gain,
    query_gain,
    key_gain,
):
    tokens, features = activations.shape
    n = key_weight.shape[1] // HD
    heads = query_weight.shape[1] // key_weight.shape[1]
    reach = WINDOW // tokens
    part = tokens // 2
    row = lax.axis_index("rows")
    col = lax.axis_index("cols")
    half, place = row // n, row % n
    meta = jnp.stack([place, half, col]).astype(jnp.int32)
    bf16, f32 = jnp.bfloat16, jnp.float32

    deep = query_weight.shape[0]
    pieces = run(
        functools.partial(cut_kernel, n),
        [jax.ShapeDtypeStruct((deep, 2 * HD), bf16)] * n
        + [jax.ShapeDtypeStruct((deep, heads * HD), bf16)] * n,
        [SMEM, VMEM, VMEM, VMEM],
        [VMEM] * (2 * n),
        [],
        0,
        4 * query_weight.size * 2,
        "cut",
    )(meta, query_weight, key_weight, value_weight)

    wide = activations.astype(f32)
    squares = jnp.sum(wide * wide, axis=-1).reshape(2, part)
    squares = (squares + swapped(squares, 0, 1, "squares")).reshape(tokens, 1)
    inverse = lax.rsqrt(squares / (2 * features) + 1e-06)
    gain = lax.dynamic_slice_in_dim(input_gain, col * features, features, 0)
    normed = (wide * inverse * gain).astype(bf16)

    z, y, c = n // 2, n // 4, 1
    blocks = {(0, 0): normed}
    blocks[z, 0] = swapped(normed, z, 0, "block_z")
    blocks[y, 0] = swapped(normed, y, 0, "block_y")
    blocks[0, 1] = swapped(normed, 0, 1, "block_x")
    blocks[z + y, 0] = swapped(blocks[z, 0], y, 0, "block_zy")
    blocks[z, 1] = swapped(blocks[z, 0], 0, 1, "block_zx")
    blocks[y, 1] = swapped(blocks[y, 0], 0, 1, "block_yx")
    blocks[z + y, 1] = swapped(blocks[z, 1], y, 0, "block_zxy")
    for m, side in list(blocks):
        blocks[m + c, side] = swapped(blocks[m, side], c, 0, f"block_c{m}{side}")
    block_list = [blocks[m, side] for m in range(n) for side in range(2)]

    def spread(mine, name):
        out = []
        for m in range(n):
            piece = mine[m] if m == 0 else swapped(mine[m], m, 0, f"{name}_{m}")
            out += [piece, swapped(piece, n, 0, f"{name}_far{m}")]
        return out

    kv_weights = spread(pieces[:n], "kv")
    q_weights = spread(pieces[n:], "q")

    in_half = lax.dynamic_slice_in_dim(positions, half * n * tokens, n * tokens, 0)
    frequency = 10000.0 ** (-(jnp.arange(HD // 2, dtype=f32) * 2.0 / HD))
    angles = in_half.astype(f32)[:, None] * frequency[None, :]
    cosine, sine = jnp.cos(angles), jnp.sin(angles)
    cosine = jnp.concatenate([cosine, cosine], -1).reshape(n, tokens, HD)
    sine = jnp.concatenate([-sine, sine], -1).reshape(n, tokens, HD)
    index = jnp.arange(positions.shape[0], dtype=jnp.int32)
    starts = jnp.concatenate(
        [jnp.full((reach * tokens,), -(2**30), jnp.int32), index - positions], 0
    )
    docs = lax.dynamic_slice_in_dim(starts, half * n * tokens, (n + reach) * tokens, 0)
    k_doc = docs.reshape(n + reach, 1, tokens)
    q_doc = docs[reach * tokens :].reshape(n, tokens, 1)

    block_bytes = 2 * n * tokens * features * 2
    stores = [
        pltpu.VMEM((n, 2, tokens, features), bf16),
        pltpu.VMEM((2, features, 2 * HD), bf16),
    ]
    sems = [pltpu.SemaphoreType.DMA((n, 2)), pltpu.SemaphoreType.DMA((2 * n,))]
    flops = 2 * n * tokens * 2 * features * 2 * HD
    kv_own, kv_tail = run(
        functools.partial(key_kernel, n, reach),
        [
            jax.ShapeDtypeStruct((n, tokens, 2 * HD), bf16),
            jax.ShapeDtypeStruct((reach, tokens, 2 * HD), bf16),
        ],
        [SMEM, VMEM, VMEM, VMEM] + [ANY] * (4 * n),
        [VMEM, VMEM],
        stores + sems,
        flops,
        block_bytes,
        "keys",
    )(meta, cosine, sine, key_gain.reshape(1, HD), *block_list, *kv_weights)
    with jax.named_scope("halo"):
        kv_back = passed_along(kv_tail, "rows", n)

    context_shape = jax.ShapeDtypeStruct((n, part, heads * HD), bf16)
    keep, send = run(
        functools.partial(attend_kernel, n, reach, heads),
        [context_shape, context_shape],
        [SMEM, VMEM, VMEM, VMEM, VMEM, VMEM, ANY, ANY] + [ANY] * (4 * n),
        [VMEM, VMEM],
        stores
        + [pltpu.VMEM((n + reach, tokens, 2 * HD), bf16)]
        + sems
        + [pltpu.SemaphoreType.DMA((n + 1,))],
        2 * flops,
        block_bytes,
        "attend",
    )(
        meta,
        cosine,
        sine,
        query_gain.reshape(1, HD),
        q_doc,
        k_doc,
        kv_own,
        kv_back,
        *block_list,
        *q_weights,
    )

    out_far = swapped(output_weight, n, 0, "out_far")
    out_weights = [
        output_weight,
        swapped(output_weight, 0, 1, "out_x"),
        out_far,
        swapped(out_far, 0, 1, "out_farx"),
    ]

    there = swapped(send, 0, 1, "context_x")
    contexts = {(0, 0): keep, (0, 1): there}
    contexts[z, 0] = swapped(keep, z, 0, "context_z")
    contexts[y, 0] = swapped(keep, y, 0, "context_y")
    contexts[z + y, 0] = swapped(contexts[z, 0], y, 0, "context_zy")
    contexts[z, 1] = swapped(there, z, 0, "context_xz")
    contexts[y, 1] = swapped(there, y, 0, "context_xy")
    contexts[z + y, 1] = swapped(contexts[y, 1], z, 0, "context_xyz")
    for m, side in list(contexts):
        contexts[m + c, side] = swapped(contexts[m, side], c, 0, f"context_c{m}{side}")
    context_list = [contexts[m, side] for m in range(n) for side in range(2)]

    out_cols = output_weight.shape[1]
    deep_out = output_weight.shape[0]
    results = run(
        functools.partial(output_kernel, n),
        [jax.ShapeDtypeStruct((part, out_cols), bf16)] * (2 * n),
        [SMEM] + [ANY] * (2 * n + 4),
        [VMEM] * (2 * n),
        [
            pltpu.VMEM((n, part, 2 * deep_out), bf16),
            pltpu.VMEM((2, 2 * deep_out, out_cols), bf16),
            pltpu.VMEM((2, n, part, out_cols), bf16),
            pltpu.SemaphoreType.DMA((2 * n,)),
            pltpu.SemaphoreType.DMA((4,)),
        ],
        2 * n * part * 2 * deep_out * 2 * out_cols,
        16 * deep_out * out_cols,
        "output",
    )(meta, *context_list, *out_weights)

    arrived = [
        [
            results[m * 2 + side]
            if (m, side) == (0, 0)
            else swapped(results[m * 2 + side], m, side, f"result_{m}{side}")
            for m in range(n)
        ]
        for side in range(2)
    ]
    lanes = []
    for side in range(2):
        ordered = arrived[side]
        bit = 1
        while bit < n:
            flip = (place & bit) != 0
            ordered = [jnp.where(flip, ordered[m ^ bit], ordered[m]) for m in range(n)]
            bit *= 2
        lanes.append(jnp.concatenate(ordered, axis=1))
    top = jnp.where(col == 0, lanes[0], lanes[1])
    bottom = jnp.where(col == 0, lanes[1], lanes[0])
    summed = jnp.concatenate([top, bottom], axis=0)
    return (wide + summed.astype(f32)).astype(bf16)


def fits(mesh, activations, key_weight):
    rows = mesh.shape["rows"]
    tokens = activations.shape[0] // (mesh.shape["groups"] * rows)
    splits = mesh.shape["cols"] * mesh.shape["sub"]
    n = key_weight.shape[1] // HD // splits
    return (
        mesh.shape["cols"] == 2
        and mesh.shape["sub"] == 1
        and n == 8
        and rows == 2 * n
        and WINDOW % tokens == 0
        and WINDOW // tokens <= n
        and tokens % 256 == 0
    )


def solution(mesh):
    placed = (
        P(("groups", "rows"), ("cols", "sub")),
        P("groups"),
        P("rows", ("cols", "sub")),
        P("rows", ("cols", "sub")),
        P("rows", ("cols", "sub")),
        P(("cols", "sub"), "rows"),
        P(),
        P(),
        P(),
    )

    def step(activations, positions, query_weight, key_weight, *rest):
        body = split_body if fits(mesh, activations, key_weight) else gathered_body
        return jax.shard_map(
            body,
            mesh=mesh,
            in_specs=placed,
            out_specs=P(("groups", "rows"), ("cols", "sub")),
            check_vma=False,
        )(activations, positions, query_weight, key_weight, *rest)

    return step
```

```python
import functools
import math

import jax
import jax.numpy as jnp
from jax import lax
from jax.experimental import pallas as pl
from jax.experimental.pallas import tpu as pltpu
from jax.sharding import PartitionSpec as P


HD = 128
WINDOW = 1024
QUERY_SCALAR = 168
VMEM_BYTES = 67_000_000
AXES = ("rows", "cols", "sub")
ANY = pl.BlockSpec(memory_space=pl.ANY)
VMEM = pl.BlockSpec(memory_space=pltpu.VMEM)
SMEM = pl.BlockSpec(memory_space=pltpu.SMEM)


def passed_along(value, axis, by):
    peers = lax.axis_size(axis)
    pairs = [(i, i + by) for i in range(peers) if 0 <= i + by < peers]
    return lax.ppermute(value, axis, pairs)


def head_norm(tensor, gain_vector):
    return (
        tensor * lax.rsqrt(jnp.mean(tensor * tensor, axis=-1, keepdims=True) + 1e-06) * gain_vector
    )


def rotate(tensor, token_positions):
    half_width = tensor.shape[-1] // 2
    frequency = 10000.0 ** (-(jnp.arange(half_width, dtype=jnp.float32) * 2.0 / tensor.shape[-1]))
    angles = token_positions.astype(jnp.float32)[:, None] * frequency[None, :]
    cosine = jnp.cos(angles)[:, None, :]
    sine_part = jnp.sin(angles)[:, None, :]
    first_half = tensor[..., :half_width]
    second_half = tensor[..., half_width:]
    return jnp.concatenate(
        [
            first_half * cosine - second_half * sine_part,
            second_half * cosine + first_half * sine_part,
        ],
        axis=-1,
    )


def attend(queries, key_rows, value_rows, query_index, key_index, query_pos, key_pos):
    row_count = queries.shape[0]
    key_count = key_rows.shape[0]
    kv_heads = key_rows.shape[1] // HD
    group_size = queries.shape[1] // key_rows.shape[1]
    query_four = queries.reshape(row_count, kv_heads, group_size, HD)
    key_three = key_rows.reshape(key_count, kv_heads, HD)
    value_three = value_rows.reshape(key_count, kv_heads, HD)
    score_scale = 1.0 / math.sqrt(QUERY_SCALAR)
    scores = (
        jnp.einsum("qgrd,kgd->grqk", query_four, key_three, preferred_element_type=jnp.float32)
        * score_scale
    )
    distance = query_index[:, None] - key_index[None, :]
    visible = (
        (key_index[None, :] >= 0)
        & (distance >= 0)
        & (distance < WINDOW)
        & (query_pos[:, None] - key_pos[None, :] == distance)
    )
    weights = jnp.where(visible[None, None], jnp.exp(scores), 0.0)
    totals = jnp.sum(weights, axis=-1)
    rounded = weights.astype(jnp.bfloat16)
    mixed_heads = jnp.einsum(
        "grqk,kgd->qgrd", rounded, value_three, preferred_element_type=jnp.float32
    )
    mixed_heads = mixed_heads / jnp.transpose(totals, (2, 0, 1))[..., None]
    return mixed_heads.astype(jnp.bfloat16).reshape(row_count, kv_heads * group_size * HD)


def reach_back(key_rows, value_rows, reach_rows):
    pieces = []
    carried = (key_rows, value_rows)
    for _ in range(reach_rows):
        carried = passed_along((carried[0], carried[1]), "rows", 1)
        pieces.append(carried)
    ordered = pieces[::-1] + [(key_rows, value_rows)]
    all_keys = jnp.concatenate([member[0] for member in ordered], axis=0)
    all_values = jnp.concatenate([member[1] for member in ordered], axis=0)
    return (all_keys, all_values)


def gathered_body(
    activations,
    positions,
    query_weight,
    key_weight,
    value_weight,
    output_weight,
    input_gain,
    query_gain,
    key_gain,
):
    rows_here = activations.shape[0]
    row_panel = lax.all_gather(activations, ("cols", "sub"), axis=1, tiled=True)
    panel_wide = row_panel.astype(jnp.float32)
    inverse = lax.rsqrt(jnp.mean(panel_wide * panel_wide, axis=-1, keepdims=True) + 1e-06)
    normed = (panel_wide * inverse * input_gain).astype(jnp.bfloat16)
    row_index = lax.axis_index("rows")
    own_positions = lax.dynamic_slice_in_dim(positions, row_index * rows_here, rows_here, 0)
    reach_rows = min(-(-WINDOW // rows_here), lax.axis_size("rows") - 1)

    def add_rows(weight_piece):
        return jnp.dot(normed, weight_piece, preferred_element_type=jnp.float32)

    query_raw = add_rows(lax.all_gather(query_weight, "rows", axis=0, tiled=True))
    key_raw = add_rows(lax.all_gather(key_weight, "rows", axis=0, tiled=True))
    value_raw = add_rows(lax.all_gather(value_weight, "rows", axis=0, tiled=True))
    key_rows = rotate(head_norm(key_raw.reshape(rows_here, -1, HD), key_gain), own_positions)
    key_rows, value_rows = (
        key_rows.astype(jnp.bfloat16).reshape(rows_here, -1),
        value_raw.astype(jnp.bfloat16),
    )
    all_keys, all_values = reach_back(key_rows, value_rows, reach_rows)
    queries = rotate(head_norm(query_raw.reshape(rows_here, -1, HD), query_gain), own_positions)
    queries = queries.astype(jnp.bfloat16).reshape(rows_here, -1)
    key_count = all_keys.shape[0]
    query_index = row_index * rows_here + jnp.arange(rows_here, dtype=jnp.int32)
    key_index = (row_index - reach_rows) * rows_here + jnp.arange(key_count, dtype=jnp.int32)
    padded = jnp.concatenate([jnp.zeros((reach_rows * rows_here,), jnp.int32), positions], axis=0)
    key_positions = lax.dynamic_slice_in_dim(padded, row_index * rows_here, key_count, 0)
    context = attend(
        queries, all_keys, all_values, query_index, key_index, own_positions, key_positions
    )
    partial_terms = jnp.dot(
        context,
        lax.all_gather(output_weight, "rows", axis=1, tiled=True),
        preferred_element_type=jnp.float32,
    )
    summed = lax.psum_scatter(
        partial_terms.astype(jnp.bfloat16), ("cols", "sub"), scatter_dimension=1, tiled=True
    ).astype(jnp.float32)
    return (activations.astype(jnp.float32) + summed).astype(jnp.bfloat16)


def swapped(value, place=0, col=0):
    rows, cols = lax.axis_size("rows"), lax.axis_size("cols")
    pairs = [
        (r * cols + c, (r ^ place) * cols + (c ^ col)) for r in range(rows) for c in range(cols)
    ]
    return lax.ppermute(value, AXES, pairs)


def run(kernel, out_shape, in_specs, out_specs, scratch, flops, bytes_moved):
    return pl.pallas_call(
        kernel,
        out_shape=out_shape,
        in_specs=in_specs,
        out_specs=out_specs,
        scratch_shapes=scratch,
        compiler_params=pltpu.CompilerParams(vmem_limit_bytes=VMEM_BYTES),
        cost_estimate=pl.CostEstimate(
            flops=int(flops), bytes_accessed=int(bytes_moved), transcendentals=0
        ),
    )


def cut_kernel(n, meta, wq, wk, wv, *outs):
    place = meta[0]
    wide_q = wq.shape[1] // n
    wide_k = wk.shape[1] // n
    for m in range(n):
        at = lax.bitwise_xor(place, m)
        cols_k = pl.ds(pl.multiple_of(at * wide_k, 128), wide_k)
        cols_q = pl.ds(pl.multiple_of(at * wide_q, 128), wide_q)
        outs[m][:, :wide_k] = wk[:, cols_k]
        outs[m][:, wide_k:] = wv[:, cols_k]
        outs[n + m][...] = wq[:, cols_q]


def load_all(n, meta, blocks, weights, block_mem, weight_mem, block_sem, weight_sem):
    place, half = meta[0], meta[1]
    deep = weights[0].shape[0]
    copies = []
    for m in range(n):
        for far in range(2):
            owner = lax.bitwise_xor(place, m)
            rows = pl.ds(pl.multiple_of(owner * deep, 16), deep)
            copies.append(
                pltpu.make_async_copy(
                    weights[m * 2 + far],
                    weight_mem.at[lax.bitwise_xor(half, far), rows, :],
                    weight_sem.at[m * 2 + far],
                )
            )
    for copy in copies:
        copy.start()
    for m in range(n):
        for side in range(2):
            pltpu.make_async_copy(
                blocks[m * 2 + side], block_mem.at[m, side], block_sem.at[m, side]
            ).start()
    return copies


def project(m, meta, blocks, block_mem, weight_mem, block_sem):
    col = meta[2]
    for side in range(2):
        pltpu.make_async_copy(blocks[side], block_mem.at[m, side], block_sem.at[m, side]).wait()
    return jnp.dot(
        block_mem[m, 0], weight_mem[col], preferred_element_type=jnp.float32
    ) + jnp.dot(
        block_mem[m, 1], weight_mem[lax.bitwise_xor(col, 1)], preferred_element_type=jnp.float32
    )


def normed_rotated(raw, gain, cosine, sine):
    scaled = raw * lax.rsqrt(jnp.mean(raw * raw, axis=-1, keepdims=True) + 1e-06) * gain
    return scaled * cosine + pltpu.roll(scaled, HD // 2, 1) * sine


def key_kernel(n, reach, meta, cosine, sine, gain, *refs):
    blocks, weights = refs[: 2 * n], refs[2 * n : 4 * n]
    kv_out, tail_out, block_mem, weight_mem, block_sem, weight_sem = refs[4 * n :]
    copies = load_all(n, meta, blocks, weights, block_mem, weight_mem, block_sem, weight_sem)
    for copy in copies:
        copy.wait()
    place = meta[0]

    @pl.loop(0, n)
    def _(m):
        at = lax.bitwise_xor(place, m)
        raw = project(m, meta, blocks, block_mem, weight_mem, block_sem)
        keys = normed_rotated(raw[:, :HD], gain[...], cosine[at], sine[at]).astype(jnp.bfloat16)
        values = raw[:, HD:].astype(jnp.bfloat16)
        kv_out[m, :, :HD] = keys
        kv_out[m, :, HD:] = values

        @pl.when(at >= n - reach)
        def _():
            tail_out[at - (n - reach), :, :HD] = keys
            tail_out[at - (n - reach), :, HD:] = values


def attend_kernel(n, reach, heads, meta, cosine, sine, gain, q_doc, k_doc, kv_own, kv_back, *refs):
    blocks, weights = refs[: 2 * n], refs[2 * n : 4 * n]
    keep_out, send_out = refs[4 * n : 4 * n + 2]
    block_mem, weight_mem, kv_mem, block_sem, weight_sem, kv_sem = refs[4 * n + 2 :]
    place, col = meta[0], meta[2]
    tokens = block_mem.shape[2]
    part = tokens // 2
    copies = load_all(n, meta, blocks, weights, block_mem, weight_mem, block_sem, weight_sem)
    more = [pltpu.make_async_copy(kv_back, kv_mem.at[pl.ds(0, reach)], kv_sem.at[n])]
    for m in range(n):
        more.append(
            pltpu.make_async_copy(
                kv_own.at[m], kv_mem.at[reach + lax.bitwise_xor(place, m)], kv_sem.at[m]
            )
        )
    for copy in more:
        copy.start()
    for copy in copies + more:
        copy.wait()
    scale = 1.0 / math.sqrt(QUERY_SCALAR)
    row_at = lax.broadcasted_iota(jnp.int32, (tokens, tokens), 0)
    col_at = lax.broadcasted_iota(jnp.int32, (tokens, tokens), 1)

    @pl.loop(0, n)
    def _(m):
        at = lax.bitwise_xor(place, m)
        raw = project(m, meta, blocks, block_mem, weight_mem, block_sem)
        cosine_here, sine_here = cosine[at], sine[at]
        queries = [
            normed_rotated(
                raw[:, h * HD : (h + 1) * HD], gain[...], cosine_here, sine_here
            ).astype(jnp.bfloat16)
            for h in range(heads)
        ]
        doc = q_doc[at]
        totals = [jnp.zeros((tokens, 1), jnp.float32) for _ in range(heads)]
        mixed = [jnp.zeros((tokens, HD), jnp.float32) for _ in range(heads)]
        for step in range(reach + 1):
            pair = kv_mem[at + step]
            visible = doc == k_doc[at + step]
            if step == 0:
                visible = visible & (row_at < col_at)
            if step == reach:
                visible = visible & (row_at >= col_at)
            for h in range(heads):
                scores = lax.dot_general(
                    queries[h],
                    pair[:, :HD],
                    (((1,), (1,)), ((), ())),
                    preferred_element_type=jnp.float32,
                )
                weights_here = jnp.where(visible, jnp.exp(scores * scale), 0.0)
                totals[h] = totals[h] + jnp.sum(weights_here, axis=-1, keepdims=True)
                mixed[h] = mixed[h] + jnp.dot(
                    weights_here.astype(jnp.bfloat16),
                    pair[:, HD:],
                    preferred_element_type=jnp.float32,
                )
        for h in range(heads):
            done = (mixed[h] / totals[h]).astype(jnp.bfloat16)
            top, bottom = done[:part], done[part:]
            keep_out[at, :, h * HD : (h + 1) * HD] = jnp.where(col == 0, top, bottom)
            send_out[at, :, h * HD : (h + 1) * HD] = jnp.where(col == 0, bottom, top)


def output_kernel(n, meta, *refs):
    contexts, weights = refs[: 2 * n], refs[2 * n : 2 * n + 4]
    outs = refs[2 * n + 4 : 4 * n + 4]
    context_mem, weight_mem, result_mem, context_sem, weight_sem = refs[4 * n + 4 :]
    place, half, col = meta[0], meta[1], meta[2]
    deep = weights[0].shape[0]
    wide = contexts[0].shape[2]
    part = contexts[0].shape[1]
    copies = []
    for far in range(2):
        for side in range(2):
            rows = pl.ds(pl.multiple_of(lax.bitwise_xor(col, side) * deep, 16), deep)
            copies.append(
                pltpu.make_async_copy(
                    weights[far * 2 + side],
                    weight_mem.at[lax.bitwise_xor(half, far), rows, :],
                    weight_sem.at[far * 2 + side],
                )
            )
    for m in range(n):
        for side in range(2):
            first = lax.bitwise_xor(col, side) * deep + lax.bitwise_xor(place, m) * wide
            copies.append(
                pltpu.make_async_copy(
                    contexts[m * 2 + side],
                    context_mem.at[:, :, pl.ds(pl.multiple_of(first, 128), wide)],
                    context_sem.at[m * 2 + side],
                )
            )
    for copy in copies:
        copy.start()
    for copy in copies:
        copy.wait()

    @pl.loop(0, n // 2)
    def _(t):
        left = context_mem[pl.ds(2 * t, 2)].reshape(2 * part, 2 * deep)
        for block in range(2):
            result = jnp.dot(left, weight_mem[block], preferred_element_type=jnp.float32)
            result_mem[block, pl.ds(2 * t, 2)] = result.astype(jnp.bfloat16).reshape(2, part, -1)

    for m in range(n):
        for side in range(2):
            outs[m * 2 + side][...] = result_mem[
                lax.bitwise_xor(col, side), lax.bitwise_xor(place, m)
            ]


def split_body(
    activations,
    positions,
    query_weight,
    key_weight,
    value_weight,
    output_weight,
    input_gain,
    query_gain,
    key_gain,
):
    tokens, features = activations.shape
    n = key_weight.shape[1] // HD
    heads = query_weight.shape[1] // key_weight.shape[1]
    reach = WINDOW // tokens
    part = tokens // 2
    row = lax.axis_index("rows")
    col = lax.axis_index("cols")
    half, place = row // n, row % n
    meta = jnp.stack([place, half, col]).astype(jnp.int32)
    bf16, f32 = jnp.bfloat16, jnp.float32

    deep = query_weight.shape[0]
    pieces = run(
        functools.partial(cut_kernel, n),
        [jax.ShapeDtypeStruct((deep, 2 * HD), bf16)] * n
        + [jax.ShapeDtypeStruct((deep, heads * HD), bf16)] * n,
        [SMEM, VMEM, VMEM, VMEM],
        [VMEM] * (2 * n),
        [],
        0,
        4 * query_weight.size * 2,
    )(meta, query_weight, key_weight, value_weight)

    wide = activations.astype(f32)
    squares = jnp.sum(wide * wide, axis=-1).reshape(2, part)
    squares = (squares + swapped(squares, 0, 1)).reshape(tokens, 1)
    inverse = lax.rsqrt(squares / (2 * features) + 1e-06)
    gain = lax.dynamic_slice_in_dim(input_gain, col * features, features, 0)
    normed = (wide * inverse * gain).astype(bf16)

    z, y, c = n // 2, n // 4, 1
    blocks = {(0, 0): normed}
    blocks[z, 0] = swapped(normed, z, 0)
    blocks[y, 0] = swapped(normed, y, 0)
    blocks[0, 1] = swapped(normed, 0, 1)
    blocks[z + y, 0] = swapped(blocks[z, 0], y, 0)
    blocks[z, 1] = swapped(blocks[z, 0], 0, 1)
    blocks[y, 1] = swapped(blocks[y, 0], 0, 1)
    blocks[z + y, 1] = swapped(blocks[z, 1], y, 0)
    for m, side in list(blocks):
        blocks[m + c, side] = swapped(blocks[m, side], c, 0)
    block_list = [blocks[m, side] for m in range(n) for side in range(2)]

    def spread(mine):
        out = []
        for m in range(n):
            piece = mine[m] if m == 0 else swapped(mine[m], m, 0)
            out += [piece, swapped(piece, n, 0)]
        return out

    kv_weights = spread(pieces[:n])
    q_weights = spread(pieces[n:])

    in_half = lax.dynamic_slice_in_dim(positions, half * n * tokens, n * tokens, 0)
    frequency = 10000.0 ** (-(jnp.arange(HD // 2, dtype=f32) * 2.0 / HD))
    angles = in_half.astype(f32)[:, None] * frequency[None, :]
    cosine, sine = jnp.cos(angles), jnp.sin(angles)
    cosine = jnp.concatenate([cosine, cosine], -1).reshape(n, tokens, HD)
    sine = jnp.concatenate([-sine, sine], -1).reshape(n, tokens, HD)
    index = jnp.arange(positions.shape[0], dtype=jnp.int32)
    starts = jnp.concatenate(
        [jnp.full((reach * tokens,), -(2**30), jnp.int32), index - positions], 0
    )
    docs = lax.dynamic_slice_in_dim(starts, half * n * tokens, (n + reach) * tokens, 0)
    k_doc = docs.reshape(n + reach, 1, tokens)
    q_doc = docs[reach * tokens :].reshape(n, tokens, 1)

    block_bytes = 2 * n * tokens * features * 2
    stores = [
        pltpu.VMEM((n, 2, tokens, features), bf16),
        pltpu.VMEM((2, features, 2 * HD), bf16),
    ]
    sems = [pltpu.SemaphoreType.DMA((n, 2)), pltpu.SemaphoreType.DMA((2 * n,))]
    flops = 2 * n * tokens * 2 * features * 2 * HD
    kv_own, kv_tail = run(
        functools.partial(key_kernel, n, reach),
        [
            jax.ShapeDtypeStruct((n, tokens, 2 * HD), bf16),
            jax.ShapeDtypeStruct((reach, tokens, 2 * HD), bf16),
        ],
        [SMEM, VMEM, VMEM, VMEM] + [ANY] * (4 * n),
        [VMEM, VMEM],
        stores + sems,
        flops,
        block_bytes,
    )(meta, cosine, sine, key_gain.reshape(1, HD), *block_list, *kv_weights)
    kv_back = passed_along(kv_tail, "rows", n)

    context_shape = jax.ShapeDtypeStruct((n, part, heads * HD), bf16)
    keep, send = run(
        functools.partial(attend_kernel, n, reach, heads),
        [context_shape, context_shape],
        [SMEM, VMEM, VMEM, VMEM, VMEM, VMEM, ANY, ANY] + [ANY] * (4 * n),
        [VMEM, VMEM],
        stores
        + [pltpu.VMEM((n + reach, tokens, 2 * HD), bf16)]
        + sems
        + [pltpu.SemaphoreType.DMA((n + 1,))],
        2 * flops,
        block_bytes,
    )(
        meta,
        cosine,
        sine,
        query_gain.reshape(1, HD),
        q_doc,
        k_doc,
        kv_own,
        kv_back,
        *block_list,
        *q_weights,
    )

    out_far = swapped(output_weight, n, 0)
    out_weights = [output_weight, swapped(output_weight, 0, 1), out_far, swapped(out_far, 0, 1)]

    there = swapped(send, 0, 1)
    contexts = {(0, 0): keep, (0, 1): there}
    contexts[z, 0] = swapped(keep, z, 0)
    contexts[y, 0] = swapped(keep, y, 0)
    contexts[z + y, 0] = swapped(contexts[z, 0], y, 0)
    contexts[z, 1] = swapped(there, z, 0)
    contexts[y, 1] = swapped(there, y, 0)
    contexts[z + y, 1] = swapped(contexts[y, 1], z, 0)
    for m, side in list(contexts):
        contexts[m + c, side] = swapped(contexts[m, side], c, 0)
    context_list = [contexts[m, side] for m in range(n) for side in range(2)]

    out_cols = output_weight.shape[1]
    deep_out = output_weight.shape[0]
    results = run(
        functools.partial(output_kernel, n),
        [jax.ShapeDtypeStruct((part, out_cols), bf16)] * (2 * n),
        [SMEM] + [ANY] * (2 * n + 4),
        [VMEM] * (2 * n),
        [
            pltpu.VMEM((n, part, 2 * deep_out), bf16),
            pltpu.VMEM((2, 2 * deep_out, out_cols), bf16),
            pltpu.VMEM((2, n, part, out_cols), bf16),
            pltpu.SemaphoreType.DMA((2 * n,)),
            pltpu.SemaphoreType.DMA((4,)),
        ],
        2 * n * part * 2 * deep_out * 2 * out_cols,
        16 * deep_out * out_cols,
    )(meta, *context_list, *out_weights)

    arrived = [
        [
            results[m * 2 + side]
            if (m, side) == (0, 0)
            else swapped(results[m * 2 + side], m, side)
            for m in range(n)
        ]
        for side in range(2)
    ]
    lanes = []
    for side in range(2):
        ordered = arrived[side]
        bit = 1
        while bit < n:
            flip = (place & bit) != 0
            ordered = [jnp.where(flip, ordered[m ^ bit], ordered[m]) for m in range(n)]
            bit *= 2
        lanes.append(jnp.concatenate(ordered, axis=1))
    top = jnp.where(col == 0, lanes[0], lanes[1])
    bottom = jnp.where(col == 0, lanes[1], lanes[0])
    summed = jnp.concatenate([top, bottom], axis=0)
    return (wide + summed.astype(f32)).astype(bf16)


def fits(mesh, activations, key_weight):
    rows = mesh.shape["rows"]
    tokens = activations.shape[0] // (mesh.shape["groups"] * rows)
    splits = mesh.shape["cols"] * mesh.shape["sub"]
    n = key_weight.shape[1] // HD // splits
    return (
        mesh.shape["cols"] == 2
        and mesh.shape["sub"] == 1
        and n == 8
        and rows == 2 * n
        and WINDOW % tokens == 0
        and WINDOW // tokens <= n
        and tokens % 256 == 0
    )


def solution(mesh):
    placed = (
        P(("groups", "rows"), ("cols", "sub")),
        P("groups"),
        P("rows", ("cols", "sub")),
        P("rows", ("cols", "sub")),
        P("rows", ("cols", "sub")),
        P(("cols", "sub"), "rows"),
        P(),
        P(),
        P(),
    )

    def step(activations, positions, query_weight, key_weight, *rest):
        whole = not fits(mesh, activations, key_weight)

        def body(*args):
            if whole:
                return gathered_body(*args)
            return split_body(*args)

        return jax.shard_map(
            body,
            mesh=mesh,
            in_specs=placed,
            out_specs=P(("groups", "rows"), ("cols", "sub")),
            check_vma=False,
        )(activations, positions, query_weight, key_weight, *rest)

    return step
```

```python
import functools
import math

import jax
import jax.numpy as jnp
from jax import lax
from jax.experimental import pallas as pl
from jax.experimental.pallas import tpu as pltpu
from jax.sharding import Mesh
from jax.sharding import PartitionSpec as P


HD = 128
WINDOW = 1024
QUERY_SCALAR = 168
VMEM_BYTES = 67_000_000
ANY = pl.BlockSpec(memory_space=pl.ANY)
VMEM = pl.BlockSpec(memory_space=pltpu.VMEM)
SMEM = pl.BlockSpec(memory_space=pltpu.SMEM)


def passed_along(value, axis, by):
    peers = lax.axis_size(axis)
    pairs = [(i, i + by) for i in range(peers) if 0 <= i + by < peers]
    return lax.ppermute(value, axis, pairs)


def head_norm(tensor, gain_vector):
    return (
        tensor * lax.rsqrt(jnp.mean(tensor * tensor, axis=-1, keepdims=True) + 1e-06) * gain_vector
    )


def rotate(tensor, token_positions):
    half_width = tensor.shape[-1] // 2
    frequency = 10000.0 ** (-(jnp.arange(half_width, dtype=jnp.float32) * 2.0 / tensor.shape[-1]))
    angles = token_positions.astype(jnp.float32)[:, None] * frequency[None, :]
    cosine = jnp.cos(angles)[:, None, :]
    sine_part = jnp.sin(angles)[:, None, :]
    first_half = tensor[..., :half_width]
    second_half = tensor[..., half_width:]
    return jnp.concatenate(
        [
            first_half * cosine - second_half * sine_part,
            second_half * cosine + first_half * sine_part,
        ],
        axis=-1,
    )


def attend(queries, key_rows, value_rows, query_index, key_index, query_pos, key_pos):
    row_count = queries.shape[0]
    key_count = key_rows.shape[0]
    kv_heads = key_rows.shape[1] // HD
    group_size = queries.shape[1] // key_rows.shape[1]
    query_four = queries.reshape(row_count, kv_heads, group_size, HD)
    key_three = key_rows.reshape(key_count, kv_heads, HD)
    value_three = value_rows.reshape(key_count, kv_heads, HD)
    score_scale = 1.0 / math.sqrt(QUERY_SCALAR)
    scores = (
        jnp.einsum("qgrd,kgd->grqk", query_four, key_three, preferred_element_type=jnp.float32)
        * score_scale
    )
    distance = query_index[:, None] - key_index[None, :]
    visible = (
        (key_index[None, :] >= 0)
        & (distance >= 0)
        & (distance < WINDOW)
        & (query_pos[:, None] - key_pos[None, :] == distance)
    )
    weights = jnp.where(visible[None, None], jnp.exp(scores), 0.0)
    totals = jnp.sum(weights, axis=-1)
    rounded = weights.astype(jnp.bfloat16)
    mixed_heads = jnp.einsum(
        "grqk,kgd->qgrd", rounded, value_three, preferred_element_type=jnp.float32
    )
    mixed_heads = mixed_heads / jnp.transpose(totals, (2, 0, 1))[..., None]
    return mixed_heads.astype(jnp.bfloat16).reshape(row_count, kv_heads * group_size * HD)


def reach_back(key_rows, value_rows, reach_rows):
    pieces = []
    carried = (key_rows, value_rows)
    for _ in range(reach_rows):
        carried = passed_along((carried[0], carried[1]), "rows", 1)
        pieces.append(carried)
    ordered = pieces[::-1] + [(key_rows, value_rows)]
    all_keys = jnp.concatenate([member[0] for member in ordered], axis=0)
    all_values = jnp.concatenate([member[1] for member in ordered], axis=0)
    return (all_keys, all_values)


def gathered_body(
    activations,
    positions,
    query_weight,
    key_weight,
    value_weight,
    output_weight,
    input_gain,
    query_gain,
    key_gain,
):
    rows_here = activations.shape[0]
    row_panel = lax.all_gather(activations, ("cols", "sub"), axis=1, tiled=True)
    panel_wide = row_panel.astype(jnp.float32)
    inverse = lax.rsqrt(jnp.mean(panel_wide * panel_wide, axis=-1, keepdims=True) + 1e-06)
    normed = (panel_wide * inverse * input_gain).astype(jnp.bfloat16)
    row_index = lax.axis_index("rows")
    own_positions = lax.dynamic_slice_in_dim(positions, row_index * rows_here, rows_here, 0)
    reach_rows = min(-(-WINDOW // rows_here), lax.axis_size("rows") - 1)

    def add_rows(weight_piece):
        return jnp.dot(normed, weight_piece, preferred_element_type=jnp.float32)

    query_raw = add_rows(lax.all_gather(query_weight, "rows", axis=0, tiled=True))
    key_raw = add_rows(lax.all_gather(key_weight, "rows", axis=0, tiled=True))
    value_raw = add_rows(lax.all_gather(value_weight, "rows", axis=0, tiled=True))
    key_rows = rotate(head_norm(key_raw.reshape(rows_here, -1, HD), key_gain), own_positions)
    key_rows, value_rows = (
        key_rows.astype(jnp.bfloat16).reshape(rows_here, -1),
        value_raw.astype(jnp.bfloat16),
    )
    all_keys, all_values = reach_back(key_rows, value_rows, reach_rows)
    queries = rotate(head_norm(query_raw.reshape(rows_here, -1, HD), query_gain), own_positions)
    queries = queries.astype(jnp.bfloat16).reshape(rows_here, -1)
    key_count = all_keys.shape[0]
    query_index = row_index * rows_here + jnp.arange(rows_here, dtype=jnp.int32)
    key_index = (row_index - reach_rows) * rows_here + jnp.arange(key_count, dtype=jnp.int32)
    padded = jnp.concatenate([jnp.zeros((reach_rows * rows_here,), jnp.int32), positions], axis=0)
    key_positions = lax.dynamic_slice_in_dim(padded, row_index * rows_here, key_count, 0)
    context = attend(
        queries, all_keys, all_values, query_index, key_index, own_positions, key_positions
    )
    partial_terms = jnp.dot(
        context,
        lax.all_gather(output_weight, "rows", axis=1, tiled=True),
        preferred_element_type=jnp.float32,
    )
    summed = lax.psum_scatter(
        partial_terms.astype(jnp.bfloat16), ("cols", "sub"), scatter_dimension=1, tiled=True
    ).astype(jnp.float32)
    return (activations.astype(jnp.float32) + summed).astype(jnp.bfloat16)


def swapped(value, place=0, col=0):
    places, cols = lax.axis_size("place"), lax.axis_size("cols")
    pairs = [
        (r * cols + c, (r ^ place) * cols + (c ^ col)) for r in range(places) for c in range(cols)
    ]
    return lax.ppermute(value, ("place", "cols"), pairs)


def run(kernel, out_shape, in_specs, out_specs, scratch, flops, bytes_moved):
    return pl.pallas_call(
        kernel,
        out_shape=out_shape,
        in_specs=in_specs,
        out_specs=out_specs,
        scratch_shapes=scratch,
        compiler_params=pltpu.CompilerParams(vmem_limit_bytes=VMEM_BYTES),
        cost_estimate=pl.CostEstimate(
            flops=int(flops), bytes_accessed=int(bytes_moved), transcendentals=0
        ),
    )


def cut_kernel(n, meta, wq, wk, wv, kv_out, *q_outs):
    place = meta[0]
    wide_q = wq.shape[1] // n
    for p in range(n):
        kv_out[:, p * 2 * HD : p * 2 * HD + HD] = wk[:, p * HD : (p + 1) * HD]
        kv_out[:, p * 2 * HD + HD : (p + 1) * 2 * HD] = wv[:, p * HD : (p + 1) * HD]
    for m in range(n):
        at = lax.bitwise_xor(place, m)
        q_outs[m][...] = wq[:, pl.ds(pl.multiple_of(at * wide_q, 128), wide_q)]


def join_kernel(*refs):
    out = refs[-1]
    deep = refs[0].shape[0]
    for m, piece in enumerate(refs[:-1]):
        out[m * deep : (m + 1) * deep] = piece[...]


def load_all(n, meta, blocks, weight_parts, block_mem, weight_mem, block_sem, weight_sem):
    place = meta[0]
    copies = []
    for m in range(n):
        for half in range(2):
            source = weight_parts(m, half)
            deep = source.shape[0]
            owner = lax.bitwise_xor(place, m)
            copies.append(
                pltpu.make_async_copy(
                    source,
                    weight_mem.at[half, pl.ds(pl.multiple_of(owner * deep, 16), deep), :],
                    weight_sem.at[m * 2 + half],
                )
            )
    for copy in copies:
        copy.start()
    for m in range(n):
        for side in range(2):
            pltpu.make_async_copy(
                blocks[m * 2 + side], block_mem.at[side, m], block_sem.at[m, side]
            ).start()
    return copies


def project(t, meta, blocks, block_mem, weight_mem, block_sem):
    col = meta[2]
    _, _, tokens, features = block_mem.shape
    for m in range(2):
        for side in range(2):
            pltpu.make_async_copy(
                blocks[side], block_mem.at[side, 2 * t + m], block_sem.at[2 * t + m, side]
            ).wait()
    same = block_mem[0, pl.ds(2 * t, 2)].reshape(2 * tokens, features)
    other = block_mem[1, pl.ds(2 * t, 2)].reshape(2 * tokens, features)
    return jnp.dot(same, weight_mem[col], preferred_element_type=jnp.float32) + jnp.dot(
        other, weight_mem[lax.bitwise_xor(col, 1)], preferred_element_type=jnp.float32
    )


def normed_rotated(raw, gain, cosine, sine):
    scaled = raw * lax.rsqrt(jnp.mean(raw * raw, axis=-1, keepdims=True) + 1e-06) * gain
    return scaled * cosine + pltpu.roll(scaled, HD // 2, 1) * sine


def key_kernel(n, reach, meta, cosine, sine, gain, *refs):
    blocks, weights = refs[: 2 * n], refs[2 * n : 3 * n]
    kv_out, tail_out, block_mem, weight_mem, block_sem, weight_sem = refs[3 * n :]
    deep = weights[0].shape[0] // 2

    def part(m, half):
        return weights[m].at[pl.ds(half * deep, deep)]

    copies = load_all(n, meta, blocks, part, block_mem, weight_mem, block_sem, weight_sem)
    for copy in copies:
        copy.wait()
    place = meta[0]
    tokens = block_mem.shape[2]

    @pl.loop(0, n // 2)
    def _(t):
        raw_two = project(t, meta, blocks, block_mem, weight_mem, block_sem)
        for m in range(2):
            slot = 2 * t + m
            at = lax.bitwise_xor(place, slot)
            raw = raw_two[m * tokens : (m + 1) * tokens]
            keys = normed_rotated(raw[:, :HD], gain[...], cosine[at], sine[at])
            keys = keys.astype(jnp.bfloat16)
            values = raw[:, HD:].astype(jnp.bfloat16)
            kv_out[slot, :, :HD] = keys
            kv_out[slot, :, HD:] = values

            @pl.when(at >= n - reach)
            def _():
                tail_out[at - (n - reach), :, :HD] = keys
                tail_out[at - (n - reach), :, HD:] = values


def attend_kernel(n, reach, heads, meta, cosine, sine, gain, q_doc, k_doc, kv_own, kv_back, *refs):
    blocks, weight = refs[: 2 * n], refs[2 * n]
    keep_out, send_out = refs[2 * n + 1 : 2 * n + 3]
    block_mem, weight_mem, kv_mem, block_sem, weight_sem, kv_sem = refs[2 * n + 3 :]
    place, col = meta[0], meta[2]
    tokens = block_mem.shape[2]
    part = tokens // 2
    deep = weight.shape[0] // (2 * n)

    def rows(m, half):
        return weight.at[pl.ds((half * n + m) * deep, deep)]

    copies = load_all(n, meta, blocks, rows, block_mem, weight_mem, block_sem, weight_sem)
    more = [pltpu.make_async_copy(kv_back, kv_mem.at[pl.ds(0, reach)], kv_sem.at[n])]
    for m in range(n):
        more.append(
            pltpu.make_async_copy(
                kv_own.at[m], kv_mem.at[reach + lax.bitwise_xor(place, m)], kv_sem.at[m]
            )
        )
    for copy in more:
        copy.start()
    for copy in copies + more:
        copy.wait()
    scale = 1.0 / math.sqrt(QUERY_SCALAR)
    row_at = lax.broadcasted_iota(jnp.int32, (tokens, tokens), 0)
    col_at = lax.broadcasted_iota(jnp.int32, (tokens, tokens), 1)

    @pl.loop(0, n // 2)
    def _(t):
        raw_two = project(t, meta, blocks, block_mem, weight_mem, block_sem)
        for m in range(2):
            at = lax.bitwise_xor(place, 2 * t + m)
            raw = raw_two[m * tokens : (m + 1) * tokens]
            cosine_here, sine_here = cosine[at], sine[at]
            queries = jnp.concatenate(
                [
                    normed_rotated(
                        raw[:, h * HD : (h + 1) * HD], gain[...], cosine_here, sine_here
                    ).astype(jnp.bfloat16)
                    for h in range(heads)
                ],
                axis=0,
            )
            doc = q_doc[at]
            totals = jnp.zeros((heads * tokens, 1), jnp.float32)
            mixed = jnp.zeros((heads * tokens, HD), jnp.float32)
            for step in range(reach + 1):
                pair = kv_mem[at + step]
                visible = doc == k_doc[at + step]
                if step == 0:
                    visible = visible & (row_at < col_at)
                if step == reach:
                    visible = visible & (row_at >= col_at)
                scores = lax.dot_general(
                    queries,
                    pair[:, :HD],
                    (((1,), (1,)), ((), ())),
                    preferred_element_type=jnp.float32,
                )
                weights_here = jnp.where(
                    visible[None],
                    jnp.exp(scores * scale).reshape(heads, tokens, tokens),
                    0.0,
                ).reshape(heads * tokens, tokens)
                totals = totals + jnp.sum(weights_here, axis=-1, keepdims=True)
                mixed = mixed + jnp.dot(
                    weights_here.astype(jnp.bfloat16),
                    pair[:, HD:],
                    preferred_element_type=jnp.float32,
                )
            done = (mixed / totals).astype(jnp.bfloat16)
            for h in range(heads):
                top = done[h * tokens : h * tokens + part]
                bottom = done[h * tokens + part : (h + 1) * tokens]
                keep_out[at, :, h * HD : (h + 1) * HD] = jnp.where(col == 0, top, bottom)
                send_out[at, :, h * HD : (h + 1) * HD] = jnp.where(col == 0, bottom, top)


def output_kernel(n, meta, *refs):
    contexts, weights = refs[: 2 * n], refs[2 * n]
    outs = refs[2 * n + 1 : 4 * n + 1]
    context_mem, weight_mem, result_mem, context_sem, weight_sem = refs[4 * n + 1 :]
    place, col = meta[0], meta[2]
    deep = weights.shape[2]
    wide = contexts[0].shape[2]
    part = contexts[0].shape[1]
    copies = []
    for half in range(2):
        for side in range(2):
            copies.append(
                pltpu.make_async_copy(
                    weights.at[half, side],
                    weight_mem.at[half, pl.ds(side * deep, deep), :],
                    weight_sem.at[half * 2 + side],
                )
            )
    for m in range(n):
        for side in range(2):
            first = lax.bitwise_xor(col, side) * deep + lax.bitwise_xor(place, m) * wide
            copies.append(
                pltpu.make_async_copy(
                    contexts[m * 2 + side],
                    context_mem.at[:, :, pl.ds(pl.multiple_of(first, 128), wide)],
                    context_sem.at[m * 2 + side],
                )
            )
    for copy in copies:
        copy.start()
    for copy in copies:
        copy.wait()

    @pl.loop(0, n // 4)
    def _(t):
        left = context_mem[pl.ds(4 * t, 4)].reshape(4 * part, 2 * deep)
        for block in range(2):
            result = jnp.dot(left, weight_mem[block], preferred_element_type=jnp.float32)
            result_mem[block, pl.ds(4 * t, 4)] = result.astype(jnp.bfloat16).reshape(4, part, -1)

    for m in range(n):
        for side in range(2):
            outs[m * 2 + side][...] = result_mem[
                lax.bitwise_xor(col, side), lax.bitwise_xor(place, m)
            ]


def split_body(
    activations,
    positions,
    query_weight,
    key_weight,
    value_weight,
    output_weight,
    input_gain,
    query_gain,
    key_gain,
):
    tokens, features = activations.shape
    n = key_weight.shape[1] // HD
    heads = query_weight.shape[1] // key_weight.shape[1]
    reach = WINDOW // tokens
    part = tokens // 2
    half, place, col = lax.axis_index("half"), lax.axis_index("place"), lax.axis_index("cols")
    meta = jnp.stack([place, half, col]).astype(jnp.int32)
    bf16, f32 = jnp.bfloat16, jnp.float32

    deep = query_weight.shape[0]
    kv_cut, *q_cut = run(
        functools.partial(cut_kernel, n),
        [jax.ShapeDtypeStruct((deep, n * 2 * HD), bf16)]
        + [jax.ShapeDtypeStruct((deep, heads * HD), bf16)] * n,
        [SMEM, VMEM, VMEM, VMEM],
        [VMEM] * (n + 1),
        [],
        0,
        4 * query_weight.size * 2,
    )(meta, query_weight, key_weight, value_weight)
    kv_rows = lax.all_gather(kv_cut, "half", axis=0, tiled=True)

    wide = activations.astype(f32)
    squares = jnp.sum(wide * wide, axis=-1).reshape(2, part)
    squares = (squares + swapped(squares, 0, 1)).reshape(tokens, 1)
    inverse = lax.rsqrt(squares / (2 * features) + 1e-06)
    gain = lax.dynamic_slice_in_dim(input_gain, col * features, features, 0)
    normed = (wide * inverse * gain).astype(bf16)

    z, y, c = n // 2, n // 4, 1
    blocks = {(0, 0): normed}
    blocks[y, 0] = swapped(normed, y, 0)
    blocks[0, 1] = swapped(normed, 0, 1)
    blocks[z, 0] = swapped(normed, z, 0)
    blocks[y, 1] = swapped(blocks[y, 0], 0, 1)
    blocks[z, 1] = swapped(blocks[z, 0], 0, 1)
    blocks[z + y, 0] = swapped(blocks[z, 0], y, 0)
    blocks[z + y, 1] = swapped(blocks[z + y, 0], 0, 1)
    for m, side in list(blocks):
        blocks[m + c, side] = swapped(blocks[m, side], c, 0)
    block_list = [blocks[m, side] for m in range(n) for side in range(2)]

    q_pieces = [q_cut[0]] + [swapped(q_cut[m], m, 0) for m in range(1, n)]
    q_own = run(
        join_kernel,
        jax.ShapeDtypeStruct((n * deep, heads * HD), bf16),
        [VMEM] * n,
        VMEM,
        [],
        0,
        4 * q_cut[0].size * n,
    )(*q_pieces)
    q_weight = lax.all_gather(q_own, "half", axis=0, tiled=True)
    kv_weights = []
    for m in range(n):
        first = lax.bitwise_xor(place, m) * 2 * HD
        piece = lax.dynamic_slice_in_dim(kv_rows, first, 2 * HD, 1)
        kv_weights.append(piece if m == 0 else swapped(piece, m, 0))

    in_half = lax.dynamic_slice_in_dim(positions, half * n * tokens, n * tokens, 0)
    frequency = 10000.0 ** (-(jnp.arange(HD // 2, dtype=f32) * 2.0 / HD))
    angles = in_half.astype(f32)[:, None] * frequency[None, :]
    cosine, sine = jnp.cos(angles), jnp.sin(angles)
    cosine = jnp.concatenate([cosine, cosine], -1).reshape(n, tokens, HD)
    sine = jnp.concatenate([-sine, sine], -1).reshape(n, tokens, HD)
    index = jnp.arange(positions.shape[0], dtype=jnp.int32)
    starts = jnp.concatenate(
        [jnp.full((reach * tokens,), -(2**30), jnp.int32), index - positions], 0
    )
    docs = lax.dynamic_slice_in_dim(starts, half * n * tokens, (n + reach) * tokens, 0)
    k_doc = docs.reshape(n + reach, 1, tokens)
    q_doc = docs[reach * tokens :].reshape(n, tokens, 1)

    block_bytes = 2 * n * tokens * features * 2
    stores = [
        pltpu.VMEM((2, n, tokens, features), bf16),
        pltpu.VMEM((2, features, 2 * HD), bf16),
    ]
    sems = [pltpu.SemaphoreType.DMA((n, 2)), pltpu.SemaphoreType.DMA((2 * n,))]
    flops = 2 * n * tokens * 2 * features * 2 * HD
    kv_own, kv_tail = run(
        functools.partial(key_kernel, n, reach),
        [
            jax.ShapeDtypeStruct((n, tokens, 2 * HD), bf16),
            jax.ShapeDtypeStruct((reach, tokens, 2 * HD), bf16),
        ],
        [SMEM, VMEM, VMEM, VMEM] + [ANY] * (3 * n),
        [VMEM, VMEM],
        stores + sems,
        flops,
        block_bytes,
    )(meta, cosine, sine, key_gain.reshape(1, HD), *block_list, *kv_weights)
    kv_back = lax.ppermute(kv_tail, "half", [(0, 1)])

    context_shape = jax.ShapeDtypeStruct((n, part, heads * HD), bf16)
    keep, send = run(
        functools.partial(attend_kernel, n, reach, heads),
        [context_shape, context_shape],
        [SMEM, VMEM, VMEM, VMEM, VMEM, VMEM, ANY, ANY] + [ANY] * (2 * n + 1),
        [VMEM, VMEM],
        stores
        + [pltpu.VMEM((n + reach, tokens, 2 * HD), bf16)]
        + sems
        + [pltpu.SemaphoreType.DMA((n + 1,))],
        2 * flops,
        block_bytes,
    )(
        meta,
        cosine,
        sine,
        query_gain.reshape(1, HD),
        q_doc,
        k_doc,
        kv_own,
        kv_back,
        *block_list,
        q_weight,
    )

    own_weight, _ = lax.optimization_barrier((output_weight, q_own))
    out_weights = lax.all_gather(own_weight, ("half", "cols"), axis=0)
    out_weights = out_weights.reshape(2, 2, *output_weight.shape)

    there = swapped(send, 0, 1)
    contexts = {(0, 0): keep, (0, 1): there}
    contexts[z, 0] = swapped(keep, z, 0)
    contexts[y, 0] = swapped(keep, y, 0)
    contexts[z + y, 0] = swapped(contexts[z, 0], y, 0)
    contexts[z, 1] = swapped(there, z, 0)
    contexts[y, 1] = swapped(there, y, 0)
    contexts[z + y, 1] = swapped(contexts[y, 1], z, 0)
    for m, side in list(contexts):
        contexts[m + c, side] = swapped(contexts[m, side], c, 0)
    context_list = [contexts[m, side] for m in range(n) for side in range(2)]

    out_cols = output_weight.shape[1]
    deep_out = output_weight.shape[0]
    results = run(
        functools.partial(output_kernel, n),
        [jax.ShapeDtypeStruct((part, out_cols), bf16)] * (2 * n),
        [SMEM] + [ANY] * (2 * n + 1),
        [VMEM] * (2 * n),
        [
            pltpu.VMEM((n, part, 2 * deep_out), bf16),
            pltpu.VMEM((2, 2 * deep_out, out_cols), bf16),
            pltpu.VMEM((2, n, part, out_cols), bf16),
            pltpu.SemaphoreType.DMA((2 * n,)),
            pltpu.SemaphoreType.DMA((4,)),
        ],
        2 * n * part * 2 * deep_out * 2 * out_cols,
        16 * deep_out * out_cols,
    )(meta, *context_list, out_weights)

    arrived = [
        [
            results[m * 2 + side]
            if (m, side) == (0, 0)
            else swapped(results[m * 2 + side], m, side)
            for m in range(n)
        ]
        for side in range(2)
    ]
    lanes = []
    for side in range(2):
        ordered = arrived[side]
        bit = 1
        while bit < n:
            flip = (place & bit) != 0
            ordered = [jnp.where(flip, ordered[m ^ bit], ordered[m]) for m in range(n)]
            bit *= 2
        lanes.append(jnp.concatenate(ordered, axis=1))
    top = jnp.where(col == 0, lanes[0], lanes[1])
    bottom = jnp.where(col == 0, lanes[1], lanes[0])
    summed = jnp.concatenate([top, bottom], axis=0)
    return (wide + summed.astype(f32)).astype(bf16)


def solution(mesh):
    sizes = mesh.shape
    if sizes["cols"] == 2 and sizes["sub"] == 1 and sizes["rows"] == 16:
        shape = (sizes["groups"], 2, sizes["rows"] // 2, sizes["cols"], sizes["sub"])
        names = ("groups", "half", "place", "cols", "sub")
        fine, rows = Mesh(mesh.devices.reshape(shape), names), ("half", "place")
    else:
        fine, rows = mesh, ("rows",)
    columns = ("cols", "sub")
    placed = (
        P(("groups", *rows), columns),
        P("groups"),
        P(rows, columns),
        P(rows, columns),
        P(rows, columns),
        P(columns, rows),
        P(),
        P(),
        P(),
    )

    def mapped(body):
        return jax.shard_map(
            body, mesh=fine, in_specs=placed, out_specs=placed[0], check_vma=False
        )

    if fine is mesh:
        return mapped(gathered_body)

    return mapped(split_body)
```

```python
import functools
import math

import jax
import jax.numpy as jnp
from jax import lax
from jax.experimental import pallas as pl
from jax.experimental.pallas import tpu as pltpu
from jax.sharding import Mesh
from jax.sharding import PartitionSpec as P


HD = 128
WINDOW = 1024
QUERY_SCALAR = 168
VMEM_BYTES = 67_000_000
ANY = pl.BlockSpec(memory_space=pl.ANY)
VMEM = pl.BlockSpec(memory_space=pltpu.VMEM)
SMEM = pl.BlockSpec(memory_space=pltpu.SMEM)


def passed_along(value, axis, by):
    peers = lax.axis_size(axis)
    pairs = [(i, i + by) for i in range(peers) if 0 <= i + by < peers]
    return lax.ppermute(value, axis, pairs)


def head_norm(tensor, gain_vector):
    return (
        tensor * lax.rsqrt(jnp.mean(tensor * tensor, axis=-1, keepdims=True) + 1e-06) * gain_vector
    )


def rotate(tensor, token_positions):
    half_width = tensor.shape[-1] // 2
    frequency = 10000.0 ** (-(jnp.arange(half_width, dtype=jnp.float32) * 2.0 / tensor.shape[-1]))
    angles = token_positions.astype(jnp.float32)[:, None] * frequency[None, :]
    cosine = jnp.cos(angles)[:, None, :]
    sine_part = jnp.sin(angles)[:, None, :]
    first_half = tensor[..., :half_width]
    second_half = tensor[..., half_width:]
    return jnp.concatenate(
        [
            first_half * cosine - second_half * sine_part,
            second_half * cosine + first_half * sine_part,
        ],
        axis=-1,
    )


def attend(queries, key_rows, value_rows, query_index, key_index, query_pos, key_pos):
    row_count = queries.shape[0]
    key_count = key_rows.shape[0]
    kv_heads = key_rows.shape[1] // HD
    group_size = queries.shape[1] // key_rows.shape[1]
    query_four = queries.reshape(row_count, kv_heads, group_size, HD)
    key_three = key_rows.reshape(key_count, kv_heads, HD)
    value_three = value_rows.reshape(key_count, kv_heads, HD)
    score_scale = 1.0 / math.sqrt(QUERY_SCALAR)
    scores = (
        jnp.einsum("qgrd,kgd->grqk", query_four, key_three, preferred_element_type=jnp.float32)
        * score_scale
    )
    distance = query_index[:, None] - key_index[None, :]
    visible = (
        (key_index[None, :] >= 0)
        & (distance >= 0)
        & (distance < WINDOW)
        & (query_pos[:, None] - key_pos[None, :] == distance)
    )
    weights = jnp.where(visible[None, None], jnp.exp(scores), 0.0)
    totals = jnp.sum(weights, axis=-1)
    rounded = weights.astype(jnp.bfloat16)
    mixed_heads = jnp.einsum(
        "grqk,kgd->qgrd", rounded, value_three, preferred_element_type=jnp.float32
    )
    mixed_heads = mixed_heads / jnp.transpose(totals, (2, 0, 1))[..., None]
    return mixed_heads.astype(jnp.bfloat16).reshape(row_count, kv_heads * group_size * HD)


def reach_back(key_rows, value_rows, reach_rows):
    pieces = []
    carried = (key_rows, value_rows)
    for _ in range(reach_rows):
        carried = passed_along((carried[0], carried[1]), "rows", 1)
        pieces.append(carried)
    ordered = pieces[::-1] + [(key_rows, value_rows)]
    all_keys = jnp.concatenate([member[0] for member in ordered], axis=0)
    all_values = jnp.concatenate([member[1] for member in ordered], axis=0)
    return (all_keys, all_values)


def gathered_body(
    activations,
    positions,
    query_weight,
    key_weight,
    value_weight,
    output_weight,
    input_gain,
    query_gain,
    key_gain,
):
    rows_here = activations.shape[0]
    row_panel = lax.all_gather(activations, ("cols", "sub"), axis=1, tiled=True)
    panel_wide = row_panel.astype(jnp.float32)
    inverse = lax.rsqrt(jnp.mean(panel_wide * panel_wide, axis=-1, keepdims=True) + 1e-06)
    normed = (panel_wide * inverse * input_gain).astype(jnp.bfloat16)
    row_index = lax.axis_index("rows")
    own_positions = lax.dynamic_slice_in_dim(positions, row_index * rows_here, rows_here, 0)
    reach_rows = min(-(-WINDOW // rows_here), lax.axis_size("rows") - 1)

    def add_rows(weight_piece):
        return jnp.dot(normed, weight_piece, preferred_element_type=jnp.float32)

    query_raw = add_rows(lax.all_gather(query_weight, "rows", axis=0, tiled=True))
    key_raw = add_rows(lax.all_gather(key_weight, "rows", axis=0, tiled=True))
    value_raw = add_rows(lax.all_gather(value_weight, "rows", axis=0, tiled=True))
    key_rows = rotate(head_norm(key_raw.reshape(rows_here, -1, HD), key_gain), own_positions)
    key_rows, value_rows = (
        key_rows.astype(jnp.bfloat16).reshape(rows_here, -1),
        value_raw.astype(jnp.bfloat16),
    )
    all_keys, all_values = reach_back(key_rows, value_rows, reach_rows)
    queries = rotate(head_norm(query_raw.reshape(rows_here, -1, HD), query_gain), own_positions)
    queries = queries.astype(jnp.bfloat16).reshape(rows_here, -1)
    key_count = all_keys.shape[0]
    query_index = row_index * rows_here + jnp.arange(rows_here, dtype=jnp.int32)
    key_index = (row_index - reach_rows) * rows_here + jnp.arange(key_count, dtype=jnp.int32)
    padded = jnp.concatenate([jnp.zeros((reach_rows * rows_here,), jnp.int32), positions], axis=0)
    key_positions = lax.dynamic_slice_in_dim(padded, row_index * rows_here, key_count, 0)
    context = attend(
        queries, all_keys, all_values, query_index, key_index, own_positions, key_positions
    )
    partial_terms = jnp.dot(
        context,
        lax.all_gather(output_weight, "rows", axis=1, tiled=True),
        preferred_element_type=jnp.float32,
    )
    summed = lax.psum_scatter(
        partial_terms.astype(jnp.bfloat16), ("cols", "sub"), scatter_dimension=1, tiled=True
    ).astype(jnp.float32)
    return (activations.astype(jnp.float32) + summed).astype(jnp.bfloat16)


def swapped(value, place=0, col=0):
    places, cols = lax.axis_size("place"), lax.axis_size("cols")
    pairs = [
        (r * cols + c, (r ^ place) * cols + (c ^ col)) for r in range(places) for c in range(cols)
    ]
    return lax.ppermute(value, ("place", "cols"), pairs)


def run(kernel, out_shape, in_specs, out_specs, scratch, flops, bytes_moved):
    return pl.pallas_call(
        kernel,
        out_shape=out_shape,
        in_specs=in_specs,
        out_specs=out_specs,
        scratch_shapes=scratch,
        compiler_params=pltpu.CompilerParams(vmem_limit_bytes=VMEM_BYTES),
        cost_estimate=pl.CostEstimate(
            flops=int(flops), bytes_accessed=int(bytes_moved), transcendentals=0
        ),
    )


def cut_kernel(n, meta, wq, wk, wv, kv_out, *outs):
    place = meta[0]
    wide_q = wq.shape[1] // n
    for p in range(n):
        kv_out[:, p * 2 * HD : p * 2 * HD + HD] = wk[:, p * HD : (p + 1) * HD]
        kv_out[:, p * 2 * HD + HD : (p + 1) * 2 * HD] = wv[:, p * HD : (p + 1) * HD]
    for m in range(n):
        at = lax.bitwise_xor(place, m)
        cols = pl.ds(pl.multiple_of(at * HD, HD), HD)
        outs[m][:, :HD] = wk[:, cols]
        outs[m][:, HD : 2 * HD] = wv[:, cols]
        outs[m][:, 2 * HD :] = wq[:, pl.ds(pl.multiple_of(at * wide_q, 128), wide_q)]


def join_kernel(*refs):
    out = refs[-1]
    deep = refs[0].shape[0]
    for m, piece in enumerate(refs[:-1]):
        out[m * deep : (m + 1) * deep] = piece[:, 2 * HD :]


def pair_kernel(first, second, out):
    out[0] = first[...]
    out[1] = second[...]


def normed_rotated(raw, gain, cosine, sine):
    scaled = raw * lax.rsqrt(jnp.mean(raw * raw, axis=-1, keepdims=True) + 1e-06) * gain
    return scaled * cosine + pltpu.roll(scaled, HD // 2, 1) * sine


def project_kernel(n, reach, heads, meta, cosine, sine, key_gain, query_gain, *refs):
    blocks, near, far = refs[: 2 * n], refs[2 * n : 3 * n], refs[3 * n : 4 * n]
    q_far = refs[4 * n]
    kv_out, tail_out, q_out = refs[4 * n + 1 : 4 * n + 4]
    block_mem, weight_mem, block_sem, weight_sem = refs[4 * n + 4 :]
    place, half, col = meta[0], meta[1], meta[2]
    other = lax.bitwise_xor(half, 1)
    _, _, tokens, features = block_mem.shape
    deep = near[0].shape[0]
    copies = []
    for m in range(n):
        rows = pl.ds(pl.multiple_of(lax.bitwise_xor(place, m) * deep, 16), deep)
        source = pl.ds(pl.multiple_of((other * n + m) * deep, 16), deep)
        for k, (start, target) in enumerate(
            [
                (near[m], weight_mem.at[half, rows, :]),
                (far[m], weight_mem.at[other, rows, pl.ds(0, 2 * HD)]),
                (q_far.at[source, :], weight_mem.at[other, rows, pl.ds(2 * HD, heads * HD)]),
            ]
        ):
            copies.append(pltpu.make_async_copy(start, target, weight_sem.at[3 * m + k]))
    for copy in copies:
        copy.start()
    for m in range(n):
        for side in range(2):
            pltpu.make_async_copy(
                blocks[m * 2 + side], block_mem.at[side, m], block_sem.at[m, side]
            ).start()
    for copy in copies:
        copy.wait()

    @pl.loop(0, n // 2)
    def _(t):
        for m in range(2):
            for side in range(2):
                pltpu.make_async_copy(
                    blocks[side], block_mem.at[side, 2 * t + m], block_sem.at[2 * t + m, side]
                ).wait()
        mine = block_mem[0, pl.ds(2 * t, 2)].reshape(2 * tokens, features)
        theirs = block_mem[1, pl.ds(2 * t, 2)].reshape(2 * tokens, features)
        raw_two = jnp.dot(mine, weight_mem[col], preferred_element_type=jnp.float32) + jnp.dot(
            theirs, weight_mem[lax.bitwise_xor(col, 1)], preferred_element_type=jnp.float32
        )
        for m in range(2):
            slot = 2 * t + m
            at = lax.bitwise_xor(place, slot)
            raw = raw_two[m * tokens : (m + 1) * tokens]
            cosine_here, sine_here = cosine[at], sine[at]
            keys = normed_rotated(raw[:, :HD], key_gain[...], cosine_here, sine_here)
            keys = keys.astype(jnp.bfloat16)
            values = raw[:, HD : 2 * HD].astype(jnp.bfloat16)
            kv_out[at, :, :HD] = keys
            kv_out[at, :, HD:] = values
            for h in range(heads):
                query = raw[:, (2 + h) * HD : (3 + h) * HD]
                query = normed_rotated(query, query_gain[...], cosine_here, sine_here)
                q_out[at, pl.ds(h * tokens, tokens), :] = query.astype(jnp.bfloat16)

            @pl.when(at >= n - reach)
            def _():
                tail_out[at - (n - reach), :, :HD] = keys
                tail_out[at - (n - reach), :, HD:] = values


def attend_kernel(low, count, reach, heads, meta, q_doc, k_doc, queries, kv_own, *refs):
    kv_back = refs[0] if low < reach else None
    keep_out, send_out = refs[-2:]
    col = meta[2]
    tokens = kv_own.shape[1]
    part = tokens // 2
    scale = 1.0 / math.sqrt(QUERY_SCALAR)
    row_at = lax.broadcasted_iota(jnp.int32, (tokens, tokens), 0)
    col_at = lax.broadcasted_iota(jnp.int32, (tokens, tokens), 1)

    for g in range(count):
        doc = q_doc[low + g]
        query = queries[low + g]
        totals = jnp.zeros((heads * tokens, 1), jnp.float32)
        mixed = jnp.zeros((heads * tokens, HD), jnp.float32)
        for step in range(reach + 1):
            at = low + g + step
            pair = kv_back[at] if at < reach else kv_own[at - reach]
            visible = doc == k_doc[at]
            if step == 0:
                visible = visible & (row_at < col_at)
            if step == reach:
                visible = visible & (row_at >= col_at)
            scores = lax.dot_general(
                query, pair[:, :HD], (((1,), (1,)), ((), ())), preferred_element_type=jnp.float32
            )
            weights_here = jnp.where(
                visible[None], jnp.exp(scores * scale).reshape(heads, tokens, tokens), 0.0
            ).reshape(heads * tokens, tokens)
            totals = totals + jnp.sum(weights_here, axis=-1, keepdims=True)
            mixed = mixed + jnp.dot(
                weights_here.astype(jnp.bfloat16), pair[:, HD:], preferred_element_type=jnp.float32
            )
        done = (mixed / totals).astype(jnp.bfloat16)
        for h in range(heads):
            top = done[h * tokens : h * tokens + part]
            bottom = done[h * tokens + part : (h + 1) * tokens]
            keep_out[g, :, h * HD : (h + 1) * HD] = jnp.where(col == 0, top, bottom)
            send_out[g, :, h * HD : (h + 1) * HD] = jnp.where(col == 0, bottom, top)


def output_kernel(n, spans, meta, *refs):
    count = n * len(spans)
    contexts, weights = refs[:count], refs[count : count + 6]
    out, context_mem, weight_mem, context_sem, weight_sem = refs[count + 6 :]
    place, half, col = meta[0], meta[1], meta[2]
    deep = weights[0].shape[1]
    wide = contexts[0].shape[3]
    part = contexts[0].shape[2]
    copies = []
    for k, source in enumerate(weights):
        owner = half if k < 2 else lax.bitwise_xor(half, 1)
        rows = source.shape[0]
        first = 0 if k < 4 else weights[2].shape[0]
        side = pl.multiple_of(lax.bitwise_xor(col, k % 2) * deep, 128)
        copies.append(
            pltpu.make_async_copy(
                source,
                weight_mem.at[owner, pl.ds(first, rows), pl.ds(side, deep)],
                weight_sem.at[k],
            )
        )
    for s, (low, size) in enumerate(spans):
        for m in range(n):
            for side in range(2):
                first = lax.bitwise_xor(col, side) * deep + lax.bitwise_xor(place, m) * wide
                copies.append(
                    pltpu.make_async_copy(
                        contexts[s * n + m].at[side],
                        context_mem.at[
                            pl.ds(low, size), :, pl.ds(pl.multiple_of(first, 128), wide)
                        ],
                        context_sem.at[(s * n + m) * 2 + side],
                    )
                )
    for copy in copies:
        copy.start()
    for copy in copies:
        copy.wait()

    @pl.loop(0, n // 4)
    def _(t):
        left = context_mem[pl.ds(4 * t, 4)].reshape(4 * part, 2 * deep)
        for block in range(2):
            result = lax.dot_general(
                left,
                weight_mem[block],
                (((1,), (1,)), ((), ())),
                preferred_element_type=jnp.float32,
            ).astype(jnp.bfloat16)
            for k in range(4):
                out[(4 * t + k) * 2 + block] = result[k * part : (k + 1) * part]


def close_kernel(n, activations, arrived, out):
    part = arrived.shape[1]
    for col in range(2):
        rows = pl.ds(col * part, part)
        whole = jnp.concatenate([arrived[2 * p + col] for p in range(n)], axis=1)
        out[rows, :] = (
            activations[rows, :].astype(jnp.float32) + whole.astype(jnp.float32)
        ).astype(jnp.bfloat16)


def split_body(
    activations,
    positions,
    query_weight,
    key_weight,
    value_weight,
    output_weight,
    input_gain,
    query_gain,
    key_gain,
):
    tokens, features = activations.shape
    n = key_weight.shape[1] // HD
    heads = query_weight.shape[1] // key_weight.shape[1]
    reach = WINDOW // tokens
    part = tokens // 2
    half, place, col = lax.axis_index("half"), lax.axis_index("place"), lax.axis_index("cols")
    meta = jnp.stack([place, half, col]).astype(jnp.int32)
    bf16, f32 = jnp.bfloat16, jnp.float32
    shaped = jax.ShapeDtypeStruct

    deep = query_weight.shape[0]
    kv_cut, *cut = run(
        functools.partial(cut_kernel, n),
        [shaped((deep, n * 2 * HD), bf16)] + [shaped((deep, (2 + heads) * HD), bf16)] * n,
        [SMEM, VMEM, VMEM, VMEM],
        [VMEM] * (n + 1),
        [],
        0,
        5 * query_weight.size * 2,
    )(meta, query_weight, key_weight, value_weight)
    kv_rows = lax.all_gather(kv_cut, "half", axis=0, tiled=True)

    wide = activations.astype(f32)
    squares = jnp.sum(wide * wide, axis=-1).reshape(2, part)
    squares = (squares + swapped(squares, 0, 1)).reshape(tokens, 1)
    inverse = lax.rsqrt(squares / (2 * features) + 1e-06)
    gain = lax.dynamic_slice_in_dim(input_gain, col * features, features, 0)
    normed = (wide * inverse * gain).astype(bf16)

    z, y, c = n // 2, n // 4, 1
    blocks = {(0, 0): normed}
    blocks[y, 0] = swapped(normed, y, 0)
    blocks[0, 1] = swapped(normed, 0, 1)
    blocks[z, 0] = swapped(normed, z, 0)
    blocks[y, 1] = swapped(blocks[y, 0], 0, 1)
    blocks[z, 1] = swapped(blocks[z, 0], 0, 1)
    blocks[z + y, 0] = swapped(blocks[z, 0], y, 0)
    blocks[z + y, 1] = swapped(blocks[z + y, 0], 0, 1)
    for m, side in list(blocks):
        blocks[m + c, side] = swapped(blocks[m, side], c, 0)
    block_list = [blocks[m, side] for m in range(n) for side in range(2)]

    in_half = lax.dynamic_slice_in_dim(positions, half * n * tokens, n * tokens, 0)
    frequency = 10000.0 ** (-(jnp.arange(HD // 2, dtype=f32) * 2.0 / HD))
    angles = in_half.astype(f32)[:, None] * frequency[None, :]
    cosine, sine = jnp.cos(angles), jnp.sin(angles)
    cosine = jnp.concatenate([cosine, cosine], -1).reshape(n, tokens, HD)
    sine = jnp.concatenate([-sine, sine], -1).reshape(n, tokens, HD)
    index = jnp.arange(positions.shape[0], dtype=jnp.int32)
    starts = jnp.concatenate(
        [jnp.full((reach * tokens,), -(2**30), jnp.int32), index - positions], 0
    )
    docs = lax.dynamic_slice_in_dim(starts, half * n * tokens, (n + reach) * tokens, 0)
    k_doc = docs.reshape(n + reach, 1, tokens)
    q_doc = docs[reach * tokens :].reshape(n, tokens, 1)

    near = [cut[0]] + [swapped(cut[m], m, 0) for m in range(1, n)]
    q_own = run(
        join_kernel,
        shaped((n * deep, heads * HD), bf16),
        [VMEM] * n,
        VMEM,
        [],
        0,
        6 * n * deep * heads * HD,
    )(*near)
    q_rows = lax.all_gather(q_own, "half", axis=0, tiled=True)
    kv_rows, cosine, sine, q_doc = lax.optimization_barrier((kv_rows, cosine, sine, q_doc))
    far = []
    for m in range(n):
        first = lax.bitwise_xor(place, m) * 2 * HD
        piece = lax.dynamic_slice(kv_rows, ((1 - half) * deep, first), (deep, 2 * HD))
        far.append(piece if m == 0 else swapped(piece, m, 0))

    flops = 2 * n * tokens * 2 * features * (2 + heads) * HD
    kv_own, kv_tail, queries = run(
        functools.partial(project_kernel, n, reach, heads),
        [
            shaped((n, tokens, 2 * HD), bf16),
            shaped((reach, tokens, 2 * HD), bf16),
            shaped((n, heads * tokens, HD), bf16),
        ],
        [SMEM, VMEM, VMEM, VMEM, VMEM] + [ANY] * (4 * n + 1),
        [VMEM, VMEM, VMEM],
        [
            pltpu.VMEM((2, n, tokens, features), bf16),
            pltpu.VMEM((2, features, (2 + heads) * HD), bf16),
            pltpu.SemaphoreType.DMA((n, 2)),
            pltpu.SemaphoreType.DMA((3 * n,)),
        ],
        flops,
        2 * n * tokens * features * 2,
    )(
        meta,
        cosine,
        sine,
        key_gain.reshape(1, HD),
        query_gain.reshape(1, HD),
        *block_list,
        *near,
        *far,
        q_rows,
    )
    kv_back = lax.ppermute(kv_tail, "half", [(0, 1)])

    own_weight = output_weight.T
    ahead = own_weight.shape[0] // 32 * 16
    own_weight, _ = lax.optimization_barrier((own_weight, q_own))
    out_weights = [own_weight, swapped(own_weight, 0, 1)]
    for rows in [own_weight[:ahead], own_weight[ahead:]]:
        both = lax.all_gather(rows, "half", axis=0)
        piece = lax.dynamic_index_in_dim(both, 1 - half, 0, keepdims=False)
        out_weights += [piece, swapped(piece, 0, 1)]

    contexts = []
    spans = [(reach, n - reach), (0, reach)]
    for low, count in spans:
        backs = [kv_back] if low < reach else []
        shape = shaped((count, part, heads * HD), bf16)
        keep, send = run(
            functools.partial(attend_kernel, low, count, reach, heads),
            [shape, shape],
            [SMEM] + [VMEM] * (4 + len(backs)),
            [VMEM, VMEM],
            [],
            8 * count * heads * tokens * (reach + 1) * tokens * HD,
            4 * n * tokens * 2 * HD,
        )(meta, q_doc, k_doc, queries, kv_own, *backs)
        there = swapped(send, 0, 1)
        pair = run(
            pair_kernel,
            shaped((2, count, part, heads * HD), bf16),
            [VMEM, VMEM],
            VMEM,
            [],
            0,
            8 * count * part * heads * HD,
        )(keep, there)
        pairs = {0: pair}
        pairs[z] = swapped(pair, z, 0)
        pairs[y] = swapped(pair, y, 0)
        pairs[z + y] = swapped(pairs[z], y, 0)
        for m in list(pairs):
            pairs[m + c] = swapped(pairs[m], c, 0)
        contexts += [pairs[m] for m in range(n)]

    out_cols = output_weight.shape[1]
    deep_out = output_weight.shape[0]
    result = run(
        functools.partial(output_kernel, n, spans),
        shaped((2 * n, part, out_cols), bf16),
        [SMEM] + [ANY] * (2 * n + 6),
        VMEM,
        [
            pltpu.VMEM((n, part, 2 * deep_out), bf16),
            pltpu.VMEM((2, out_cols, 2 * deep_out), bf16),
            pltpu.SemaphoreType.DMA((4 * n,)),
            pltpu.SemaphoreType.DMA((6,)),
        ],
        2 * n * part * 2 * deep_out * 2 * out_cols,
        16 * deep_out * out_cols,
    )(meta, *contexts, *out_weights)

    arrived = lax.all_to_all(result, ("place", "cols"), 0, 0, tiled=True)
    return run(
        functools.partial(close_kernel, n),
        shaped((tokens, features), bf16),
        [VMEM, VMEM],
        VMEM,
        [],
        0,
        6 * tokens * features,
    )(activations, arrived)


def solution(mesh):
    sizes = mesh.shape
    if sizes["cols"] == 2 and sizes["sub"] == 1 and sizes["rows"] == 16:
        shape = (sizes["groups"], 2, sizes["rows"] // 2, sizes["cols"], sizes["sub"])
        names = ("groups", "half", "place", "cols", "sub")
        fine, rows = Mesh(mesh.devices.reshape(shape), names), ("half", "place")
    else:
        fine, rows = mesh, ("rows",)
    columns = ("cols", "sub")
    placed = (
        P(("groups", *rows), columns),
        P("groups"),
        P(rows, columns),
        P(rows, columns),
        P(rows, columns),
        P(columns, rows),
        P(),
        P(),
        P(),
    )

    def mapped(body):
        return jax.shard_map(
            body, mesh=fine, in_specs=placed, out_specs=placed[0], check_vma=False
        )

    if fine is mesh:
        return mapped(gathered_body)

    return mapped(split_body)
```

```python
import functools
import math

import jax
import jax.numpy as jnp
from jax import lax
from jax.experimental import pallas as pl
from jax.experimental.pallas import tpu as pltpu
from jax.sharding import Mesh
from jax.sharding import PartitionSpec as P


HD = 128
WINDOW = 1024
QUERY_SCALAR = 168
VMEM_BYTES = 67_000_000
ANY = pl.BlockSpec(memory_space=pl.ANY)
VMEM = pl.BlockSpec(memory_space=pltpu.VMEM)
SMEM = pl.BlockSpec(memory_space=pltpu.SMEM)


def passed_along(value, axis, by):
    peers = lax.axis_size(axis)
    pairs = [(i, i + by) for i in range(peers) if 0 <= i + by < peers]
    return lax.ppermute(value, axis, pairs)


def head_norm(tensor, gain_vector):
    return (
        tensor * lax.rsqrt(jnp.mean(tensor * tensor, axis=-1, keepdims=True) + 1e-06) * gain_vector
    )


def rotate(tensor, token_positions):
    half_width = tensor.shape[-1] // 2
    frequency = 10000.0 ** (-(jnp.arange(half_width, dtype=jnp.float32) * 2.0 / tensor.shape[-1]))
    angles = token_positions.astype(jnp.float32)[:, None] * frequency[None, :]
    cosine = jnp.cos(angles)[:, None, :]
    sine_part = jnp.sin(angles)[:, None, :]
    first_half = tensor[..., :half_width]
    second_half = tensor[..., half_width:]
    return jnp.concatenate(
        [
            first_half * cosine - second_half * sine_part,
            second_half * cosine + first_half * sine_part,
        ],
        axis=-1,
    )


def attend(queries, key_rows, value_rows, query_index, key_index, query_pos, key_pos):
    row_count = queries.shape[0]
    key_count = key_rows.shape[0]
    kv_heads = key_rows.shape[1] // HD
    group_size = queries.shape[1] // key_rows.shape[1]
    query_four = queries.reshape(row_count, kv_heads, group_size, HD)
    key_three = key_rows.reshape(key_count, kv_heads, HD)
    value_three = value_rows.reshape(key_count, kv_heads, HD)
    score_scale = 1.0 / math.sqrt(QUERY_SCALAR)
    scores = (
        jnp.einsum("qgrd,kgd->grqk", query_four, key_three, preferred_element_type=jnp.float32)
        * score_scale
    )
    distance = query_index[:, None] - key_index[None, :]
    visible = (
        (key_index[None, :] >= 0)
        & (distance >= 0)
        & (distance < WINDOW)
        & (query_pos[:, None] - key_pos[None, :] == distance)
    )
    weights = jnp.where(visible[None, None], jnp.exp(scores), 0.0)
    totals = jnp.sum(weights, axis=-1)
    rounded = weights.astype(jnp.bfloat16)
    mixed_heads = jnp.einsum(
        "grqk,kgd->qgrd", rounded, value_three, preferred_element_type=jnp.float32
    )
    mixed_heads = mixed_heads / jnp.transpose(totals, (2, 0, 1))[..., None]
    return mixed_heads.astype(jnp.bfloat16).reshape(row_count, kv_heads * group_size * HD)


def reach_back(key_rows, value_rows, reach_rows):
    pieces = []
    carried = (key_rows, value_rows)
    for _ in range(reach_rows):
        carried = passed_along((carried[0], carried[1]), "rows", 1)
        pieces.append(carried)
    ordered = pieces[::-1] + [(key_rows, value_rows)]
    all_keys = jnp.concatenate([member[0] for member in ordered], axis=0)
    all_values = jnp.concatenate([member[1] for member in ordered], axis=0)
    return (all_keys, all_values)


def gathered_body(
    activations,
    positions,
    query_weight,
    key_weight,
    value_weight,
    output_weight,
    input_gain,
    query_gain,
    key_gain,
):
    rows_here = activations.shape[0]
    row_panel = lax.all_gather(activations, ("cols", "sub"), axis=1, tiled=True)
    panel_wide = row_panel.astype(jnp.float32)
    inverse = lax.rsqrt(jnp.mean(panel_wide * panel_wide, axis=-1, keepdims=True) + 1e-06)
    normed = (panel_wide * inverse * input_gain).astype(jnp.bfloat16)
    row_index = lax.axis_index("rows")
    own_positions = lax.dynamic_slice_in_dim(positions, row_index * rows_here, rows_here, 0)
    reach_rows = min(-(-WINDOW // rows_here), lax.axis_size("rows") - 1)

    def add_rows(weight_piece):
        return jnp.dot(normed, weight_piece, preferred_element_type=jnp.float32)

    query_raw = add_rows(lax.all_gather(query_weight, "rows", axis=0, tiled=True))
    key_raw = add_rows(lax.all_gather(key_weight, "rows", axis=0, tiled=True))
    value_raw = add_rows(lax.all_gather(value_weight, "rows", axis=0, tiled=True))
    key_rows = rotate(head_norm(key_raw.reshape(rows_here, -1, HD), key_gain), own_positions)
    key_rows, value_rows = (
        key_rows.astype(jnp.bfloat16).reshape(rows_here, -1),
        value_raw.astype(jnp.bfloat16),
    )
    all_keys, all_values = reach_back(key_rows, value_rows, reach_rows)
    queries = rotate(head_norm(query_raw.reshape(rows_here, -1, HD), query_gain), own_positions)
    queries = queries.astype(jnp.bfloat16).reshape(rows_here, -1)
    key_count = all_keys.shape[0]
    query_index = row_index * rows_here + jnp.arange(rows_here, dtype=jnp.int32)
    key_index = (row_index - reach_rows) * rows_here + jnp.arange(key_count, dtype=jnp.int32)
    padded = jnp.concatenate([jnp.zeros((reach_rows * rows_here,), jnp.int32), positions], axis=0)
    key_positions = lax.dynamic_slice_in_dim(padded, row_index * rows_here, key_count, 0)
    context = attend(
        queries, all_keys, all_values, query_index, key_index, own_positions, key_positions
    )
    partial_terms = jnp.dot(
        context,
        lax.all_gather(output_weight, "rows", axis=1, tiled=True),
        preferred_element_type=jnp.float32,
    )
    summed = lax.psum_scatter(
        partial_terms.astype(jnp.bfloat16), ("cols", "sub"), scatter_dimension=1, tiled=True
    ).astype(jnp.float32)
    return (activations.astype(jnp.float32) + summed).astype(jnp.bfloat16)


def swapped(value, place=0, col=0):
    places, cols = lax.axis_size("place"), lax.axis_size("cols")
    pairs = [
        (r * cols + c, (r ^ place) * cols + (c ^ col)) for r in range(places) for c in range(cols)
    ]
    return lax.ppermute(value, ("place", "cols"), pairs)


def run(kernel, out_shape, in_specs, out_specs, scratch, flops, bytes_moved):
    return pl.pallas_call(
        kernel,
        out_shape=out_shape,
        in_specs=in_specs,
        out_specs=out_specs,
        scratch_shapes=scratch,
        compiler_params=pltpu.CompilerParams(vmem_limit_bytes=VMEM_BYTES),
        cost_estimate=pl.CostEstimate(
            flops=int(flops), bytes_accessed=int(bytes_moved), transcendentals=0
        ),
    )


def cut_kernel(n, meta, wq, wk, wv, kv_out, *q_outs):
    place = meta[0]
    wide_q = wq.shape[1] // n
    for p in range(n):
        kv_out[:, p * 2 * HD : p * 2 * HD + HD] = wk[:, p * HD : (p + 1) * HD]
        kv_out[:, p * 2 * HD + HD : (p + 1) * 2 * HD] = wv[:, p * HD : (p + 1) * HD]
    for m in range(n):
        at = lax.bitwise_xor(place, m)
        q_outs[m][...] = wq[:, pl.ds(pl.multiple_of(at * wide_q, 128), wide_q)]


def join_kernel(*refs):
    out = refs[-1]
    deep = refs[0].shape[0]
    for m, piece in enumerate(refs[:-1]):
        out[m * deep : (m + 1) * deep] = piece[...]


def pair_kernel(first, second, out):
    out[0] = first[...]
    out[1] = second[...]


def normed_rotated(raw, gain, cosine, sine):
    scaled = raw * lax.rsqrt(jnp.mean(raw * raw, axis=-1, keepdims=True) + 1e-06) * gain
    return scaled * cosine + pltpu.roll(scaled, HD // 2, 1) * sine


def project_kernel(n, reach, heads, meta, cosine, sine, key_gain, query_gain, *refs):
    blocks, kv_parts = refs[: 2 * n], refs[2 * n : 3 * n]
    q_rows = refs[3 * n]
    kv_out, tail_out, q_out = refs[3 * n + 1 : 3 * n + 4]
    block_mem, weight_mem, block_sem, weight_sem = refs[3 * n + 4 :]
    place, col = meta[0], meta[2]
    _, _, tokens, features = block_mem.shape
    deep = kv_parts[0].shape[0] // 2
    copies = []
    for m in range(n):
        rows = pl.ds(pl.multiple_of(lax.bitwise_xor(place, m) * deep, 16), deep)
        for half in range(2):
            for k, (source, target) in enumerate(
                [
                    (
                        kv_parts[m].at[pl.ds(half * deep, deep)],
                        weight_mem.at[half, rows, pl.ds(0, 2 * HD)],
                    ),
                    (
                        q_rows.at[pl.ds((half * n + m) * deep, deep)],
                        weight_mem.at[half, rows, pl.ds(2 * HD, heads * HD)],
                    ),
                ]
            ):
                sem = weight_sem.at[4 * m + 2 * half + k]
                copies.append(pltpu.make_async_copy(source, target, sem))
    for copy in copies:
        copy.start()
    for m in range(n):
        for side in range(2):
            pltpu.make_async_copy(
                blocks[m * 2 + side], block_mem.at[side, m], block_sem.at[m, side]
            ).start()
    for copy in copies:
        copy.wait()

    @pl.loop(0, n // 2)
    def _(t):
        for m in range(2):
            for side in range(2):
                pltpu.make_async_copy(
                    blocks[side], block_mem.at[side, 2 * t + m], block_sem.at[2 * t + m, side]
                ).wait()
        mine = block_mem[0, pl.ds(2 * t, 2)].reshape(2 * tokens, features)
        theirs = block_mem[1, pl.ds(2 * t, 2)].reshape(2 * tokens, features)
        raw_two = jnp.dot(mine, weight_mem[col], preferred_element_type=jnp.float32) + jnp.dot(
            theirs, weight_mem[lax.bitwise_xor(col, 1)], preferred_element_type=jnp.float32
        )
        for m in range(2):
            slot = 2 * t + m
            at = lax.bitwise_xor(place, slot)
            raw = raw_two[m * tokens : (m + 1) * tokens]
            cosine_here, sine_here = cosine[at], sine[at]
            keys = normed_rotated(raw[:, :HD], key_gain[...], cosine_here, sine_here)
            keys = keys.astype(jnp.bfloat16)
            values = raw[:, HD : 2 * HD].astype(jnp.bfloat16)
            kv_out[at, :, :HD] = keys
            kv_out[at, :, HD:] = values
            for h in range(heads):
                query = raw[:, (2 + h) * HD : (3 + h) * HD]
                query = normed_rotated(query, query_gain[...], cosine_here, sine_here)
                q_out[at, pl.ds(h * tokens, tokens), :] = query.astype(jnp.bfloat16)

            @pl.when(at >= n - reach)
            def _():
                tail_out[at - (n - reach), :, :HD] = keys
                tail_out[at - (n - reach), :, HD:] = values


def attend_kernel(low, count, reach, heads, meta, q_doc, k_doc, queries, kv_own, *refs):
    kv_back = refs[0] if low < reach else None
    keep_out, send_out = refs[-2:]
    col = meta[2]
    tokens = kv_own.shape[1]
    part = tokens // 2
    scale = 1.0 / math.sqrt(QUERY_SCALAR)
    row_at = lax.broadcasted_iota(jnp.int32, (tokens, tokens), 0)
    col_at = lax.broadcasted_iota(jnp.int32, (tokens, tokens), 1)

    for g in range(count):
        doc = q_doc[low + g]
        query = queries[low + g]
        totals = jnp.zeros((heads * tokens, 1), jnp.float32)
        mixed = jnp.zeros((heads * tokens, HD), jnp.float32)
        for step in range(reach + 1):
            at = low + g + step
            pair = kv_back[at] if at < reach else kv_own[at - reach]
            visible = doc == k_doc[at]
            if step == 0:
                visible = visible & (row_at < col_at)
            if step == reach:
                visible = visible & (row_at >= col_at)
            scores = lax.dot_general(
                query, pair[:, :HD], (((1,), (1,)), ((), ())), preferred_element_type=jnp.float32
            )
            weights_here = jnp.where(
                visible[None], jnp.exp(scores * scale).reshape(heads, tokens, tokens), 0.0
            ).reshape(heads * tokens, tokens)
            totals = totals + jnp.sum(weights_here, axis=-1, keepdims=True)
            mixed = mixed + jnp.dot(
                weights_here.astype(jnp.bfloat16), pair[:, HD:], preferred_element_type=jnp.float32
            )
        done = (mixed / totals).astype(jnp.bfloat16)
        for h in range(heads):
            top = done[h * tokens : h * tokens + part]
            bottom = done[h * tokens + part : (h + 1) * tokens]
            keep_out[g, :, h * HD : (h + 1) * HD] = jnp.where(col == 0, top, bottom)
            send_out[g, :, h * HD : (h + 1) * HD] = jnp.where(col == 0, bottom, top)


def output_kernel(n, spans, meta, *refs):
    count = n * len(spans)
    contexts, weights = refs[:count], refs[count : count + 6]
    out, context_mem, weight_mem, context_sem, weight_sem = refs[count + 6 :]
    place, half, col = meta[0], meta[1], meta[2]
    deep = weights[0].shape[1]
    wide = contexts[0].shape[3]
    part = contexts[0].shape[2]
    copies = []
    for k, source in enumerate(weights):
        owner = half if k < 2 else lax.bitwise_xor(half, 1)
        rows = source.shape[0]
        first = 0 if k < 4 else weights[2].shape[0]
        side = pl.multiple_of(lax.bitwise_xor(col, k % 2) * deep, 128)
        copies.append(
            pltpu.make_async_copy(
                source,
                weight_mem.at[owner, pl.ds(first, rows), pl.ds(side, deep)],
                weight_sem.at[k],
            )
        )
    for s, (low, size) in enumerate(spans):
        for m in range(n):
            for side in range(2):
                first = lax.bitwise_xor(col, side) * deep + lax.bitwise_xor(place, m) * wide
                copies.append(
                    pltpu.make_async_copy(
                        contexts[s * n + m].at[side],
                        context_mem.at[
                            pl.ds(low, size), :, pl.ds(pl.multiple_of(first, 128), wide)
                        ],
                        context_sem.at[(s * n + m) * 2 + side],
                    )
                )
    for copy in copies:
        copy.start()
    for copy in copies:
        copy.wait()

    @pl.loop(0, n // 4)
    def _(t):
        left = context_mem[pl.ds(4 * t, 4)].reshape(4 * part, 2 * deep)
        for block in range(2):
            result = lax.dot_general(
                left,
                weight_mem[block],
                (((1,), (1,)), ((), ())),
                preferred_element_type=jnp.float32,
            ).astype(jnp.bfloat16)
            for k in range(4):
                out[(4 * t + k) * 2 + block] = result[k * part : (k + 1) * part]


def close_kernel(n, activations, arrived, out):
    part = arrived.shape[1]
    for col in range(2):
        rows = pl.ds(col * part, part)
        whole = jnp.concatenate([arrived[2 * p + col] for p in range(n)], axis=1)
        out[rows, :] = (
            activations[rows, :].astype(jnp.float32) + whole.astype(jnp.float32)
        ).astype(jnp.bfloat16)


def split_body(
    activations,
    positions,
    query_weight,
    key_weight,
    value_weight,
    output_weight,
    input_gain,
    query_gain,
    key_gain,
):
    tokens, features = activations.shape
    n = key_weight.shape[1] // HD
    heads = query_weight.shape[1] // key_weight.shape[1]
    reach = WINDOW // tokens
    part = tokens // 2
    half, place, col = lax.axis_index("half"), lax.axis_index("place"), lax.axis_index("cols")
    meta = jnp.stack([place, half, col]).astype(jnp.int32)
    bf16, f32 = jnp.bfloat16, jnp.float32
    shaped = jax.ShapeDtypeStruct

    deep = query_weight.shape[0]
    kv_cut, *cut = run(
        functools.partial(cut_kernel, n),
        [shaped((deep, n * 2 * HD), bf16)] + [shaped((deep, heads * HD), bf16)] * n,
        [SMEM, VMEM, VMEM, VMEM],
        [VMEM] * (n + 1),
        [],
        0,
        4 * query_weight.size * 2,
    )(meta, query_weight, key_weight, value_weight)
    kv_rows = lax.all_gather(kv_cut, "half", axis=0, tiled=True)

    wide = activations.astype(f32)
    squares = jnp.sum(wide * wide, axis=-1).reshape(2, part)
    squares = (squares + swapped(squares, 0, 1)).reshape(tokens, 1)
    inverse = lax.rsqrt(squares / (2 * features) + 1e-06)
    gain = lax.dynamic_slice_in_dim(input_gain, col * features, features, 0)
    normed = (wide * inverse * gain).astype(bf16)

    z, y, c = n // 2, n // 4, 1
    blocks = {(0, 0): normed}
    blocks[y, 0] = swapped(normed, y, 0)
    blocks[0, 1] = swapped(normed, 0, 1)
    blocks[z, 0] = swapped(normed, z, 0)
    blocks[y, 1] = swapped(blocks[y, 0], 0, 1)
    blocks[z, 1] = swapped(blocks[z, 0], 0, 1)
    blocks[z + y, 0] = swapped(blocks[z, 0], y, 0)
    blocks[z + y, 1] = swapped(blocks[z + y, 0], 0, 1)
    for m, side in list(blocks):
        blocks[m + c, side] = swapped(blocks[m, side], c, 0)
    block_list = [blocks[m, side] for m in range(n) for side in range(2)]

    in_half = lax.dynamic_slice_in_dim(positions, half * n * tokens, n * tokens, 0)
    frequency = 10000.0 ** (-(jnp.arange(HD // 2, dtype=f32) * 2.0 / HD))
    angles = in_half.astype(f32)[:, None] * frequency[None, :]
    cosine, sine = jnp.cos(angles), jnp.sin(angles)
    cosine = jnp.concatenate([cosine, cosine], -1).reshape(n, tokens, HD)
    sine = jnp.concatenate([-sine, sine], -1).reshape(n, tokens, HD)
    index = jnp.arange(positions.shape[0], dtype=jnp.int32)
    starts = jnp.concatenate(
        [jnp.full((reach * tokens,), -(2**30), jnp.int32), index - positions], 0
    )
    docs = lax.dynamic_slice_in_dim(starts, half * n * tokens, (n + reach) * tokens, 0)
    k_doc = docs.reshape(n + reach, 1, tokens)
    q_doc = docs[reach * tokens :].reshape(n, tokens, 1)

    near = [cut[0]] + [swapped(cut[m], m, 0) for m in range(1, n)]
    q_own = run(
        join_kernel,
        shaped((n * deep, heads * HD), bf16),
        [VMEM] * n,
        VMEM,
        [],
        0,
        4 * n * deep * heads * HD,
    )(*near)
    q_rows = lax.all_gather(q_own, "half", axis=0, tiled=True)
    kv_rows, cosine, sine, q_doc = lax.optimization_barrier((kv_rows, cosine, sine, q_doc))
    kv_parts = []
    for m in range(n):
        first = lax.bitwise_xor(place, m) * 2 * HD
        piece = lax.dynamic_slice_in_dim(kv_rows, first, 2 * HD, 1)
        kv_parts.append(piece if m == 0 else swapped(piece, m, 0))

    flops = 2 * n * tokens * 2 * features * (2 + heads) * HD
    kv_own, kv_tail, queries = run(
        functools.partial(project_kernel, n, reach, heads),
        [
            shaped((n, tokens, 2 * HD), bf16),
            shaped((reach, tokens, 2 * HD), bf16),
            shaped((n, heads * tokens, HD), bf16),
        ],
        [SMEM, VMEM, VMEM, VMEM, VMEM] + [ANY] * (3 * n + 1),
        [VMEM, VMEM, VMEM],
        [
            pltpu.VMEM((2, n, tokens, features), bf16),
            pltpu.VMEM((2, features, (2 + heads) * HD), bf16),
            pltpu.SemaphoreType.DMA((n, 2)),
            pltpu.SemaphoreType.DMA((4 * n,)),
        ],
        flops,
        2 * n * tokens * features * 2,
    )(
        meta,
        cosine,
        sine,
        key_gain.reshape(1, HD),
        query_gain.reshape(1, HD),
        *block_list,
        *kv_parts,
        q_rows,
    )
    kv_back = lax.ppermute(kv_tail, "half", [(0, 1)])

    own_weight = output_weight.T
    ahead = own_weight.shape[0] // 32 * 16
    own_weight, _ = lax.optimization_barrier((own_weight, q_own))
    out_weights = [own_weight, swapped(own_weight, 0, 1)]
    for rows in [own_weight[:ahead], own_weight[ahead:]]:
        both = lax.all_gather(rows, "half", axis=0)
        piece = lax.dynamic_index_in_dim(both, 1 - half, 0, keepdims=False)
        out_weights += [piece, swapped(piece, 0, 1)]

    contexts = []
    spans = [(reach, n - reach), (0, reach)]
    for low, count in spans:
        backs = [kv_back] if low < reach else []
        shape = shaped((count, part, heads * HD), bf16)
        keep, send = run(
            functools.partial(attend_kernel, low, count, reach, heads),
            [shape, shape],
            [SMEM] + [VMEM] * (4 + len(backs)),
            [VMEM, VMEM],
            [],
            8 * count * heads * tokens * (reach + 1) * tokens * HD,
            4 * n * tokens * 2 * HD,
        )(meta, q_doc, k_doc, queries, kv_own, *backs)
        there = swapped(send, 0, 1)
        pair = run(
            pair_kernel,
            shaped((2, count, part, heads * HD), bf16),
            [VMEM, VMEM],
            VMEM,
            [],
            0,
            8 * count * part * heads * HD,
        )(keep, there)
        pairs = {0: pair}
        pairs[z] = swapped(pair, z, 0)
        pairs[y] = swapped(pair, y, 0)
        pairs[z + y] = swapped(pairs[z], y, 0)
        for m in list(pairs):
            pairs[m + c] = swapped(pairs[m], c, 0)
        contexts += [pairs[m] for m in range(n)]

    out_cols = output_weight.shape[1]
    deep_out = output_weight.shape[0]
    result = run(
        functools.partial(output_kernel, n, spans),
        shaped((2 * n, part, out_cols), bf16),
        [SMEM] + [ANY] * (2 * n + 6),
        VMEM,
        [
            pltpu.VMEM((n, part, 2 * deep_out), bf16),
            pltpu.VMEM((2, out_cols, 2 * deep_out), bf16),
            pltpu.SemaphoreType.DMA((4 * n,)),
            pltpu.SemaphoreType.DMA((6,)),
        ],
        2 * n * part * 2 * deep_out * 2 * out_cols,
        16 * deep_out * out_cols,
    )(meta, *contexts, *out_weights)

    arrived = lax.all_to_all(result, ("place", "cols"), 0, 0, tiled=True)
    return run(
        functools.partial(close_kernel, n),
        shaped((tokens, features), bf16),
        [VMEM, VMEM],
        VMEM,
        [],
        0,
        6 * tokens * features,
    )(activations, arrived)


def solution(mesh):
    sizes = mesh.shape
    if sizes["cols"] == 2 and sizes["sub"] == 1 and sizes["rows"] == 16:
        shape = (sizes["groups"], 2, sizes["rows"] // 2, sizes["cols"], sizes["sub"])
        names = ("groups", "half", "place", "cols", "sub")
        fine, rows = Mesh(mesh.devices.reshape(shape), names), ("half", "place")
    else:
        fine, rows = mesh, ("rows",)
    columns = ("cols", "sub")
    placed = (
        P(("groups", *rows), columns),
        P("groups"),
        P(rows, columns),
        P(rows, columns),
        P(rows, columns),
        P(columns, rows),
        P(),
        P(),
        P(),
    )

    def mapped(body):
        return jax.shard_map(
            body, mesh=fine, in_specs=placed, out_specs=placed[0], check_vma=False
        )

    if fine is mesh:
        return mapped(gathered_body)

    return mapped(split_body)
```

```python
import functools
import math

import jax
import jax.numpy as jnp
from jax import lax
from jax.experimental import pallas as pl
from jax.experimental.pallas import tpu as pltpu
from jax.sharding import Mesh
from jax.sharding import PartitionSpec as P


HD = 128
WINDOW = 1024
QUERY_SCALAR = 168
VMEM_BYTES = 67_000_000
ANY = pl.BlockSpec(memory_space=pl.ANY)
VMEM = pl.BlockSpec(memory_space=pltpu.VMEM)
SMEM = pl.BlockSpec(memory_space=pltpu.SMEM)


def passed_along(value, axis, by):
    peers = lax.axis_size(axis)
    pairs = [(i, i + by) for i in range(peers) if 0 <= i + by < peers]
    return lax.ppermute(value, axis, pairs)


def head_norm(tensor, gain_vector):
    return (
        tensor * lax.rsqrt(jnp.mean(tensor * tensor, axis=-1, keepdims=True) + 1e-06) * gain_vector
    )


def rotate(tensor, token_positions):
    half_width = tensor.shape[-1] // 2
    frequency = 10000.0 ** (-(jnp.arange(half_width, dtype=jnp.float32) * 2.0 / tensor.shape[-1]))
    angles = token_positions.astype(jnp.float32)[:, None] * frequency[None, :]
    cosine = jnp.cos(angles)[:, None, :]
    sine_part = jnp.sin(angles)[:, None, :]
    first_half = tensor[..., :half_width]
    second_half = tensor[..., half_width:]
    return jnp.concatenate(
        [
            first_half * cosine - second_half * sine_part,
            second_half * cosine + first_half * sine_part,
        ],
        axis=-1,
    )


def attend(queries, key_rows, value_rows, query_index, key_index, query_pos, key_pos):
    row_count = queries.shape[0]
    key_count = key_rows.shape[0]
    kv_heads = key_rows.shape[1] // HD
    group_size = queries.shape[1] // key_rows.shape[1]
    query_four = queries.reshape(row_count, kv_heads, group_size, HD)
    key_three = key_rows.reshape(key_count, kv_heads, HD)
    value_three = value_rows.reshape(key_count, kv_heads, HD)
    score_scale = 1.0 / math.sqrt(QUERY_SCALAR)
    scores = (
        jnp.einsum("qgrd,kgd->grqk", query_four, key_three, preferred_element_type=jnp.float32)
        * score_scale
    )
    distance = query_index[:, None] - key_index[None, :]
    visible = (
        (key_index[None, :] >= 0)
        & (distance >= 0)
        & (distance < WINDOW)
        & (query_pos[:, None] - key_pos[None, :] == distance)
    )
    weights = jnp.where(visible[None, None], jnp.exp(scores), 0.0)
    totals = jnp.sum(weights, axis=-1)
    rounded = weights.astype(jnp.bfloat16)
    mixed_heads = jnp.einsum(
        "grqk,kgd->qgrd", rounded, value_three, preferred_element_type=jnp.float32
    )
    mixed_heads = mixed_heads / jnp.transpose(totals, (2, 0, 1))[..., None]
    return mixed_heads.astype(jnp.bfloat16).reshape(row_count, kv_heads * group_size * HD)


def reach_back(key_rows, value_rows, reach_rows):
    pieces = []
    carried = (key_rows, value_rows)
    for _ in range(reach_rows):
        carried = passed_along((carried[0], carried[1]), "rows", 1)
        pieces.append(carried)
    ordered = pieces[::-1] + [(key_rows, value_rows)]
    all_keys = jnp.concatenate([member[0] for member in ordered], axis=0)
    all_values = jnp.concatenate([member[1] for member in ordered], axis=0)
    return (all_keys, all_values)


def gathered_body(
    activations,
    positions,
    query_weight,
    key_weight,
    value_weight,
    output_weight,
    input_gain,
    query_gain,
    key_gain,
):
    rows_here = activations.shape[0]
    row_panel = lax.all_gather(activations, ("cols", "sub"), axis=1, tiled=True)
    panel_wide = row_panel.astype(jnp.float32)
    inverse = lax.rsqrt(jnp.mean(panel_wide * panel_wide, axis=-1, keepdims=True) + 1e-06)
    normed = (panel_wide * inverse * input_gain).astype(jnp.bfloat16)
    row_index = lax.axis_index("rows")
    own_positions = lax.dynamic_slice_in_dim(positions, row_index * rows_here, rows_here, 0)
    reach_rows = min(-(-WINDOW // rows_here), lax.axis_size("rows") - 1)

    def add_rows(weight_piece):
        return jnp.dot(normed, weight_piece, preferred_element_type=jnp.float32)

    query_raw = add_rows(lax.all_gather(query_weight, "rows", axis=0, tiled=True))
    key_raw = add_rows(lax.all_gather(key_weight, "rows", axis=0, tiled=True))
    value_raw = add_rows(lax.all_gather(value_weight, "rows", axis=0, tiled=True))
    key_rows = rotate(head_norm(key_raw.reshape(rows_here, -1, HD), key_gain), own_positions)
    key_rows, value_rows = (
        key_rows.astype(jnp.bfloat16).reshape(rows_here, -1),
        value_raw.astype(jnp.bfloat16),
    )
    all_keys, all_values = reach_back(key_rows, value_rows, reach_rows)
    queries = rotate(head_norm(query_raw.reshape(rows_here, -1, HD), query_gain), own_positions)
    queries = queries.astype(jnp.bfloat16).reshape(rows_here, -1)
    key_count = all_keys.shape[0]
    query_index = row_index * rows_here + jnp.arange(rows_here, dtype=jnp.int32)
    key_index = (row_index - reach_rows) * rows_here + jnp.arange(key_count, dtype=jnp.int32)
    padded = jnp.concatenate([jnp.zeros((reach_rows * rows_here,), jnp.int32), positions], axis=0)
    key_positions = lax.dynamic_slice_in_dim(padded, row_index * rows_here, key_count, 0)
    context = attend(
        queries, all_keys, all_values, query_index, key_index, own_positions, key_positions
    )
    partial_terms = jnp.dot(
        context,
        lax.all_gather(output_weight, "rows", axis=1, tiled=True),
        preferred_element_type=jnp.float32,
    )
    summed = lax.psum_scatter(
        partial_terms.astype(jnp.bfloat16), ("cols", "sub"), scatter_dimension=1, tiled=True
    ).astype(jnp.float32)
    return (activations.astype(jnp.float32) + summed).astype(jnp.bfloat16)


def swapped(value, place=0, col=0):
    places, cols = lax.axis_size("place"), lax.axis_size("cols")
    pairs = [
        (r * cols + c, (r ^ place) * cols + (c ^ col)) for r in range(places) for c in range(cols)
    ]
    return lax.ppermute(value, ("place", "cols"), pairs)


def run(kernel, out_shape, in_specs, out_specs, scratch, flops, bytes_moved):
    return pl.pallas_call(
        kernel,
        out_shape=out_shape,
        in_specs=in_specs,
        out_specs=out_specs,
        scratch_shapes=scratch,
        compiler_params=pltpu.CompilerParams(vmem_limit_bytes=VMEM_BYTES),
        cost_estimate=pl.CostEstimate(
            flops=int(flops), bytes_accessed=int(bytes_moved), transcendentals=0
        ),
    )


def cut_kernel(n, meta, wq, wk, wv, kv_out, *q_outs):
    place = meta[0]
    wide_q = wq.shape[1] // n
    for p in range(n):
        kv_out[:, p * 2 * HD : p * 2 * HD + HD] = wk[:, p * HD : (p + 1) * HD]
        kv_out[:, p * 2 * HD + HD : (p + 1) * 2 * HD] = wv[:, p * HD : (p + 1) * HD]
    for m in range(n):
        at = lax.bitwise_xor(place, m)
        q_outs[m][...] = wq[:, pl.ds(pl.multiple_of(at * wide_q, 128), wide_q)]


def join_kernel(*refs):
    out = refs[-1]
    deep = refs[0].shape[0]
    for m, piece in enumerate(refs[:-1]):
        out[m * deep : (m + 1) * deep] = piece[...]


def pair_kernel(first, second, out):
    out[0] = first[...]
    out[1] = second[...]


def normed_rotated(raw, gain, cosine, sine):
    scaled = raw * lax.rsqrt(jnp.mean(raw * raw, axis=-1, keepdims=True) + 1e-06) * gain
    return scaled * cosine + pltpu.roll(scaled, HD // 2, 1) * sine


def project_kernel(n, reach, heads, meta, cosine, sine, key_gain, query_gain, *refs):
    blocks, kv_parts = refs[: 2 * n], refs[2 * n : 3 * n]
    q_rows = refs[3 * n]
    kv_out, tail_out, q_out = refs[3 * n + 1 : 3 * n + 4]
    block_mem, kv_mem, q_mem, block_sem, weight_sem = refs[3 * n + 4 :]
    place, col = meta[0], meta[2]
    _, _, tokens, features = block_mem.shape
    deep = kv_parts[0].shape[0] // 2
    copies = []
    for m in range(n):
        rows = pl.ds(pl.multiple_of(lax.bitwise_xor(place, m) * deep, 16), deep)
        for half in range(2):
            for k, (source, target) in enumerate(
                [
                    (kv_parts[m].at[pl.ds(half * deep, deep)], kv_mem.at[half, rows, :]),
                    (q_rows.at[pl.ds((half * n + m) * deep, deep)], q_mem.at[half, rows, :]),
                ]
            ):
                sem = weight_sem.at[4 * m + 2 * half + k]
                copies.append(pltpu.make_async_copy(source, target, sem))
    for copy in copies:
        copy.start()
    for m in range(n):
        for side in range(2):
            pltpu.make_async_copy(
                blocks[m * 2 + side], block_mem.at[side, m], block_sem.at[m, side]
            ).start()
    for copy in copies:
        copy.wait()

    @pl.loop(0, n // 2)
    def _(t):
        for m in range(2):
            for side in range(2):
                pltpu.make_async_copy(
                    blocks[side], block_mem.at[side, 2 * t + m], block_sem.at[2 * t + m, side]
                ).wait()
        mine = block_mem[0, pl.ds(2 * t, 2)].reshape(2 * tokens, features)
        theirs = block_mem[1, pl.ds(2 * t, 2)].reshape(2 * tokens, features)
        kv_two, q_two = [
            jnp.dot(mine, mem[col], preferred_element_type=jnp.float32)
            + jnp.dot(theirs, mem[lax.bitwise_xor(col, 1)], preferred_element_type=jnp.float32)
            for mem in (kv_mem, q_mem)
        ]
        for m in range(2):
            slot = 2 * t + m
            at = lax.bitwise_xor(place, slot)
            raw = kv_two[m * tokens : (m + 1) * tokens]
            cosine_here, sine_here = cosine[at], sine[at]
            keys = normed_rotated(raw[:, :HD], key_gain[...], cosine_here, sine_here)
            keys = keys.astype(jnp.bfloat16)
            values = raw[:, HD : 2 * HD].astype(jnp.bfloat16)
            kv_out[at, :, :HD] = keys
            kv_out[at, :, HD:] = values
            for h in range(heads):
                query = q_two[m * tokens : (m + 1) * tokens, h * HD : (h + 1) * HD]
                query = normed_rotated(query, query_gain[...], cosine_here, sine_here)
                q_out[at, pl.ds(h * tokens, tokens), :] = query.astype(jnp.bfloat16)

            @pl.when(at >= n - reach)
            def _():
                tail_out[at - (n - reach), :, :HD] = keys
                tail_out[at - (n - reach), :, HD:] = values


def attend_kernel(low, count, reach, heads, meta, q_doc, k_doc, queries, kv_own, *refs):
    kv_back = refs[0] if low < reach else None
    keep_out, send_out = refs[-2:]
    col = meta[2]
    tokens = kv_own.shape[1]
    part = tokens // 2
    scale = 1.0 / math.sqrt(QUERY_SCALAR)
    row_at = lax.broadcasted_iota(jnp.int32, (tokens, tokens), 0)
    col_at = lax.broadcasted_iota(jnp.int32, (tokens, tokens), 1)

    for g in range(count):
        doc = q_doc[low + g]
        query = queries[low + g]
        totals = jnp.zeros((heads * tokens, 1), jnp.float32)
        mixed = jnp.zeros((heads * tokens, HD), jnp.float32)
        for step in range(reach + 1):
            at = low + g + step
            pair = kv_back[at] if at < reach else kv_own[at - reach]
            visible = doc == k_doc[at]
            if step == 0:
                visible = visible & (row_at < col_at)
            if step == reach:
                visible = visible & (row_at >= col_at)
            scores = lax.dot_general(
                query, pair[:, :HD], (((1,), (1,)), ((), ())), preferred_element_type=jnp.float32
            )
            weights_here = jnp.where(
                visible[None], jnp.exp(scores * scale).reshape(heads, tokens, tokens), 0.0
            ).reshape(heads * tokens, tokens)
            totals = totals + jnp.sum(weights_here, axis=-1, keepdims=True)
            mixed = mixed + jnp.dot(
                weights_here.astype(jnp.bfloat16), pair[:, HD:], preferred_element_type=jnp.float32
            )
        done = (mixed / totals).astype(jnp.bfloat16)
        for h in range(heads):
            top = done[h * tokens : h * tokens + part]
            bottom = done[h * tokens + part : (h + 1) * tokens]
            keep_out[g, :, h * HD : (h + 1) * HD] = jnp.where(col == 0, top, bottom)
            send_out[g, :, h * HD : (h + 1) * HD] = jnp.where(col == 0, bottom, top)


def output_kernel(n, spans, far, meta, *refs):
    count = n * len(spans)
    contexts, weights = refs[:count], refs[count:-5]
    if far:
        weights, before = weights[:-1], weights[-1]
    out, context_mem, weight_mem, context_sem, weight_sem = refs[-5:]
    place, half, col = meta[0], meta[1], meta[2]
    deep = weights[0].shape[1]
    wide = contexts[0].shape[3]
    part = contexts[0].shape[2]
    copies = []
    for k, source in enumerate(weights):
        first = sum(weights[j].shape[0] for j in range(k % 2, k, 2))
        side = pl.multiple_of(lax.bitwise_xor(col, k % 2) * deep, 128)
        copies.append(
            pltpu.make_async_copy(
                source,
                weight_mem.at[pl.ds(first, source.shape[0]), pl.ds(side, deep)],
                weight_sem.at[k],
            )
        )
    for s, (low, size) in enumerate(spans):
        for m in range(n):
            for side in range(2):
                first = lax.bitwise_xor(col, side) * deep + lax.bitwise_xor(place, m) * wide
                copies.append(
                    pltpu.make_async_copy(
                        contexts[s * n + m].at[side],
                        context_mem.at[
                            pl.ds(low, size), :, pl.ds(pl.multiple_of(first, 128), wide)
                        ],
                        context_sem.at[(s * n + m) * 2 + side],
                    )
                )
    for copy in copies:
        copy.start()
    for copy in copies:
        copy.wait()

    @pl.loop(0, n // 4)
    def _(t):
        left = context_mem[pl.ds(4 * t, 4)].reshape(4 * part, 2 * deep)
        result = lax.dot_general(
            left, weight_mem[...], (((1,), (1,)), ((), ())), preferred_element_type=jnp.float32
        ).astype(jnp.bfloat16)
        for k in range(4):
            slab = result[k * part : (k + 1) * part]
            if far:
                out[2 * (4 * t + k) + lax.bitwise_xor(half, 1)] = slab
                out[2 * (4 * t + k) + half] = before[4 * t + k]
            else:
                out[4 * t + k] = slab


def close_kernel(n, activations, arrived, out):
    part = arrived.shape[1]
    for col in range(2):
        rows = pl.ds(col * part, part)
        whole = jnp.concatenate([arrived[2 * p + col] for p in range(n)], axis=1)
        out[rows, :] = (
            activations[rows, :].astype(jnp.float32) + whole.astype(jnp.float32)
        ).astype(jnp.bfloat16)


def split_body(
    activations,
    positions,
    query_weight,
    key_weight,
    value_weight,
    output_weight,
    input_gain,
    query_gain,
    key_gain,
):
    tokens, features = activations.shape
    n = key_weight.shape[1] // HD
    heads = query_weight.shape[1] // key_weight.shape[1]
    reach = WINDOW // tokens
    part = tokens // 2
    half, place, col = lax.axis_index("half"), lax.axis_index("place"), lax.axis_index("cols")
    meta = jnp.stack([place, half, col]).astype(jnp.int32)
    bf16, f32 = jnp.bfloat16, jnp.float32
    shaped = jax.ShapeDtypeStruct

    deep = query_weight.shape[0]
    kv_cut, *cut = run(
        functools.partial(cut_kernel, n),
        [shaped((deep, n * 2 * HD), bf16)] + [shaped((deep, heads * HD), bf16)] * n,
        [SMEM, VMEM, VMEM, VMEM],
        [VMEM] * (n + 1),
        [],
        0,
        4 * query_weight.size * 2,
    )(meta, query_weight, key_weight, value_weight)
    kv_rows = lax.all_gather(kv_cut, "half", axis=0, tiled=True)

    wide = activations.astype(f32)
    squares = jnp.sum(wide * wide, axis=-1).reshape(2, part)
    squares = (squares + swapped(squares, 0, 1)).reshape(tokens, 1)
    inverse = lax.rsqrt(squares / (2 * features) + 1e-06)
    gain = lax.dynamic_slice_in_dim(input_gain, col * features, features, 0)
    normed = (wide * inverse * gain).astype(bf16)

    z, y, c = n // 2, n // 4, 1
    blocks = {(0, 0): normed}
    blocks[y, 0] = swapped(normed, y, 0)
    blocks[0, 1] = swapped(normed, 0, 1)
    blocks[z, 0] = swapped(normed, z, 0)
    blocks[y, 1] = swapped(blocks[y, 0], 0, 1)
    blocks[z, 1] = swapped(blocks[z, 0], 0, 1)
    blocks[z + y, 0] = swapped(blocks[z, 0], y, 0)
    blocks[z + y, 1] = swapped(blocks[z + y, 0], 0, 1)
    for m, side in list(blocks):
        blocks[m + c, side] = swapped(blocks[m, side], c, 0)
    block_list = [blocks[m, side] for m in range(n) for side in range(2)]

    in_half = lax.dynamic_slice_in_dim(positions, half * n * tokens, n * tokens, 0)
    frequency = 10000.0 ** (-(jnp.arange(HD // 2, dtype=f32) * 2.0 / HD))
    angles = in_half.astype(f32)[:, None] * frequency[None, :]
    cosine, sine = jnp.cos(angles), jnp.sin(angles)
    cosine = jnp.concatenate([cosine, cosine], -1).reshape(n, tokens, HD)
    sine = jnp.concatenate([-sine, sine], -1).reshape(n, tokens, HD)
    index = jnp.arange(positions.shape[0], dtype=jnp.int32)
    starts = jnp.concatenate(
        [jnp.full((reach * tokens,), -(2**30), jnp.int32), index - positions], 0
    )
    docs = lax.dynamic_slice_in_dim(starts, half * n * tokens, (n + reach) * tokens, 0)
    k_doc = docs.reshape(n + reach, 1, tokens)
    q_doc = docs[reach * tokens :].reshape(n, tokens, 1)

    near = [cut[0]] + [swapped(cut[m], m, 0) for m in range(1, n)]
    q_own = run(
        join_kernel,
        shaped((n * deep, heads * HD), bf16),
        [VMEM] * n,
        VMEM,
        [],
        0,
        4 * n * deep * heads * HD,
    )(*near)
    q_rows = lax.all_gather(q_own, "half", axis=0, tiled=True)
    kv_rows, cosine, sine, q_doc = lax.optimization_barrier((kv_rows, cosine, sine, q_doc))
    kv_parts = []
    for m in range(n):
        first = lax.bitwise_xor(place, m) * 2 * HD
        piece = lax.dynamic_slice_in_dim(kv_rows, first, 2 * HD, 1)
        kv_parts.append(piece if m == 0 else swapped(piece, m, 0))

    flops = 2 * n * tokens * 2 * features * (2 + heads) * HD
    kv_own, kv_tail, queries = run(
        functools.partial(project_kernel, n, reach, heads),
        [
            shaped((n, tokens, 2 * HD), bf16),
            shaped((reach, tokens, 2 * HD), bf16),
            shaped((n, heads * tokens, HD), bf16),
        ],
        [SMEM, VMEM, VMEM, VMEM, VMEM] + [ANY] * (3 * n + 1),
        [VMEM, VMEM, VMEM],
        [
            pltpu.VMEM((2, n, tokens, features), bf16),
            pltpu.VMEM((2, features, 2 * HD), bf16),
            pltpu.VMEM((2, features, heads * HD), bf16),
            pltpu.SemaphoreType.DMA((n, 2)),
            pltpu.SemaphoreType.DMA((4 * n,)),
        ],
        flops,
        2 * n * tokens * features * 2,
    )(
        meta,
        cosine,
        sine,
        key_gain.reshape(1, HD),
        query_gain.reshape(1, HD),
        *block_list,
        *kv_parts,
        q_rows,
    )
    kv_back = lax.ppermute(kv_tail, "half", [(0, 1)])

    own_weight, _ = lax.optimization_barrier((output_weight.T, q_own))
    ahead = own_weight.shape[0] * 4 // 7 // 16 * 16
    near_weights = [own_weight, swapped(own_weight, 0, 1)]
    far_weights = []
    for rows in [own_weight[:ahead], own_weight[ahead:]]:
        both = lax.all_gather(rows, "half", axis=0)
        piece = lax.dynamic_index_in_dim(both, 1 - half, 0, keepdims=False)
        far_weights += [piece, swapped(piece, 0, 1)]

    contexts = []
    spans = [(reach, n - reach), (0, reach)]
    for low, count in spans:
        backs = [kv_back] if low < reach else []
        shape = shaped((count, part, heads * HD), bf16)
        keep, send = run(
            functools.partial(attend_kernel, low, count, reach, heads),
            [shape, shape],
            [SMEM] + [VMEM] * (4 + len(backs)),
            [VMEM, VMEM],
            [],
            8 * count * heads * tokens * (reach + 1) * tokens * HD,
            4 * n * tokens * 2 * HD,
        )(meta, q_doc, k_doc, queries, kv_own, *backs)
        there = swapped(send, 0, 1)
        pair = run(
            pair_kernel,
            shaped((2, count, part, heads * HD), bf16),
            [VMEM, VMEM],
            VMEM,
            [],
            0,
            8 * count * part * heads * HD,
        )(keep, there)
        pairs = {0: pair}
        pairs[z] = swapped(pair, z, 0)
        pairs[y] = swapped(pair, y, 0)
        pairs[z + y] = swapped(pairs[z], y, 0)
        for m in list(pairs):
            pairs[m + c] = swapped(pairs[m], c, 0)
        contexts += [pairs[m] for m in range(n)]

    out_cols = output_weight.shape[1]
    deep_out = output_weight.shape[0]
    result = []
    for weights, shape in ((near_weights, (n,)), (far_weights, (2 * n,))):
        result = [
            run(
                functools.partial(output_kernel, n, spans, len(result)),
                shaped((*shape, part, out_cols), bf16),
                [SMEM] + [ANY] * (2 * n + len(weights)) + [VMEM] * len(result),
                VMEM,
                [
                    pltpu.VMEM((n, part, 2 * deep_out), bf16),
                    pltpu.VMEM((out_cols, 2 * deep_out), bf16),
                    pltpu.SemaphoreType.DMA((4 * n,)),
                    pltpu.SemaphoreType.DMA((len(weights),)),
                ],
                2 * n * part * 2 * deep_out * out_cols,
                8 * deep_out * out_cols,
            )(meta, *contexts, *weights, *result)
        ]

    arrived = lax.all_to_all(result[0], ("place", "cols"), 0, 0, tiled=True)
    return run(
        functools.partial(close_kernel, n),
        shaped((tokens, features), bf16),
        [VMEM, VMEM],
        VMEM,
        [],
        0,
        6 * tokens * features,
    )(activations, arrived)


def solution(mesh):
    sizes = mesh.shape
    if sizes["cols"] == 2 and sizes["sub"] == 1 and sizes["rows"] == 16:
        shape = (sizes["groups"], 2, sizes["rows"] // 2, sizes["cols"], sizes["sub"])
        names = ("groups", "half", "place", "cols", "sub")
        fine, rows = Mesh(mesh.devices.reshape(shape), names), ("half", "place")
    else:
        fine, rows = mesh, ("rows",)
    columns = ("cols", "sub")
    placed = (
        P(("groups", *rows), columns),
        P("groups"),
        P(rows, columns),
        P(rows, columns),
        P(rows, columns),
        P(columns, rows),
        P(),
        P(),
        P(),
    )

    def mapped(body):
        return jax.shard_map(
            body, mesh=fine, in_specs=placed, out_specs=placed[0], check_vma=False
        )

    if fine is mesh:
        return mapped(gathered_body)

    return mapped(split_body)
```

```python
import functools
import math

import jax
import jax.numpy as jnp
from jax import lax
from jax.experimental import pallas as pl
from jax.experimental.pallas import tpu as pltpu
from jax.sharding import Mesh
from jax.sharding import PartitionSpec as P


HD = 128
WINDOW = 1024
QUERY_SCALAR = 168
VMEM_BYTES = 67_000_000
ANY = pl.BlockSpec(memory_space=pl.ANY)
VMEM = pl.BlockSpec(memory_space=pltpu.VMEM)
SMEM = pl.BlockSpec(memory_space=pltpu.SMEM)


def passed_along(value, axis, by):
    peers = lax.axis_size(axis)
    pairs = [(i, i + by) for i in range(peers) if 0 <= i + by < peers]
    return lax.ppermute(value, axis, pairs)


def head_norm(tensor, gain_vector):
    return (
        tensor * lax.rsqrt(jnp.mean(tensor * tensor, axis=-1, keepdims=True) + 1e-06) * gain_vector
    )


def rotate(tensor, token_positions):
    half_width = tensor.shape[-1] // 2
    frequency = 10000.0 ** (-(jnp.arange(half_width, dtype=jnp.float32) * 2.0 / tensor.shape[-1]))
    angles = token_positions.astype(jnp.float32)[:, None] * frequency[None, :]
    cosine = jnp.cos(angles)[:, None, :]
    sine_part = jnp.sin(angles)[:, None, :]
    first_half = tensor[..., :half_width]
    second_half = tensor[..., half_width:]
    return jnp.concatenate(
        [
            first_half * cosine - second_half * sine_part,
            second_half * cosine + first_half * sine_part,
        ],
        axis=-1,
    )


def attend(queries, key_rows, value_rows, query_index, key_index, query_pos, key_pos):
    row_count = queries.shape[0]
    key_count = key_rows.shape[0]
    kv_heads = key_rows.shape[1] // HD
    group_size = queries.shape[1] // key_rows.shape[1]
    query_four = queries.reshape(row_count, kv_heads, group_size, HD)
    key_three = key_rows.reshape(key_count, kv_heads, HD)
    value_three = value_rows.reshape(key_count, kv_heads, HD)
    score_scale = 1.0 / math.sqrt(QUERY_SCALAR)
    scores = (
        jnp.einsum("qgrd,kgd->grqk", query_four, key_three, preferred_element_type=jnp.float32)
        * score_scale
    )
    distance = query_index[:, None] - key_index[None, :]
    visible = (
        (key_index[None, :] >= 0)
        & (distance >= 0)
        & (distance < WINDOW)
        & (query_pos[:, None] - key_pos[None, :] == distance)
    )
    weights = jnp.where(visible[None, None], jnp.exp(scores), 0.0)
    totals = jnp.sum(weights, axis=-1)
    rounded = weights.astype(jnp.bfloat16)
    mixed_heads = jnp.einsum(
        "grqk,kgd->qgrd", rounded, value_three, preferred_element_type=jnp.float32
    )
    mixed_heads = mixed_heads / jnp.transpose(totals, (2, 0, 1))[..., None]
    return mixed_heads.astype(jnp.bfloat16).reshape(row_count, kv_heads * group_size * HD)


def reach_back(key_rows, value_rows, reach_rows):
    pieces = []
    carried = (key_rows, value_rows)
    for _ in range(reach_rows):
        carried = passed_along((carried[0], carried[1]), "rows", 1)
        pieces.append(carried)
    ordered = pieces[::-1] + [(key_rows, value_rows)]
    all_keys = jnp.concatenate([member[0] for member in ordered], axis=0)
    all_values = jnp.concatenate([member[1] for member in ordered], axis=0)
    return (all_keys, all_values)


def gathered_body(
    activations,
    positions,
    query_weight,
    key_weight,
    value_weight,
    output_weight,
    input_gain,
    query_gain,
    key_gain,
):
    rows_here = activations.shape[0]
    row_panel = lax.all_gather(activations, ("cols", "sub"), axis=1, tiled=True)
    panel_wide = row_panel.astype(jnp.float32)
    inverse = lax.rsqrt(jnp.mean(panel_wide * panel_wide, axis=-1, keepdims=True) + 1e-06)
    normed = (panel_wide * inverse * input_gain).astype(jnp.bfloat16)
    row_index = lax.axis_index("rows")
    own_positions = lax.dynamic_slice_in_dim(positions, row_index * rows_here, rows_here, 0)
    reach_rows = min(-(-WINDOW // rows_here), lax.axis_size("rows") - 1)

    def add_rows(weight_piece):
        return jnp.dot(normed, weight_piece, preferred_element_type=jnp.float32)

    query_raw = add_rows(lax.all_gather(query_weight, "rows", axis=0, tiled=True))
    key_raw = add_rows(lax.all_gather(key_weight, "rows", axis=0, tiled=True))
    value_raw = add_rows(lax.all_gather(value_weight, "rows", axis=0, tiled=True))
    key_rows = rotate(head_norm(key_raw.reshape(rows_here, -1, HD), key_gain), own_positions)
    key_rows, value_rows = (
        key_rows.astype(jnp.bfloat16).reshape(rows_here, -1),
        value_raw.astype(jnp.bfloat16),
    )
    all_keys, all_values = reach_back(key_rows, value_rows, reach_rows)
    queries = rotate(head_norm(query_raw.reshape(rows_here, -1, HD), query_gain), own_positions)
    queries = queries.astype(jnp.bfloat16).reshape(rows_here, -1)
    key_count = all_keys.shape[0]
    query_index = row_index * rows_here + jnp.arange(rows_here, dtype=jnp.int32)
    key_index = (row_index - reach_rows) * rows_here + jnp.arange(key_count, dtype=jnp.int32)
    padded = jnp.concatenate([jnp.zeros((reach_rows * rows_here,), jnp.int32), positions], axis=0)
    key_positions = lax.dynamic_slice_in_dim(padded, row_index * rows_here, key_count, 0)
    context = attend(
        queries, all_keys, all_values, query_index, key_index, own_positions, key_positions
    )
    partial_terms = jnp.dot(
        context,
        lax.all_gather(output_weight, "rows", axis=1, tiled=True),
        preferred_element_type=jnp.float32,
    )
    summed = lax.psum_scatter(
        partial_terms.astype(jnp.bfloat16), ("cols", "sub"), scatter_dimension=1, tiled=True
    ).astype(jnp.float32)
    return (activations.astype(jnp.float32) + summed).astype(jnp.bfloat16)


def swapped(value, place=0, col=0):
    places, cols = lax.axis_size("place"), lax.axis_size("cols")
    pairs = [
        (r * cols + c, (r ^ place) * cols + (c ^ col)) for r in range(places) for c in range(cols)
    ]
    return lax.ppermute(value, ("place", "cols"), pairs)


def run(kernel, out_shape, in_specs, out_specs, scratch, flops, bytes_moved):
    return pl.pallas_call(
        kernel,
        out_shape=out_shape,
        in_specs=in_specs,
        out_specs=out_specs,
        scratch_shapes=scratch,
        compiler_params=pltpu.CompilerParams(vmem_limit_bytes=VMEM_BYTES),
        cost_estimate=pl.CostEstimate(
            flops=int(flops), bytes_accessed=int(bytes_moved), transcendentals=0
        ),
    )


def cut_kernel(n, meta, wq, wk, wv, kv_out, *q_outs):
    place = meta[0]
    wide_q = wq.shape[1] // n
    for p in range(n):
        kv_out[:, p * 2 * HD : p * 2 * HD + HD] = wk[:, p * HD : (p + 1) * HD]
        kv_out[:, p * 2 * HD + HD : (p + 1) * 2 * HD] = wv[:, p * HD : (p + 1) * HD]
    for m in range(n):
        at = lax.bitwise_xor(place, m)
        q_outs[m][...] = wq[:, pl.ds(pl.multiple_of(at * wide_q, 128), wide_q)]


def join_kernel(*refs):
    out = refs[-1]
    deep = refs[0].shape[0]
    for m, piece in enumerate(refs[:-1]):
        out[m * deep : (m + 1) * deep] = piece[...]


def pair_kernel(first, second, out):
    out[0] = first[...]
    out[1] = second[...]


def normed_rotated(raw, gain, cosine, sine):
    scaled = raw * lax.rsqrt(jnp.mean(raw * raw, axis=-1, keepdims=True) + 1e-06) * gain
    return scaled * cosine + pltpu.roll(scaled, HD // 2, 1) * sine


def project_kernel(n, reach, heads, meta, cosine, sine, key_gain, query_gain, *refs):
    blocks, kv_parts = refs[: 2 * n], refs[2 * n : 3 * n]
    q_rows = refs[3 * n]
    kv_out, tail_out, q_out = refs[3 * n + 1 : 3 * n + 4]
    block_mem, kv_mem, q_mem, block_sem, weight_sem = refs[3 * n + 4 :]
    place, col = meta[0], meta[2]
    _, _, tokens, _ = block_mem.shape
    deep = kv_parts[0].shape[0] // 2
    copies = []
    for m in range(n):
        rows = pl.ds(pl.multiple_of(lax.bitwise_xor(place, m) * deep, 16), deep)
        for half in range(2):
            for k, (source, target) in enumerate(
                [
                    (kv_parts[m].at[pl.ds(half * deep, deep)], kv_mem.at[half, rows, :]),
                    (q_rows.at[pl.ds((half * n + m) * deep, deep)], q_mem.at[half, rows, :]),
                ]
            ):
                sem = weight_sem.at[4 * m + 2 * half + k]
                copies.append(pltpu.make_async_copy(source, target, sem))

    def loads(m):
        return [
            pltpu.make_async_copy(blocks[m * 2 + side], block_mem.at[side, m], block_sem.at[m, side])
            for side in range(2)
        ]

    ahead = 1
    for copy in copies:
        copy.start()
    for m in range(ahead):
        for copy in loads(m):
            copy.start()
    for copy in copies:
        copy.wait()

    @pl.loop(0, n)
    def _(t):
        for m in range(ahead, n):

            @pl.when(t == m - ahead)
            def _():
                for copy in loads(m):
                    copy.start()

        for side in range(2):
            pltpu.make_async_copy(blocks[side], block_mem.at[side, t], block_sem.at[t, side]).wait()
        kv, q = [
            jnp.dot(block_mem[0, t], mem[col], preferred_element_type=jnp.float32)
            + jnp.dot(
                block_mem[1, t],
                mem[lax.bitwise_xor(col, 1)],
                preferred_element_type=jnp.float32,
            )
            for mem in (kv_mem, q_mem)
        ]
        at = lax.bitwise_xor(place, t)
        cosine_here, sine_here = cosine[at], sine[at]
        keys = normed_rotated(kv[:, :HD], key_gain[...], cosine_here, sine_here)
        keys = keys.astype(jnp.bfloat16)
        values = kv[:, HD : 2 * HD].astype(jnp.bfloat16)
        kv_out[at, :, :HD] = keys
        kv_out[at, :, HD:] = values
        for h in range(heads):
            query = normed_rotated(
                q[:, h * HD : (h + 1) * HD], query_gain[...], cosine_here, sine_here
            )
            q_out[at, pl.ds(h * tokens, tokens), :] = query.astype(jnp.bfloat16)

        @pl.when(at >= n - reach)
        def _():
            tail_out[at - (n - reach), :, :HD] = keys
            tail_out[at - (n - reach), :, HD:] = values


def attend_kernel(low, count, reach, heads, meta, q_doc, k_doc, queries, kv_own, *refs):
    kv_back = refs[0] if low < reach else None
    keep_out, send_out = refs[-2:]
    col = meta[2]
    tokens = kv_own.shape[1]
    part = tokens // 2
    scale = 1.0 / math.sqrt(QUERY_SCALAR)
    row_at = lax.broadcasted_iota(jnp.int32, (tokens, tokens), 0)
    col_at = lax.broadcasted_iota(jnp.int32, (tokens, tokens), 1)

    for g in range(count):
        doc = q_doc[low + g]
        query = queries[low + g]
        totals = jnp.zeros((heads * tokens, 1), jnp.float32)
        mixed = jnp.zeros((heads * tokens, HD), jnp.float32)
        for step in range(reach + 1):
            at = low + g + step
            pair = kv_back[at] if at < reach else kv_own[at - reach]
            visible = doc == k_doc[at]
            if step == 0:
                visible = visible & (row_at < col_at)
            if step == reach:
                visible = visible & (row_at >= col_at)
            scores = lax.dot_general(
                query, pair[:, :HD], (((1,), (1,)), ((), ())), preferred_element_type=jnp.float32
            )
            weights_here = jnp.where(
                visible[None], jnp.exp(scores * scale).reshape(heads, tokens, tokens), 0.0
            ).reshape(heads * tokens, tokens)
            totals = totals + jnp.sum(weights_here, axis=-1, keepdims=True)
            mixed = mixed + jnp.dot(
                weights_here.astype(jnp.bfloat16), pair[:, HD:], preferred_element_type=jnp.float32
            )
        done = (mixed / totals).astype(jnp.bfloat16)
        for h in range(heads):
            top = done[h * tokens : h * tokens + part]
            bottom = done[h * tokens + part : (h + 1) * tokens]
            keep_out[g, :, h * HD : (h + 1) * HD] = jnp.where(col == 0, top, bottom)
            send_out[g, :, h * HD : (h + 1) * HD] = jnp.where(col == 0, bottom, top)


def output_kernel(n, spans, far, meta, *refs):
    count = n * len(spans)
    contexts, weights = refs[:count], refs[count:-5]
    if far:
        weights, before = weights[:-1], weights[-1]
    out, context_mem, weight_mem, context_sem, weight_sem = refs[-5:]
    place, half, col = meta[0], meta[1], meta[2]
    deep = weights[0].shape[1]
    wide = contexts[0].shape[3]
    part = contexts[0].shape[2]
    copies = []
    for k, source in enumerate(weights):
        first = sum(weights[j].shape[0] for j in range(k % 2, k, 2))
        side = pl.multiple_of(lax.bitwise_xor(col, k % 2) * deep, 128)
        copies.append(
            pltpu.make_async_copy(
                source,
                weight_mem.at[pl.ds(first, source.shape[0]), pl.ds(side, deep)],
                weight_sem.at[k],
            )
        )
    loads = []
    for s, (low, size) in enumerate(spans):
        loads.append([])
        for m in range(n):
            for side in range(2):
                first = lax.bitwise_xor(col, side) * deep + lax.bitwise_xor(place, m) * wide
                loads[s].append(
                    pltpu.make_async_copy(
                        contexts[s * n + m].at[side],
                        context_mem.at[
                            pl.ds(low, size), :, pl.ds(pl.multiple_of(first, 128), wide)
                        ],
                        context_sem.at[(s * n + m) * 2 + side],
                    )
                )
    for copy in copies + loads[0]:
        copy.start()
    for copy in copies:
        copy.wait()
    for s, (low, size) in enumerate(spans):
        for copy in loads[s]:
            copy.wait()
        if s + 1 < len(spans):
            for copy in loads[s + 1]:
                copy.start()
        left = context_mem[low : low + size].reshape(size * part, 2 * deep)
        result = lax.dot_general(
            left, weight_mem[...], (((1,), (1,)), ((), ())), preferred_element_type=jnp.float32
        ).astype(jnp.bfloat16)
        for k in range(size):
            slab = result[k * part : (k + 1) * part]
            if far:
                out[2 * (low + k) + lax.bitwise_xor(half, 1)] = slab
                out[2 * (low + k) + half] = before[low + k]
            else:
                out[low + k] = slab


def close_kernel(n, activations, arrived, out):
    part = arrived.shape[1]
    for col in range(2):
        rows = pl.ds(col * part, part)
        whole = jnp.concatenate([arrived[2 * p + col] for p in range(n)], axis=1)
        out[rows, :] = (
            activations[rows, :].astype(jnp.float32) + whole.astype(jnp.float32)
        ).astype(jnp.bfloat16)


def split_body(
    activations,
    positions,
    query_weight,
    key_weight,
    value_weight,
    output_weight,
    input_gain,
    query_gain,
    key_gain,
):
    tokens, features = activations.shape
    n = key_weight.shape[1] // HD
    heads = query_weight.shape[1] // key_weight.shape[1]
    reach = WINDOW // tokens
    part = tokens // 2
    half, place, col = lax.axis_index("half"), lax.axis_index("place"), lax.axis_index("cols")
    meta = jnp.stack([place, half, col]).astype(jnp.int32)
    bf16, f32 = jnp.bfloat16, jnp.float32
    shaped = jax.ShapeDtypeStruct

    deep = query_weight.shape[0]
    kv_cut, *cut = run(
        functools.partial(cut_kernel, n),
        [shaped((deep, n * 2 * HD), bf16)] + [shaped((deep, heads * HD), bf16)] * n,
        [SMEM, VMEM, VMEM, VMEM],
        [VMEM] * (n + 1),
        [],
        0,
        4 * query_weight.size * 2,
    )(meta, query_weight, key_weight, value_weight)
    kv_rows = lax.all_gather(kv_cut, "half", axis=0, tiled=True)

    wide = activations.astype(f32)
    squares = jnp.sum(wide * wide, axis=-1).reshape(2, part)
    squares = (squares + swapped(squares, 0, 1)).reshape(tokens, 1)
    inverse = lax.rsqrt(squares / (2 * features) + 1e-06)
    gain = lax.dynamic_slice_in_dim(input_gain, col * features, features, 0)
    normed = (wide * inverse * gain).astype(bf16)

    z, y, c = n // 2, n // 4, 1
    blocks = {(0, 0): normed}
    blocks[y, 0] = swapped(normed, y, 0)
    blocks[0, 1] = swapped(normed, 0, 1)
    blocks[z, 0] = swapped(normed, z, 0)
    blocks[y, 1] = swapped(blocks[y, 0], 0, 1)
    blocks[z, 1] = swapped(blocks[z, 0], 0, 1)
    blocks[z + y, 0] = swapped(blocks[z, 0], y, 0)
    blocks[z + y, 1] = swapped(blocks[z + y, 0], 0, 1)
    for m, side in list(blocks):
        blocks[m + c, side] = swapped(blocks[m, side], c, 0)
    block_list = [blocks[m, side] for m in range(n) for side in range(2)]

    in_half = lax.dynamic_slice_in_dim(positions, half * n * tokens, n * tokens, 0)
    frequency = 10000.0 ** (-(jnp.arange(HD // 2, dtype=f32) * 2.0 / HD))
    angles = in_half.astype(f32)[:, None] * frequency[None, :]
    cosine, sine = jnp.cos(angles), jnp.sin(angles)
    cosine = jnp.concatenate([cosine, cosine], -1).reshape(n, tokens, HD)
    sine = jnp.concatenate([-sine, sine], -1).reshape(n, tokens, HD)
    index = jnp.arange(positions.shape[0], dtype=jnp.int32)
    starts = jnp.concatenate(
        [jnp.full((reach * tokens,), -(2**30), jnp.int32), index - positions], 0
    )
    docs = lax.dynamic_slice_in_dim(starts, half * n * tokens, (n + reach) * tokens, 0)
    k_doc = docs.reshape(n + reach, 1, tokens)
    q_doc = docs[reach * tokens :].reshape(n, tokens, 1)

    near = [cut[0]] + [swapped(cut[m], m, 0) for m in range(1, n)]
    q_own = run(
        join_kernel,
        shaped((n * deep, heads * HD), bf16),
        [VMEM] * n,
        VMEM,
        [],
        0,
        4 * n * deep * heads * HD,
    )(*near)
    q_rows = lax.all_gather(q_own, "half", axis=0, tiled=True)
    kv_rows, cosine, sine, q_doc = lax.optimization_barrier((kv_rows, cosine, sine, q_doc))
    kv_parts = []
    for m in range(n):
        first = lax.bitwise_xor(place, m) * 2 * HD
        piece = lax.dynamic_slice_in_dim(kv_rows, first, 2 * HD, 1)
        kv_parts.append(piece if m == 0 else swapped(piece, m, 0))

    flops = 2 * n * tokens * 2 * features * (2 + heads) * HD
    kv_own, kv_tail, queries = run(
        functools.partial(project_kernel, n, reach, heads),
        [
            shaped((n, tokens, 2 * HD), bf16),
            shaped((reach, tokens, 2 * HD), bf16),
            shaped((n, heads * tokens, HD), bf16),
        ],
        [SMEM, VMEM, VMEM, VMEM, VMEM] + [ANY] * (3 * n + 1),
        [VMEM, VMEM, VMEM],
        [
            pltpu.VMEM((2, n, tokens, features), bf16),
            pltpu.VMEM((2, features, 2 * HD), bf16),
            pltpu.VMEM((2, features, heads * HD), bf16),
            pltpu.SemaphoreType.DMA((n, 2)),
            pltpu.SemaphoreType.DMA((4 * n,)),
        ],
        flops,
        2 * n * tokens * features * 2,
    )(
        meta,
        cosine,
        sine,
        key_gain.reshape(1, HD),
        query_gain.reshape(1, HD),
        *block_list,
        *kv_parts,
        q_rows,
    )
    kv_back = lax.ppermute(kv_tail, "half", [(0, 1)])

    own_weight, _ = lax.optimization_barrier((output_weight.T, q_own))
    ahead = own_weight.shape[0] * 4 // 7 // 16 * 16
    near_weights = [own_weight, swapped(own_weight, 0, 1)]
    far_weights = []
    for rows in [own_weight[:ahead], own_weight[ahead:]]:
        both = lax.all_gather(rows, "half", axis=0)
        piece = lax.dynamic_index_in_dim(both, 1 - half, 0, keepdims=False)
        far_weights += [piece, swapped(piece, 0, 1)]

    contexts = []
    spans = [(reach, n - reach), (0, reach)]
    for low, count in spans:
        backs = [kv_back] if low < reach else []
        shape = shaped((count, part, heads * HD), bf16)
        keep, send = run(
            functools.partial(attend_kernel, low, count, reach, heads),
            [shape, shape],
            [SMEM] + [VMEM] * (4 + len(backs)),
            [VMEM, VMEM],
            [],
            8 * count * heads * tokens * (reach + 1) * tokens * HD,
            4 * n * tokens * 2 * HD,
        )(meta, q_doc, k_doc, queries, kv_own, *backs)
        there = swapped(send, 0, 1)
        pair = run(
            pair_kernel,
            shaped((2, count, part, heads * HD), bf16),
            [VMEM, VMEM],
            VMEM,
            [],
            0,
            8 * count * part * heads * HD,
        )(keep, there)
        pairs = {0: pair}
        pairs[z] = swapped(pair, z, 0)
        pairs[y] = swapped(pair, y, 0)
        pairs[z + y] = swapped(pairs[z], y, 0)
        for m in list(pairs):
            pairs[m + c] = swapped(pairs[m], c, 0)
        contexts += [pairs[m] for m in range(n)]

    out_cols = output_weight.shape[1]
    deep_out = output_weight.shape[0]
    result = []
    for weights, shape in ((near_weights, (n,)), (far_weights, (2 * n,))):
        result = [
            run(
                functools.partial(output_kernel, n, spans, len(result)),
                shaped((*shape, part, out_cols), bf16),
                [SMEM] + [ANY] * (2 * n + len(weights)) + [VMEM] * len(result),
                VMEM,
                [
                    pltpu.VMEM((n, part, 2 * deep_out), bf16),
                    pltpu.VMEM((out_cols, 2 * deep_out), bf16),
                    pltpu.SemaphoreType.DMA((4 * n,)),
                    pltpu.SemaphoreType.DMA((len(weights),)),
                ],
                2 * n * part * 2 * deep_out * out_cols,
                8 * deep_out * out_cols,
            )(meta, *contexts, *weights, *result)
        ]

    arrived = lax.all_to_all(result[0], ("place", "cols"), 0, 0, tiled=True)
    return run(
        functools.partial(close_kernel, n),
        shaped((tokens, features), bf16),
        [VMEM, VMEM],
        VMEM,
        [],
        0,
        6 * tokens * features,
    )(activations, arrived)


def solution(mesh):
    sizes = mesh.shape
    if sizes["cols"] == 2 and sizes["sub"] == 1 and sizes["rows"] == 16:
        shape = (sizes["groups"], 2, sizes["rows"] // 2, sizes["cols"], sizes["sub"])
        names = ("groups", "half", "place", "cols", "sub")
        fine, rows = Mesh(mesh.devices.reshape(shape), names), ("half", "place")
    else:
        fine, rows = mesh, ("rows",)
    columns = ("cols", "sub")
    placed = (
        P(("groups", *rows), columns),
        P("groups"),
        P(rows, columns),
        P(rows, columns),
        P(rows, columns),
        P(columns, rows),
        P(),
        P(),
        P(),
    )

    def mapped(body):
        return jax.shard_map(
            body, mesh=fine, in_specs=placed, out_specs=placed[0], check_vma=False
        )

    if fine is mesh:
        return mapped(gathered_body)

    return mapped(split_body)
```

```python
import functools
import math

import jax
import jax.numpy as jnp
from jax import lax
from jax.experimental import pallas as pl
from jax.experimental.pallas import tpu as pltpu
from jax.sharding import Mesh
from jax.sharding import PartitionSpec as P


HD = 128
WINDOW = 1024
QUERY_SCALAR = 168
VMEM_BYTES = 67_000_000
ANY = pl.BlockSpec(memory_space=pl.ANY)
VMEM = pl.BlockSpec(memory_space=pltpu.VMEM)
SMEM = pl.BlockSpec(memory_space=pltpu.SMEM)


def passed_along(value, axis, by):
    peers = lax.axis_size(axis)
    pairs = [(i, i + by) for i in range(peers) if 0 <= i + by < peers]
    return lax.ppermute(value, axis, pairs)


def head_norm(tensor, gain_vector):
    return (
        tensor * lax.rsqrt(jnp.mean(tensor * tensor, axis=-1, keepdims=True) + 1e-06) * gain_vector
    )


def rotate(tensor, token_positions):
    half_width = tensor.shape[-1] // 2
    frequency = 10000.0 ** (-(jnp.arange(half_width, dtype=jnp.float32) * 2.0 / tensor.shape[-1]))
    angles = token_positions.astype(jnp.float32)[:, None] * frequency[None, :]
    cosine = jnp.cos(angles)[:, None, :]
    sine_part = jnp.sin(angles)[:, None, :]
    first_half = tensor[..., :half_width]
    second_half = tensor[..., half_width:]
    return jnp.concatenate(
        [
            first_half * cosine - second_half * sine_part,
            second_half * cosine + first_half * sine_part,
        ],
        axis=-1,
    )


def attend(queries, key_rows, value_rows, query_index, key_index, query_pos, key_pos):
    row_count = queries.shape[0]
    key_count = key_rows.shape[0]
    kv_heads = key_rows.shape[1] // HD
    group_size = queries.shape[1] // key_rows.shape[1]
    query_four = queries.reshape(row_count, kv_heads, group_size, HD)
    key_three = key_rows.reshape(key_count, kv_heads, HD)
    value_three = value_rows.reshape(key_count, kv_heads, HD)
    score_scale = 1.0 / math.sqrt(QUERY_SCALAR)
    scores = (
        jnp.einsum("qgrd,kgd->grqk", query_four, key_three, preferred_element_type=jnp.float32)
        * score_scale
    )
    distance = query_index[:, None] - key_index[None, :]
    visible = (
        (key_index[None, :] >= 0)
        & (distance >= 0)
        & (distance < WINDOW)
        & (query_pos[:, None] - key_pos[None, :] == distance)
    )
    weights = jnp.where(visible[None, None], jnp.exp(scores), 0.0)
    totals = jnp.sum(weights, axis=-1)
    rounded = weights.astype(jnp.bfloat16)
    mixed_heads = jnp.einsum(
        "grqk,kgd->qgrd", rounded, value_three, preferred_element_type=jnp.float32
    )
    mixed_heads = mixed_heads / jnp.transpose(totals, (2, 0, 1))[..., None]
    return mixed_heads.astype(jnp.bfloat16).reshape(row_count, kv_heads * group_size * HD)


def reach_back(key_rows, value_rows, reach_rows):
    pieces = []
    carried = (key_rows, value_rows)
    for _ in range(reach_rows):
        carried = passed_along((carried[0], carried[1]), "rows", 1)
        pieces.append(carried)
    ordered = pieces[::-1] + [(key_rows, value_rows)]
    all_keys = jnp.concatenate([member[0] for member in ordered], axis=0)
    all_values = jnp.concatenate([member[1] for member in ordered], axis=0)
    return (all_keys, all_values)


def gathered_body(
    activations,
    positions,
    query_weight,
    key_weight,
    value_weight,
    output_weight,
    input_gain,
    query_gain,
    key_gain,
):
    rows_here = activations.shape[0]
    row_panel = lax.all_gather(activations, ("cols", "sub"), axis=1, tiled=True)
    panel_wide = row_panel.astype(jnp.float32)
    inverse = lax.rsqrt(jnp.mean(panel_wide * panel_wide, axis=-1, keepdims=True) + 1e-06)
    normed = (panel_wide * inverse * input_gain).astype(jnp.bfloat16)
    row_index = lax.axis_index("rows")
    own_positions = lax.dynamic_slice_in_dim(positions, row_index * rows_here, rows_here, 0)
    reach_rows = min(-(-WINDOW // rows_here), lax.axis_size("rows") - 1)

    def add_rows(weight_piece):
        return jnp.dot(normed, weight_piece, preferred_element_type=jnp.float32)

    query_raw = add_rows(lax.all_gather(query_weight, "rows", axis=0, tiled=True))
    key_raw = add_rows(lax.all_gather(key_weight, "rows", axis=0, tiled=True))
    value_raw = add_rows(lax.all_gather(value_weight, "rows", axis=0, tiled=True))
    key_rows = rotate(head_norm(key_raw.reshape(rows_here, -1, HD), key_gain), own_positions)
    key_rows, value_rows = (
        key_rows.astype(jnp.bfloat16).reshape(rows_here, -1),
        value_raw.astype(jnp.bfloat16),
    )
    all_keys, all_values = reach_back(key_rows, value_rows, reach_rows)
    queries = rotate(head_norm(query_raw.reshape(rows_here, -1, HD), query_gain), own_positions)
    queries = queries.astype(jnp.bfloat16).reshape(rows_here, -1)
    key_count = all_keys.shape[0]
    query_index = row_index * rows_here + jnp.arange(rows_here, dtype=jnp.int32)
    key_index = (row_index - reach_rows) * rows_here + jnp.arange(key_count, dtype=jnp.int32)
    padded = jnp.concatenate([jnp.zeros((reach_rows * rows_here,), jnp.int32), positions], axis=0)
    key_positions = lax.dynamic_slice_in_dim(padded, row_index * rows_here, key_count, 0)
    context = attend(
        queries, all_keys, all_values, query_index, key_index, own_positions, key_positions
    )
    partial_terms = jnp.dot(
        context,
        lax.all_gather(output_weight, "rows", axis=1, tiled=True),
        preferred_element_type=jnp.float32,
    )
    summed = lax.psum_scatter(
        partial_terms.astype(jnp.bfloat16), ("cols", "sub"), scatter_dimension=1, tiled=True
    ).astype(jnp.float32)
    return (activations.astype(jnp.float32) + summed).astype(jnp.bfloat16)


def swapped(value, place=0, col=0):
    places, cols = lax.axis_size("place"), lax.axis_size("cols")
    pairs = [
        (r * cols + c, (r ^ place) * cols + (c ^ col)) for r in range(places) for c in range(cols)
    ]
    return lax.ppermute(value, ("place", "cols"), pairs)


def run(kernel, out_shape, in_specs, out_specs, scratch, flops, bytes_moved):
    return pl.pallas_call(
        kernel,
        out_shape=out_shape,
        in_specs=in_specs,
        out_specs=out_specs,
        scratch_shapes=scratch,
        compiler_params=pltpu.CompilerParams(vmem_limit_bytes=VMEM_BYTES),
        cost_estimate=pl.CostEstimate(
            flops=int(flops), bytes_accessed=int(bytes_moved), transcendentals=0
        ),
    )


def cut_kernel(n, meta, wq, wk, wv, kv_out, *q_outs):
    place = meta[0]
    wide_q = wq.shape[1] // n
    for p in range(n):
        kv_out[:, p * 2 * HD : p * 2 * HD + HD] = wk[:, p * HD : (p + 1) * HD]
        kv_out[:, p * 2 * HD + HD : (p + 1) * 2 * HD] = wv[:, p * HD : (p + 1) * HD]
    for m in range(n):
        at = lax.bitwise_xor(place, m)
        q_outs[m][...] = wq[:, pl.ds(pl.multiple_of(at * wide_q, 128), wide_q)]


def join_kernel(*refs):
    out = refs[-1]
    deep = refs[0].shape[0]
    for m, piece in enumerate(refs[:-1]):
        out[m * deep : (m + 1) * deep] = piece[...]


def pair_kernel(first, second, out):
    out[0] = first[...]
    out[1] = second[...]


def normed_rotated(raw, gain, cosine, sine):
    scaled = raw * lax.rsqrt(jnp.mean(raw * raw, axis=-1, keepdims=True) + 1e-06) * gain
    return scaled * cosine + pltpu.roll(scaled, HD // 2, 1) * sine


def project_kernel(n, reach, heads, meta, cosine, sine, key_gain, query_gain, *refs):
    blocks, kv_parts = refs[: 2 * n], refs[2 * n : 3 * n]
    q_rows = refs[3 * n]
    kv_out, tail_out, q_out = refs[3 * n + 1 : 3 * n + 4]
    block_mem, kv_mem, q_mem, block_sem, weight_sem = refs[3 * n + 4 :]
    place, col = meta[0], meta[2]
    _, _, tokens, _ = block_mem.shape
    deep = kv_parts[0].shape[0] // 2
    copies = []
    for m in range(n):
        rows = pl.ds(pl.multiple_of(lax.bitwise_xor(place, m) * deep, 16), deep)
        for half in range(2):
            for k, (source, target) in enumerate(
                [
                    (kv_parts[m].at[pl.ds(half * deep, deep)], kv_mem.at[half, rows, :]),
                    (q_rows.at[pl.ds((half * n + m) * deep, deep)], q_mem.at[half, rows, :]),
                ]
            ):
                sem = weight_sem.at[4 * m + 2 * half + k]
                copies.append(pltpu.make_async_copy(source, target, sem))

    def loads(m):
        return [
            pltpu.make_async_copy(blocks[m * 2 + side], block_mem.at[side, m], block_sem.at[m, side])
            for side in range(2)
        ]

    ahead = 1
    for copy in copies:
        copy.start()
    for m in range(ahead):
        for copy in loads(m):
            copy.start()
    for copy in copies:
        copy.wait()

    @pl.loop(0, n)
    def _(t):
        for m in range(ahead, n):

            @pl.when(t == m - ahead)
            def _():
                for copy in loads(m):
                    copy.start()

        for side in range(2):
            pltpu.make_async_copy(blocks[side], block_mem.at[side, t], block_sem.at[t, side]).wait()
        kv, q = [
            jnp.dot(block_mem[0, t], mem[col], preferred_element_type=jnp.float32)
            + jnp.dot(
                block_mem[1, t],
                mem[lax.bitwise_xor(col, 1)],
                preferred_element_type=jnp.float32,
            )
            for mem in (kv_mem, q_mem)
        ]
        at = lax.bitwise_xor(place, t)
        cosine_here, sine_here = cosine[at], sine[at]
        keys = normed_rotated(kv[:, :HD], key_gain[...], cosine_here, sine_here)
        keys = keys.astype(jnp.bfloat16)
        values = kv[:, HD : 2 * HD].astype(jnp.bfloat16)
        kv_out[at, :, :HD] = keys
        kv_out[at, :, HD:] = values
        for h in range(heads):
            query = normed_rotated(
                q[:, h * HD : (h + 1) * HD], query_gain[...], cosine_here, sine_here
            )
            q_out[at, pl.ds(h * tokens, tokens), :] = query.astype(jnp.bfloat16)

        @pl.when(at >= n - reach)
        def _():
            tail_out[at - (n - reach), :, :HD] = keys
            tail_out[at - (n - reach), :, HD:] = values


def attend_kernel(low, count, reach, heads, meta, q_doc, k_doc, queries, kv_own, *refs):
    kv_back = refs[0] if low < reach else None
    keep_out, send_out = refs[-2:]
    col = meta[2]
    tokens = kv_own.shape[1]
    part = tokens // 2
    scale = 1.0 / math.sqrt(QUERY_SCALAR)
    row_at = lax.broadcasted_iota(jnp.int32, (tokens, tokens), 0)
    col_at = lax.broadcasted_iota(jnp.int32, (tokens, tokens), 1)

    for g in range(count):
        doc = q_doc[low + g]
        query = queries[low + g]
        totals = jnp.zeros((heads * tokens, 1), jnp.float32)
        mixed = jnp.zeros((heads * tokens, HD), jnp.float32)
        for step in range(reach + 1):
            at = low + g + step
            pair = kv_back[at] if at < reach else kv_own[at - reach]
            visible = doc == k_doc[at]
            if step == 0:
                visible = visible & (row_at < col_at)
            if step == reach:
                visible = visible & (row_at >= col_at)
            scores = lax.dot_general(
                query, pair[:, :HD], (((1,), (1,)), ((), ())), preferred_element_type=jnp.float32
            )
            weights_here = jnp.where(
                visible[None], jnp.exp(scores * scale).reshape(heads, tokens, tokens), 0.0
            ).reshape(heads * tokens, tokens)
            totals = totals + jnp.sum(weights_here, axis=-1, keepdims=True)
            mixed = mixed + jnp.dot(
                weights_here.astype(jnp.bfloat16), pair[:, HD:], preferred_element_type=jnp.float32
            )
        done = (mixed / totals).astype(jnp.bfloat16)
        for h in range(heads):
            top = done[h * tokens : h * tokens + part]
            bottom = done[h * tokens + part : (h + 1) * tokens]
            keep_out[g, :, h * HD : (h + 1) * HD] = jnp.where(col == 0, top, bottom)
            send_out[g, :, h * HD : (h + 1) * HD] = jnp.where(col == 0, bottom, top)


def output_kernel(n, size, meta, *refs):
    contexts, weights, after = refs[:n], refs[n : n + 6], refs[n + 6 : -5]
    out, context_mem, weight_mem, context_sem, weight_sem = refs[-5:]
    place, half, col = meta[0], meta[1], meta[2]
    rows_all, deep = weights[0].shape
    wide = contexts[0].shape[3]
    part = contexts[0].shape[2]
    copies = []
    for k, source in enumerate(weights):
        first = (half if k < 2 else lax.bitwise_xor(half, 1)) * rows_all
        first = first + (0 if k < 4 else weights[2].shape[0])
        side = pl.multiple_of(lax.bitwise_xor(col, k % 2) * deep, 128)
        copies.append(
            pltpu.make_async_copy(
                source,
                weight_mem.at[
                    pl.ds(pl.multiple_of(first, 16), source.shape[0]), pl.ds(side, deep)
                ],
                weight_sem.at[k],
            )
        )
    for m in range(n):
        for side in range(2):
            first = lax.bitwise_xor(col, side) * deep + lax.bitwise_xor(place, m) * wide
            copies.append(
                pltpu.make_async_copy(
                    contexts[m].at[side],
                    context_mem.at[:, :, pl.ds(pl.multiple_of(first, 128), wide)],
                    context_sem.at[m * 2 + side],
                )
            )
    for copy in copies:
        copy.start()
    for copy in copies:
        copy.wait()
    result = lax.dot_general(
        weight_mem[...],
        context_mem[...].reshape(size * part, 2 * deep),
        (((1,), (1,)), ((), ())),
        preferred_element_type=jnp.float32,
    ).astype(jnp.bfloat16)
    for k in range(size):
        for block in range(2):
            out[2 * k + block] = result[
                block * rows_all : (block + 1) * rows_all, k * part : (k + 1) * part
            ]
    if after:
        out[2 * size :] = after[0][...]


def close_kernel(n, activations, arrived, out):
    _, _, part = arrived.shape
    for col in range(2):
        rows = pl.ds(col * part, part)
        whole = jnp.concatenate([arrived[2 * p + col] for p in range(n)], axis=0)
        out[rows, :] = (
            activations[rows, :].astype(jnp.float32) + whole.astype(jnp.float32).T
        ).astype(jnp.bfloat16)


def split_body(
    activations,
    positions,
    query_weight,
    key_weight,
    value_weight,
    output_weight,
    input_gain,
    query_gain,
    key_gain,
):
    tokens, features = activations.shape
    n = key_weight.shape[1] // HD
    heads = query_weight.shape[1] // key_weight.shape[1]
    reach = WINDOW // tokens
    part = tokens // 2
    half, place, col = lax.axis_index("half"), lax.axis_index("place"), lax.axis_index("cols")
    meta = jnp.stack([place, half, col]).astype(jnp.int32)
    bf16, f32 = jnp.bfloat16, jnp.float32
    shaped = jax.ShapeDtypeStruct

    deep = query_weight.shape[0]
    kv_cut, *cut = run(
        functools.partial(cut_kernel, n),
        [shaped((deep, n * 2 * HD), bf16)] + [shaped((deep, heads * HD), bf16)] * n,
        [SMEM, VMEM, VMEM, VMEM],
        [VMEM] * (n + 1),
        [],
        0,
        4 * query_weight.size * 2,
    )(meta, query_weight, key_weight, value_weight)
    kv_rows = lax.all_gather(kv_cut, "half", axis=0, tiled=True)

    wide = activations.astype(f32)
    squares = jnp.sum(wide * wide, axis=-1).reshape(2, part)
    squares = (squares + swapped(squares, 0, 1)).reshape(tokens, 1)
    inverse = lax.rsqrt(squares / (2 * features) + 1e-06)
    gain = lax.dynamic_slice_in_dim(input_gain, col * features, features, 0)
    normed = (wide * inverse * gain).astype(bf16)

    z, y, c = n // 2, n // 4, 1
    blocks = {(0, 0): normed}
    blocks[y, 0] = swapped(normed, y, 0)
    blocks[0, 1] = swapped(normed, 0, 1)
    blocks[z, 0] = swapped(normed, z, 0)
    blocks[y, 1] = swapped(blocks[y, 0], 0, 1)
    blocks[z, 1] = swapped(blocks[z, 0], 0, 1)
    blocks[z + y, 0] = swapped(blocks[z, 0], y, 0)
    blocks[z + y, 1] = swapped(blocks[z + y, 0], 0, 1)
    for m, side in list(blocks):
        blocks[m + c, side] = swapped(blocks[m, side], c, 0)
    block_list = [blocks[m, side] for m in range(n) for side in range(2)]

    in_half = lax.dynamic_slice_in_dim(positions, half * n * tokens, n * tokens, 0)
    frequency = 10000.0 ** (-(jnp.arange(HD // 2, dtype=f32) * 2.0 / HD))
    angles = in_half.astype(f32)[:, None] * frequency[None, :]
    cosine, sine = jnp.cos(angles), jnp.sin(angles)
    cosine = jnp.concatenate([cosine, cosine], -1).reshape(n, tokens, HD)
    sine = jnp.concatenate([-sine, sine], -1).reshape(n, tokens, HD)
    index = jnp.arange(positions.shape[0], dtype=jnp.int32)
    starts = jnp.concatenate(
        [jnp.full((reach * tokens,), -(2**30), jnp.int32), index - positions], 0
    )
    docs = lax.dynamic_slice_in_dim(starts, half * n * tokens, (n + reach) * tokens, 0)
    k_doc = docs.reshape(n + reach, 1, tokens)
    q_doc = docs[reach * tokens :].reshape(n, tokens, 1)

    near = [cut[0]] + [swapped(cut[m], m, 0) for m in range(1, n)]
    q_own = run(
        join_kernel,
        shaped((n * deep, heads * HD), bf16),
        [VMEM] * n,
        VMEM,
        [],
        0,
        4 * n * deep * heads * HD,
    )(*near)
    q_rows = lax.all_gather(q_own, "half", axis=0, tiled=True)
    kv_rows, cosine, sine, q_doc = lax.optimization_barrier((kv_rows, cosine, sine, q_doc))
    kv_parts = []
    for m in range(n):
        first = lax.bitwise_xor(place, m) * 2 * HD
        piece = lax.dynamic_slice_in_dim(kv_rows, first, 2 * HD, 1)
        kv_parts.append(piece if m == 0 else swapped(piece, m, 0))

    flops = 2 * n * tokens * 2 * features * (2 + heads) * HD
    kv_own, kv_tail, queries = run(
        functools.partial(project_kernel, n, reach, heads),
        [
            shaped((n, tokens, 2 * HD), bf16),
            shaped((reach, tokens, 2 * HD), bf16),
            shaped((n, heads * tokens, HD), bf16),
        ],
        [SMEM, VMEM, VMEM, VMEM, VMEM] + [ANY] * (3 * n + 1),
        [VMEM, VMEM, VMEM],
        [
            pltpu.VMEM((2, n, tokens, features), bf16),
            pltpu.VMEM((2, features, 2 * HD), bf16),
            pltpu.VMEM((2, features, heads * HD), bf16),
            pltpu.SemaphoreType.DMA((n, 2)),
            pltpu.SemaphoreType.DMA((4 * n,)),
        ],
        flops,
        2 * n * tokens * features * 2,
    )(
        meta,
        cosine,
        sine,
        key_gain.reshape(1, HD),
        query_gain.reshape(1, HD),
        *block_list,
        *kv_parts,
        q_rows,
    )
    kv_back = lax.ppermute(kv_tail, "half", [(0, 1)])

    own_weight, _ = lax.optimization_barrier((output_weight.T, q_own))
    ahead = own_weight.shape[0] * 4 // 7 // 16 * 16
    out_weights = [own_weight, swapped(own_weight, 0, 1)]
    for rows in [own_weight[:ahead], own_weight[ahead:]]:
        both = lax.all_gather(rows, "half", axis=0)
        piece = lax.dynamic_index_in_dim(both, 1 - half, 0, keepdims=False)
        out_weights += [piece, swapped(piece, 0, 1)]

    contexts = []
    spans = [(reach, n - reach), (0, reach)]
    for low, count in spans:
        backs = [kv_back] if low < reach else []
        shape = shaped((count, part, heads * HD), bf16)
        keep, send = run(
            functools.partial(attend_kernel, low, count, reach, heads),
            [shape, shape],
            [SMEM] + [VMEM] * (4 + len(backs)),
            [VMEM, VMEM],
            [],
            8 * count * heads * tokens * (reach + 1) * tokens * HD,
            4 * n * tokens * 2 * HD,
        )(meta, q_doc, k_doc, queries, kv_own, *backs)
        there = swapped(send, 0, 1)
        pair = run(
            pair_kernel,
            shaped((2, count, part, heads * HD), bf16),
            [VMEM, VMEM],
            VMEM,
            [],
            0,
            8 * count * part * heads * HD,
        )(keep, there)
        pairs = {0: pair}
        pairs[z] = swapped(pair, z, 0)
        pairs[y] = swapped(pair, y, 0)
        pairs[z + y] = swapped(pairs[z], y, 0)
        for m in list(pairs):
            pairs[m + c] = swapped(pairs[m], c, 0)
        contexts.append([pairs[m] for m in range(n)])

    out_cols = output_weight.shape[1]
    deep_out = output_weight.shape[0]
    result = []
    for s, (low, count) in enumerate(spans):
        blocks_out = 2 * count + sum(r.shape[0] for r in result)
        result = [
            run(
                functools.partial(output_kernel, n, count),
                shaped((blocks_out, out_cols, part), bf16),
                [SMEM] + [ANY] * (n + 6) + [VMEM] * len(result),
                VMEM,
                [
                    pltpu.VMEM((count, part, 2 * deep_out), bf16),
                    pltpu.VMEM((2 * out_cols, 2 * deep_out), bf16),
                    pltpu.SemaphoreType.DMA((2 * n,)),
                    pltpu.SemaphoreType.DMA((6,)),
                ],
                8 * count * part * deep_out * out_cols,
                8 * deep_out * out_cols,
            )(meta, *contexts[s], *out_weights, *result)
        ]

    arrived = lax.all_to_all(result[0], ("place", "cols"), 0, 0, tiled=True)
    return run(
        functools.partial(close_kernel, n),
        shaped((tokens, features), bf16),
        [VMEM, VMEM],
        VMEM,
        [],
        0,
        6 * tokens * features,
    )(activations, arrived)


def solution(mesh):
    sizes = mesh.shape
    if sizes["cols"] == 2 and sizes["sub"] == 1 and sizes["rows"] == 16:
        shape = (sizes["groups"], 2, sizes["rows"] // 2, sizes["cols"], sizes["sub"])
        names = ("groups", "half", "place", "cols", "sub")
        fine, rows = Mesh(mesh.devices.reshape(shape), names), ("half", "place")
    else:
        fine, rows = mesh, ("rows",)
    columns = ("cols", "sub")
    placed = (
        P(("groups", *rows), columns),
        P("groups"),
        P(rows, columns),
        P(rows, columns),
        P(rows, columns),
        P(columns, rows),
        P(),
        P(),
        P(),
    )

    def mapped(body):
        return jax.shard_map(
            body, mesh=fine, in_specs=placed, out_specs=placed[0], check_vma=False
        )

    if fine is mesh:
        return mapped(gathered_body)

    return mapped(split_body)
```

```python
import functools
import math

import jax
import jax.numpy as jnp
from jax import lax
from jax.experimental import pallas as pl
from jax.experimental.pallas import tpu as pltpu
from jax.sharding import Mesh
from jax.sharding import PartitionSpec as P


HD = 128
WINDOW = 1024
QUERY_SCALAR = 168
VMEM_BYTES = 67_000_000
ANY = pl.BlockSpec(memory_space=pl.ANY)
VMEM = pl.BlockSpec(memory_space=pltpu.VMEM)
SMEM = pl.BlockSpec(memory_space=pltpu.SMEM)


def passed_along(value, axis, by):
    peers = lax.axis_size(axis)
    pairs = [(i, i + by) for i in range(peers) if 0 <= i + by < peers]
    return lax.ppermute(value, axis, pairs)


def head_norm(tensor, gain_vector):
    return (
        tensor * lax.rsqrt(jnp.mean(tensor * tensor, axis=-1, keepdims=True) + 1e-06) * gain_vector
    )


def rotate(tensor, token_positions):
    half_width = tensor.shape[-1] // 2
    frequency = 10000.0 ** (-(jnp.arange(half_width, dtype=jnp.float32) * 2.0 / tensor.shape[-1]))
    angles = token_positions.astype(jnp.float32)[:, None] * frequency[None, :]
    cosine = jnp.cos(angles)[:, None, :]
    sine_part = jnp.sin(angles)[:, None, :]
    first_half = tensor[..., :half_width]
    second_half = tensor[..., half_width:]
    return jnp.concatenate(
        [
            first_half * cosine - second_half * sine_part,
            second_half * cosine + first_half * sine_part,
        ],
        axis=-1,
    )


def attend(queries, key_rows, value_rows, query_index, key_index, query_pos, key_pos):
    row_count = queries.shape[0]
    key_count = key_rows.shape[0]
    kv_heads = key_rows.shape[1] // HD
    group_size = queries.shape[1] // key_rows.shape[1]
    query_four = queries.reshape(row_count, kv_heads, group_size, HD)
    key_three = key_rows.reshape(key_count, kv_heads, HD)
    value_three = value_rows.reshape(key_count, kv_heads, HD)
    score_scale = 1.0 / math.sqrt(QUERY_SCALAR)
    scores = (
        jnp.einsum("qgrd,kgd->grqk", query_four, key_three, preferred_element_type=jnp.float32)
        * score_scale
    )
    distance = query_index[:, None] - key_index[None, :]
    visible = (
        (key_index[None, :] >= 0)
        & (distance >= 0)
        & (distance < WINDOW)
        & (query_pos[:, None] - key_pos[None, :] == distance)
    )
    weights = jnp.where(visible[None, None], jnp.exp(scores), 0.0)
    totals = jnp.sum(weights, axis=-1)
    rounded = weights.astype(jnp.bfloat16)
    mixed_heads = jnp.einsum(
        "grqk,kgd->qgrd", rounded, value_three, preferred_element_type=jnp.float32
    )
    mixed_heads = mixed_heads / jnp.transpose(totals, (2, 0, 1))[..., None]
    return mixed_heads.astype(jnp.bfloat16).reshape(row_count, kv_heads * group_size * HD)


def reach_back(key_rows, value_rows, reach_rows):
    pieces = []
    carried = (key_rows, value_rows)
    for _ in range(reach_rows):
        carried = passed_along((carried[0], carried[1]), "rows", 1)
        pieces.append(carried)
    ordered = pieces[::-1] + [(key_rows, value_rows)]
    all_keys = jnp.concatenate([member[0] for member in ordered], axis=0)
    all_values = jnp.concatenate([member[1] for member in ordered], axis=0)
    return (all_keys, all_values)


def gathered_body(
    activations,
    positions,
    query_weight,
    key_weight,
    value_weight,
    output_weight,
    input_gain,
    query_gain,
    key_gain,
):
    rows_here = activations.shape[0]
    row_panel = lax.all_gather(activations, ("cols", "sub"), axis=1, tiled=True)
    panel_wide = row_panel.astype(jnp.float32)
    inverse = lax.rsqrt(jnp.mean(panel_wide * panel_wide, axis=-1, keepdims=True) + 1e-06)
    normed = (panel_wide * inverse * input_gain).astype(jnp.bfloat16)
    row_index = lax.axis_index("rows")
    own_positions = lax.dynamic_slice_in_dim(positions, row_index * rows_here, rows_here, 0)
    reach_rows = min(-(-WINDOW // rows_here), lax.axis_size("rows") - 1)

    def add_rows(weight_piece):
        return jnp.dot(normed, weight_piece, preferred_element_type=jnp.float32)

    query_raw = add_rows(lax.all_gather(query_weight, "rows", axis=0, tiled=True))
    key_raw = add_rows(lax.all_gather(key_weight, "rows", axis=0, tiled=True))
    value_raw = add_rows(lax.all_gather(value_weight, "rows", axis=0, tiled=True))
    key_rows = rotate(head_norm(key_raw.reshape(rows_here, -1, HD), key_gain), own_positions)
    key_rows, value_rows = (
        key_rows.astype(jnp.bfloat16).reshape(rows_here, -1),
        value_raw.astype(jnp.bfloat16),
    )
    all_keys, all_values = reach_back(key_rows, value_rows, reach_rows)
    queries = rotate(head_norm(query_raw.reshape(rows_here, -1, HD), query_gain), own_positions)
    queries = queries.astype(jnp.bfloat16).reshape(rows_here, -1)
    key_count = all_keys.shape[0]
    query_index = row_index * rows_here + jnp.arange(rows_here, dtype=jnp.int32)
    key_index = (row_index - reach_rows) * rows_here + jnp.arange(key_count, dtype=jnp.int32)
    padded = jnp.concatenate([jnp.zeros((reach_rows * rows_here,), jnp.int32), positions], axis=0)
    key_positions = lax.dynamic_slice_in_dim(padded, row_index * rows_here, key_count, 0)
    context = attend(
        queries, all_keys, all_values, query_index, key_index, own_positions, key_positions
    )
    partial_terms = jnp.dot(
        context,
        lax.all_gather(output_weight, "rows", axis=1, tiled=True),
        preferred_element_type=jnp.float32,
    )
    summed = lax.psum_scatter(
        partial_terms.astype(jnp.bfloat16), ("cols", "sub"), scatter_dimension=1, tiled=True
    ).astype(jnp.float32)
    return (activations.astype(jnp.float32) + summed).astype(jnp.bfloat16)


def swapped(value, place=0, col=0):
    places, cols = lax.axis_size("place"), lax.axis_size("cols")
    pairs = [
        (r * cols + c, (r ^ place) * cols + (c ^ col)) for r in range(places) for c in range(cols)
    ]
    return lax.ppermute(value, ("place", "cols"), pairs)


def run(kernel, out_shape, in_specs, out_specs, scratch, flops, bytes_moved):
    return pl.pallas_call(
        kernel,
        out_shape=out_shape,
        in_specs=in_specs,
        out_specs=out_specs,
        scratch_shapes=scratch,
        compiler_params=pltpu.CompilerParams(vmem_limit_bytes=VMEM_BYTES),
        cost_estimate=pl.CostEstimate(
            flops=int(flops), bytes_accessed=int(bytes_moved), transcendentals=0
        ),
    )


def cut_kernel(n, meta, wq, wk, wv, kv_out, *q_outs):
    place = meta[0]
    wide_q = wq.shape[1] // n
    for p in range(n):
        kv_out[:, p * 2 * HD : p * 2 * HD + HD] = wk[:, p * HD : (p + 1) * HD]
        kv_out[:, p * 2 * HD + HD : (p + 1) * 2 * HD] = wv[:, p * HD : (p + 1) * HD]
    for m in range(n):
        at = lax.bitwise_xor(place, m)
        q_outs[m][...] = wq[:, pl.ds(pl.multiple_of(at * wide_q, 128), wide_q)]


def join_kernel(*refs):
    out = refs[-1]
    deep = refs[0].shape[0]
    for m, piece in enumerate(refs[:-1]):
        out[m * deep : (m + 1) * deep] = piece[...]


def pair_kernel(first, second, out):
    out[0] = first[...]
    out[1] = second[...]


def normed_rotated(raw, gain, cosine, sine):
    scaled = raw * lax.rsqrt(jnp.mean(raw * raw, axis=-1, keepdims=True) + 1e-06) * gain
    return scaled * cosine + pltpu.roll(scaled, HD // 2, 1) * sine


def project_kernel(n, reach, heads, meta, cosine, sine, gain, *refs):
    blocks = refs[: 2 * n]
    weights = refs[2 * n : -6 if heads == 0 else -5]
    block_mem, weight_mem, block_sem, weight_sem = refs[-4:]
    place, col = meta[0], meta[2]
    tokens = block_mem.shape[2]
    deep = weight_mem.shape[1] // n
    copies = []
    for m in range(n):
        rows = pl.ds(pl.multiple_of(lax.bitwise_xor(place, m) * deep, 16), deep)
        for half in range(2):
            if heads == 0:
                source = weights[m].at[pl.ds(half * deep, deep)]
            else:
                source = weights[0].at[pl.ds((half * n + m) * deep, deep)]
            copies.append(
                pltpu.make_async_copy(
                    source, weight_mem.at[half, rows, :], weight_sem.at[2 * m + half]
                )
            )

    def loads(m):
        return [
            pltpu.make_async_copy(blocks[m * 2 + side], block_mem.at[side, m], block_sem.at[m, side])
            for side in range(2)
        ]

    ahead = 2
    for copy in copies:
        copy.start()
    for m in range(ahead):
        for copy in loads(m):
            copy.start()
    for copy in copies:
        copy.wait()

    @pl.loop(0, n)
    def _(t):
        for m in range(ahead, n):

            @pl.when(t == m - ahead)
            def _():
                for copy in loads(m):
                    copy.start()

        for side in range(2):
            pltpu.make_async_copy(blocks[side], block_mem.at[side, t], block_sem.at[t, side]).wait()
        raw = jnp.dot(
            block_mem[0, t], weight_mem[col], preferred_element_type=jnp.float32
        ) + jnp.dot(
            block_mem[1, t],
            weight_mem[lax.bitwise_xor(col, 1)],
            preferred_element_type=jnp.float32,
        )
        at = lax.bitwise_xor(place, t)
        cosine_here, sine_here = cosine[at], sine[at]
        if heads == 0:
            kv_out, tail_out = refs[-6:-4]
            keys = normed_rotated(raw[:, :HD], gain[...], cosine_here, sine_here)
            keys = keys.astype(jnp.bfloat16)
            values = raw[:, HD:].astype(jnp.bfloat16)
            kv_out[at, :, :HD] = keys
            kv_out[at, :, HD:] = values

            @pl.when(at >= n - reach)
            def _():
                tail_out[at - (n - reach), :, :HD] = keys
                tail_out[at - (n - reach), :, HD:] = values

        q_out = refs[-5]
        for h in range(heads):
            query = normed_rotated(
                raw[:, h * HD : (h + 1) * HD], gain[...], cosine_here, sine_here
            )
            q_out[at, pl.ds(h * tokens, tokens), :] = query.astype(jnp.bfloat16)


def attend_kernel(low, count, reach, heads, meta, q_doc, k_doc, queries, kv_own, *refs):
    kv_back = refs[0] if low < reach else None
    keep_out, send_out = refs[-2:]
    col = meta[2]
    tokens = kv_own.shape[1]
    part = tokens // 2
    scale = 1.0 / math.sqrt(QUERY_SCALAR)
    row_at = lax.broadcasted_iota(jnp.int32, (tokens, tokens), 0)
    col_at = lax.broadcasted_iota(jnp.int32, (tokens, tokens), 1)

    for g in range(count):
        doc = q_doc[low + g]
        query = queries[low + g]
        totals = jnp.zeros((heads * tokens, 1), jnp.float32)
        mixed = jnp.zeros((heads * tokens, HD), jnp.float32)
        for step in range(reach + 1):
            at = low + g + step
            pair = kv_back[at] if at < reach else kv_own[at - reach]
            visible = doc == k_doc[at]
            if step == 0:
                visible = visible & (row_at < col_at)
            if step == reach:
                visible = visible & (row_at >= col_at)
            scores = lax.dot_general(
                query, pair[:, :HD], (((1,), (1,)), ((), ())), preferred_element_type=jnp.float32
            )
            weights_here = jnp.where(
                visible[None], jnp.exp(scores * scale).reshape(heads, tokens, tokens), 0.0
            ).reshape(heads * tokens, tokens)
            totals = totals + jnp.sum(weights_here, axis=-1, keepdims=True)
            mixed = mixed + jnp.dot(
                weights_here.astype(jnp.bfloat16), pair[:, HD:], preferred_element_type=jnp.float32
            )
        done = (mixed / totals).astype(jnp.bfloat16)
        for h in range(heads):
            top = done[h * tokens : h * tokens + part]
            bottom = done[h * tokens + part : (h + 1) * tokens]
            keep_out[g, :, h * HD : (h + 1) * HD] = jnp.where(col == 0, top, bottom)
            send_out[g, :, h * HD : (h + 1) * HD] = jnp.where(col == 0, bottom, top)


def output_kernel(n, size, meta, *refs):
    contexts, weights, after = refs[:n], refs[n : n + 8], refs[n + 8 : -5]
    out, context_mem, weight_mem, context_sem, weight_sem = refs[-5:]
    place, half, col = meta[0], meta[1], meta[2]
    rows_all, deep = weights[0].shape
    wide = contexts[0].shape[3]
    part = contexts[0].shape[2]
    copies = []
    for k, source in enumerate(weights):
        first = (half if k < 2 else lax.bitwise_xor(half, 1)) * rows_all
        first = first + sum(weights[j].shape[0] for j in range(2 + k % 2, k, 2))
        side = pl.multiple_of(lax.bitwise_xor(col, k % 2) * deep, 128)
        copies.append(
            pltpu.make_async_copy(
                source,
                weight_mem.at[
                    pl.ds(pl.multiple_of(first, 16), source.shape[0]), pl.ds(side, deep)
                ],
                weight_sem.at[k],
            )
        )
    for m in range(n):
        for side in range(2):
            first = lax.bitwise_xor(col, side) * deep + lax.bitwise_xor(place, m) * wide
            copies.append(
                pltpu.make_async_copy(
                    contexts[m].at[side],
                    context_mem.at[:, :, pl.ds(pl.multiple_of(first, 128), wide)],
                    context_sem.at[m * 2 + side],
                )
            )
    for copy in copies:
        copy.start()
    for copy in copies:
        copy.wait()
    result = lax.dot_general(
        weight_mem[...],
        context_mem[...].reshape(size * part, 2 * deep),
        (((1,), (1,)), ((), ())),
        preferred_element_type=jnp.float32,
    ).astype(jnp.bfloat16)
    for k in range(size):
        for block in range(2):
            out[2 * k + block] = result[
                block * rows_all : (block + 1) * rows_all, k * part : (k + 1) * part
            ]
    if after:
        out[2 * size :] = after[0][...]


def close_kernel(n, activations, arrived, out):
    _, _, part = arrived.shape
    for col in range(2):
        rows = pl.ds(col * part, part)
        whole = jnp.concatenate([arrived[2 * p + col] for p in range(n)], axis=0)
        out[rows, :] = (
            activations[rows, :].astype(jnp.float32) + whole.astype(jnp.float32).T
        ).astype(jnp.bfloat16)


def split_body(
    activations,
    positions,
    query_weight,
    key_weight,
    value_weight,
    output_weight,
    input_gain,
    query_gain,
    key_gain,
):
    tokens, features = activations.shape
    n = key_weight.shape[1] // HD
    heads = query_weight.shape[1] // key_weight.shape[1]
    reach = WINDOW // tokens
    part = tokens // 2
    half, place, col = lax.axis_index("half"), lax.axis_index("place"), lax.axis_index("cols")
    meta = jnp.stack([place, half, col]).astype(jnp.int32)
    bf16, f32 = jnp.bfloat16, jnp.float32
    shaped = jax.ShapeDtypeStruct

    deep = query_weight.shape[0]
    kv_cut, *cut = run(
        functools.partial(cut_kernel, n),
        [shaped((deep, n * 2 * HD), bf16)] + [shaped((deep, heads * HD), bf16)] * n,
        [SMEM, VMEM, VMEM, VMEM],
        [VMEM] * (n + 1),
        [],
        0,
        4 * query_weight.size * 2,
    )(meta, query_weight, key_weight, value_weight)
    kv_rows = lax.all_gather(kv_cut, "half", axis=0, tiled=True)

    wide = activations.astype(f32)
    squares = jnp.sum(wide * wide, axis=-1).reshape(2, part)
    squares = (squares + swapped(squares, 0, 1)).reshape(tokens, 1)
    inverse = lax.rsqrt(squares / (2 * features) + 1e-06)
    gain = lax.dynamic_slice_in_dim(input_gain, col * features, features, 0)
    normed = (wide * inverse * gain).astype(bf16)

    z, y, c = n // 2, n // 4, 1
    blocks = {(0, 0): normed}
    blocks[y, 0] = swapped(normed, y, 0)
    blocks[0, 1] = swapped(normed, 0, 1)
    blocks[z, 0] = swapped(normed, z, 0)
    blocks[y, 1] = swapped(blocks[y, 0], 0, 1)
    blocks[z, 1] = swapped(blocks[z, 0], 0, 1)
    blocks[z + y, 0] = swapped(blocks[z, 0], y, 0)
    blocks[z + y, 1] = swapped(blocks[z + y, 0], 0, 1)
    for m, side in list(blocks):
        blocks[m + c, side] = swapped(blocks[m, side], c, 0)
    block_list = [blocks[m, side] for m in range(n) for side in range(2)]

    in_half = lax.dynamic_slice_in_dim(positions, half * n * tokens, n * tokens, 0)
    frequency = 10000.0 ** (-(jnp.arange(HD // 2, dtype=f32) * 2.0 / HD))
    angles = in_half.astype(f32)[:, None] * frequency[None, :]
    cosine, sine = jnp.cos(angles), jnp.sin(angles)
    cosine = jnp.concatenate([cosine, cosine], -1).reshape(n, tokens, HD)
    sine = jnp.concatenate([-sine, sine], -1).reshape(n, tokens, HD)
    index = jnp.arange(positions.shape[0], dtype=jnp.int32)
    starts = jnp.concatenate(
        [jnp.full((reach * tokens,), -(2**30), jnp.int32), index - positions], 0
    )
    docs = lax.dynamic_slice_in_dim(starts, half * n * tokens, (n + reach) * tokens, 0)
    k_doc = docs.reshape(n + reach, 1, tokens)
    q_doc = docs[reach * tokens :].reshape(n, tokens, 1)

    near = [cut[0]] + [swapped(cut[m], m, 0) for m in range(1, n)]
    q_own = run(
        join_kernel,
        shaped((n * deep, heads * HD), bf16),
        [VMEM] * n,
        VMEM,
        [],
        0,
        4 * n * deep * heads * HD,
    )(*near)
    q_rows = lax.all_gather(q_own, "half", axis=0, tiled=True)
    kv_rows, cosine, sine, q_doc = lax.optimization_barrier((kv_rows, cosine, sine, q_doc))
    kv_parts = []
    for m in range(n):
        first = lax.bitwise_xor(place, m) * 2 * HD
        piece = lax.dynamic_slice_in_dim(kv_rows, first, 2 * HD, 1)
        kv_parts.append(piece if m == 0 else swapped(piece, m, 0))

    def project(kept, gain, weights, outs):
        return run(
            functools.partial(project_kernel, n, reach, kept),
            outs,
            [SMEM, VMEM, VMEM, VMEM] + [ANY] * (2 * n + len(weights)),
            [VMEM] * len(outs),
            [
                pltpu.VMEM((2, n, tokens, features), bf16),
                pltpu.VMEM((2, features, (kept or 2) * HD), bf16),
                pltpu.SemaphoreType.DMA((n, 2)),
                pltpu.SemaphoreType.DMA((2 * n,)),
            ],
            2 * n * tokens * 2 * features * (kept or 2) * HD,
            2 * n * tokens * features * 2,
        )(meta, cosine, sine, gain.reshape(1, HD), *block_list, *weights)

    kv_own, kv_tail = project(
        0,
        key_gain,
        kv_parts,
        [shaped((n, tokens, 2 * HD), bf16), shaped((reach, tokens, 2 * HD), bf16)],
    )
    kv_back = lax.ppermute(kv_tail, "half", [(0, 1)])
    queries = project(heads, query_gain, [q_rows], [shaped((n, heads * tokens, HD), bf16)])[0]

    own_weight, _ = lax.optimization_barrier((output_weight.T, q_own))
    rows_all = own_weight.shape[0]
    step = rows_all * 8 // 21 // 16 * 16
    cuts = [0, rows_all - 2 * step, rows_all - step, rows_all]
    out_weights = [own_weight, swapped(own_weight, 0, 1)]
    for k in range(3):
        piece = own_weight[cuts[k] : cuts[k + 1]]
        if k == 0:
            piece = lax.ppermute(piece, "half", [(0, 1), (1, 0)])
        else:
            both = lax.all_gather(piece, "half", axis=0)
            piece = lax.dynamic_index_in_dim(both, 1 - half, 0, keepdims=False)
        out_weights += [piece, swapped(piece, 0, 1)]

    contexts = []
    spans = [(reach, n - reach), (0, reach)]
    for low, count in spans:
        backs = [kv_back] if low < reach else []
        shape = shaped((count, part, heads * HD), bf16)
        keep, send = run(
            functools.partial(attend_kernel, low, count, reach, heads),
            [shape, shape],
            [SMEM] + [VMEM] * (4 + len(backs)),
            [VMEM, VMEM],
            [],
            8 * count * heads * tokens * (reach + 1) * tokens * HD,
            4 * n * tokens * 2 * HD,
        )(meta, q_doc, k_doc, queries, kv_own, *backs)
        there = swapped(send, 0, 1)
        pair = run(
            pair_kernel,
            shaped((2, count, part, heads * HD), bf16),
            [VMEM, VMEM],
            VMEM,
            [],
            0,
            8 * count * part * heads * HD,
        )(keep, there)
        pairs = {0: pair}
        pairs[z] = swapped(pair, z, 0)
        pairs[y] = swapped(pair, y, 0)
        pairs[z + y] = swapped(pairs[z], y, 0)
        for m in list(pairs):
            pairs[m + c] = swapped(pairs[m], c, 0)
        contexts.append([pairs[m] for m in range(n)])

    out_cols = output_weight.shape[1]
    deep_out = output_weight.shape[0]
    result = []
    for s, (low, count) in enumerate(spans):
        blocks_out = 2 * count + sum(r.shape[0] for r in result)
        result = [
            run(
                functools.partial(output_kernel, n, count),
                shaped((blocks_out, out_cols, part), bf16),
                [SMEM] + [ANY] * (n + 8) + [VMEM] * len(result),
                VMEM,
                [
                    pltpu.VMEM((count, part, 2 * deep_out), bf16),
                    pltpu.VMEM((2 * out_cols, 2 * deep_out), bf16),
                    pltpu.SemaphoreType.DMA((2 * n,)),
                    pltpu.SemaphoreType.DMA((8,)),
                ],
                8 * count * part * deep_out * out_cols,
                8 * deep_out * out_cols,
            )(meta, *contexts[s], *out_weights, *result)
        ]

    arrived = lax.all_to_all(result[0], ("place", "cols"), 0, 0, tiled=True)
    return run(
        functools.partial(close_kernel, n),
        shaped((tokens, features), bf16),
        [VMEM, VMEM],
        VMEM,
        [],
        0,
        6 * tokens * features,
    )(activations, arrived)


def solution(mesh):
    sizes = mesh.shape
    if sizes["cols"] == 2 and sizes["sub"] == 1 and sizes["rows"] == 16:
        shape = (sizes["groups"], 2, sizes["rows"] // 2, sizes["cols"], sizes["sub"])
        names = ("groups", "half", "place", "cols", "sub")
        fine, rows = Mesh(mesh.devices.reshape(shape), names), ("half", "place")
    else:
        fine, rows = mesh, ("rows",)
    columns = ("cols", "sub")
    placed = (
        P(("groups", *rows), columns),
        P("groups"),
        P(rows, columns),
        P(rows, columns),
        P(rows, columns),
        P(columns, rows),
        P(),
        P(),
        P(),
    )

    def mapped(body):
        return jax.shard_map(
            body, mesh=fine, in_specs=placed, out_specs=placed[0], check_vma=False
        )

    if fine is mesh:
        return mapped(gathered_body)

    return mapped(split_body)
```

```python
import functools
import math

import jax
import jax.numpy as jnp
from jax import lax
from jax.experimental import pallas as pl
from jax.experimental.pallas import tpu as pltpu
from jax.sharding import Mesh
from jax.sharding import PartitionSpec as P


HD = 128
WINDOW = 1024
QUERY_SCALAR = 168
VMEM_BYTES = 67_000_000
ANY = pl.BlockSpec(memory_space=pl.ANY)
VMEM = pl.BlockSpec(memory_space=pltpu.VMEM)
SMEM = pl.BlockSpec(memory_space=pltpu.SMEM)


def passed_along(value, axis, by):
    peers = lax.axis_size(axis)
    pairs = [(i, i + by) for i in range(peers) if 0 <= i + by < peers]
    return lax.ppermute(value, axis, pairs)


def head_norm(tensor, gain_vector):
    return (
        tensor * lax.rsqrt(jnp.mean(tensor * tensor, axis=-1, keepdims=True) + 1e-06) * gain_vector
    )


def rotate(tensor, token_positions):
    half_width = tensor.shape[-1] // 2
    frequency = 10000.0 ** (-(jnp.arange(half_width, dtype=jnp.float32) * 2.0 / tensor.shape[-1]))
    angles = token_positions.astype(jnp.float32)[:, None] * frequency[None, :]
    cosine = jnp.cos(angles)[:, None, :]
    sine_part = jnp.sin(angles)[:, None, :]
    first_half = tensor[..., :half_width]
    second_half = tensor[..., half_width:]
    return jnp.concatenate(
        [
            first_half * cosine - second_half * sine_part,
            second_half * cosine + first_half * sine_part,
        ],
        axis=-1,
    )


def attend(queries, key_rows, value_rows, query_index, key_index, query_pos, key_pos):
    row_count = queries.shape[0]
    key_count = key_rows.shape[0]
    kv_heads = key_rows.shape[1] // HD
    group_size = queries.shape[1] // key_rows.shape[1]
    query_four = queries.reshape(row_count, kv_heads, group_size, HD)
    key_three = key_rows.reshape(key_count, kv_heads, HD)
    value_three = value_rows.reshape(key_count, kv_heads, HD)
    score_scale = 1.0 / math.sqrt(QUERY_SCALAR)
    scores = (
        jnp.einsum("qgrd,kgd->grqk", query_four, key_three, preferred_element_type=jnp.float32)
        * score_scale
    )
    distance = query_index[:, None] - key_index[None, :]
    visible = (
        (key_index[None, :] >= 0)
        & (distance >= 0)
        & (distance < WINDOW)
        & (query_pos[:, None] - key_pos[None, :] == distance)
    )
    weights = jnp.where(visible[None, None], jnp.exp(scores), 0.0)
    totals = jnp.sum(weights, axis=-1)
    rounded = weights.astype(jnp.bfloat16)
    mixed_heads = jnp.einsum(
        "grqk,kgd->qgrd", rounded, value_three, preferred_element_type=jnp.float32
    )
    mixed_heads = mixed_heads / jnp.transpose(totals, (2, 0, 1))[..., None]
    return mixed_heads.astype(jnp.bfloat16).reshape(row_count, kv_heads * group_size * HD)


def reach_back(key_rows, value_rows, reach_rows):
    pieces = []
    carried = (key_rows, value_rows)
    for _ in range(reach_rows):
        carried = passed_along((carried[0], carried[1]), "rows", 1)
        pieces.append(carried)
    ordered = pieces[::-1] + [(key_rows, value_rows)]
    all_keys = jnp.concatenate([member[0] for member in ordered], axis=0)
    all_values = jnp.concatenate([member[1] for member in ordered], axis=0)
    return (all_keys, all_values)


def gathered_body(
    activations,
    positions,
    query_weight,
    key_weight,
    value_weight,
    output_weight,
    input_gain,
    query_gain,
    key_gain,
):
    rows_here = activations.shape[0]
    row_panel = lax.all_gather(activations, ("cols", "sub"), axis=1, tiled=True)
    panel_wide = row_panel.astype(jnp.float32)
    inverse = lax.rsqrt(jnp.mean(panel_wide * panel_wide, axis=-1, keepdims=True) + 1e-06)
    normed = (panel_wide * inverse * input_gain).astype(jnp.bfloat16)
    row_index = lax.axis_index("rows")
    own_positions = lax.dynamic_slice_in_dim(positions, row_index * rows_here, rows_here, 0)
    reach_rows = min(-(-WINDOW // rows_here), lax.axis_size("rows") - 1)

    def add_rows(weight_piece):
        return jnp.dot(normed, weight_piece, preferred_element_type=jnp.float32)

    query_raw = add_rows(lax.all_gather(query_weight, "rows", axis=0, tiled=True))
    key_raw = add_rows(lax.all_gather(key_weight, "rows", axis=0, tiled=True))
    value_raw = add_rows(lax.all_gather(value_weight, "rows", axis=0, tiled=True))
    key_rows = rotate(head_norm(key_raw.reshape(rows_here, -1, HD), key_gain), own_positions)
    key_rows, value_rows = (
        key_rows.astype(jnp.bfloat16).reshape(rows_here, -1),
        value_raw.astype(jnp.bfloat16),
    )
    all_keys, all_values = reach_back(key_rows, value_rows, reach_rows)
    queries = rotate(head_norm(query_raw.reshape(rows_here, -1, HD), query_gain), own_positions)
    queries = queries.astype(jnp.bfloat16).reshape(rows_here, -1)
    key_count = all_keys.shape[0]
    query_index = row_index * rows_here + jnp.arange(rows_here, dtype=jnp.int32)
    key_index = (row_index - reach_rows) * rows_here + jnp.arange(key_count, dtype=jnp.int32)
    padded = jnp.concatenate([jnp.zeros((reach_rows * rows_here,), jnp.int32), positions], axis=0)
    key_positions = lax.dynamic_slice_in_dim(padded, row_index * rows_here, key_count, 0)
    context = attend(
        queries, all_keys, all_values, query_index, key_index, own_positions, key_positions
    )
    partial_terms = jnp.dot(
        context,
        lax.all_gather(output_weight, "rows", axis=1, tiled=True),
        preferred_element_type=jnp.float32,
    )
    summed = lax.psum_scatter(
        partial_terms.astype(jnp.bfloat16), ("cols", "sub"), scatter_dimension=1, tiled=True
    ).astype(jnp.float32)
    return (activations.astype(jnp.float32) + summed).astype(jnp.bfloat16)


def swapped(value, place=0, col=0):
    places, cols = lax.axis_size("place"), lax.axis_size("cols")
    pairs = [
        (r * cols + c, (r ^ place) * cols + (c ^ col)) for r in range(places) for c in range(cols)
    ]
    return lax.ppermute(value, ("place", "cols"), pairs)


def run(kernel, out_shape, in_specs, out_specs, scratch, flops, bytes_moved):
    return pl.pallas_call(
        kernel,
        out_shape=out_shape,
        in_specs=in_specs,
        out_specs=out_specs,
        scratch_shapes=scratch,
        compiler_params=pltpu.CompilerParams(vmem_limit_bytes=VMEM_BYTES),
        cost_estimate=pl.CostEstimate(
            flops=int(flops), bytes_accessed=int(bytes_moved), transcendentals=0
        ),
    )


def cut_kv_kernel(n, wk, wv, kv_out):
    for p in range(n):
        kv_out[:, p * 2 * HD : p * 2 * HD + HD] = wk[:, p * HD : (p + 1) * HD]
        kv_out[:, p * 2 * HD + HD : (p + 1) * 2 * HD] = wv[:, p * HD : (p + 1) * HD]


def cut_kernel(n, meta, wq, *q_outs):
    place = meta[0]
    wide = wq.shape[1] // n
    for m in range(n):
        at = lax.bitwise_xor(place, m)
        q_outs[m][...] = wq[:, pl.ds(pl.multiple_of(at * wide, 128), wide)]


def join_kernel(*refs):
    out = refs[-1]
    deep = refs[0].shape[0]
    for m, piece in enumerate(refs[:-1]):
        out[m * deep : (m + 1) * deep] = piece[...]


def pair_kernel(first, second, out):
    out[0] = first[...]
    out[1] = second[...]


def normed_rotated(raw, gain, cosine, sine):
    scaled = raw * lax.rsqrt(jnp.mean(raw * raw, axis=-1, keepdims=True) + 1e-06) * gain
    return scaled * cosine + pltpu.roll(scaled, HD // 2, 1) * sine


def project_kernel(n, reach, heads, meta, cosine, sine, key_gain, query_gain, *refs):
    blocks, kv_parts = refs[: 2 * n], refs[2 * n : 3 * n]
    q_rows = refs[3 * n]
    kv_out, tail_out, q_out = refs[3 * n + 1 : 3 * n + 4]
    block_mem, kv_mem, q_mem, block_sem, weight_sem = refs[3 * n + 4 :]
    place, col = meta[0], meta[2]
    _, _, tokens, _ = block_mem.shape
    deep = kv_parts[0].shape[0] // 2
    copies = []
    for m in range(n):
        rows = pl.ds(pl.multiple_of(lax.bitwise_xor(place, m) * deep, 16), deep)
        for half in range(2):
            for k, (source, target) in enumerate(
                [
                    (kv_parts[m].at[pl.ds(half * deep, deep)], kv_mem.at[half, rows, :]),
                    (q_rows.at[pl.ds((half * n + m) * deep, deep)], q_mem.at[half, rows, :]),
                ]
            ):
                sem = weight_sem.at[4 * m + 2 * half + k]
                copies.append(pltpu.make_async_copy(source, target, sem))

    def loads(m):
        return [
            pltpu.make_async_copy(blocks[m * 2 + side], block_mem.at[side, m], block_sem.at[m, side])
            for side in range(2)
        ]

    ahead = 1
    for copy in copies:
        copy.start()
    for m in range(ahead):
        for copy in loads(m):
            copy.start()
    for copy in copies:
        copy.wait()

    @pl.loop(0, n)
    def _(t):
        for m in range(ahead, n):

            @pl.when(t == m - ahead)
            def _():
                for copy in loads(m):
                    copy.start()

        for side in range(2):
            pltpu.make_async_copy(blocks[side], block_mem.at[side, t], block_sem.at[t, side]).wait()
        kv, q = [
            jnp.dot(block_mem[0, t], mem[col], preferred_element_type=jnp.float32)
            + jnp.dot(
                block_mem[1, t],
                mem[lax.bitwise_xor(col, 1)],
                preferred_element_type=jnp.float32,
            )
            for mem in (kv_mem, q_mem)
        ]
        at = lax.bitwise_xor(place, t)
        cosine_here, sine_here = cosine[at], sine[at]
        keys = normed_rotated(kv[:, :HD], key_gain[...], cosine_here, sine_here)
        keys = keys.astype(jnp.bfloat16)
        values = kv[:, HD : 2 * HD].astype(jnp.bfloat16)
        kv_out[at, :, :HD] = keys
        kv_out[at, :, HD:] = values
        for h in range(heads):
            query = normed_rotated(
                q[:, h * HD : (h + 1) * HD], query_gain[...], cosine_here, sine_here
            )
            q_out[at, pl.ds(h * tokens, tokens), :] = query.astype(jnp.bfloat16)

        @pl.when(at >= n - reach)
        def _():
            tail_out[at - (n - reach), :, :HD] = keys
            tail_out[at - (n - reach), :, HD:] = values


def attend_kernel(low, count, reach, heads, meta, q_doc, k_doc, queries, kv_own, *refs):
    kv_back = refs[0] if low < reach else None
    keep_out, send_out = refs[-2:]
    col = meta[2]
    tokens = kv_own.shape[1]
    part = tokens // 2
    scale = 1.0 / math.sqrt(QUERY_SCALAR)
    row_at = lax.broadcasted_iota(jnp.int32, (tokens, tokens), 0)
    col_at = lax.broadcasted_iota(jnp.int32, (tokens, tokens), 1)

    for g in range(count):
        doc = q_doc[low + g]
        query = queries[low + g]
        totals = jnp.zeros((heads * tokens, 1), jnp.float32)
        mixed = jnp.zeros((heads * tokens, HD), jnp.float32)
        for step in range(reach + 1):
            at = low + g + step
            pair = kv_back[at] if at < reach else kv_own[at - reach]
            visible = doc == k_doc[at]
            if step == 0:
                visible = visible & (row_at < col_at)
            if step == reach:
                visible = visible & (row_at >= col_at)
            scores = lax.dot_general(
                query, pair[:, :HD], (((1,), (1,)), ((), ())), preferred_element_type=jnp.float32
            )
            weights_here = jnp.where(
                visible[None], jnp.exp(scores * scale).reshape(heads, tokens, tokens), 0.0
            ).reshape(heads * tokens, tokens)
            totals = totals + jnp.sum(weights_here, axis=-1, keepdims=True)
            mixed = mixed + jnp.dot(
                weights_here.astype(jnp.bfloat16), pair[:, HD:], preferred_element_type=jnp.float32
            )
        done = (mixed / totals).astype(jnp.bfloat16)
        for h in range(heads):
            top = done[h * tokens : h * tokens + part]
            bottom = done[h * tokens + part : (h + 1) * tokens]
            keep_out[g, :, h * HD : (h + 1) * HD] = jnp.where(col == 0, top, bottom)
            send_out[g, :, h * HD : (h + 1) * HD] = jnp.where(col == 0, bottom, top)


def output_kernel(n, low, size, meta, *refs):
    last = low is not None
    groups = 2 if last else 1
    contexts, rest = refs[: groups * n], refs[groups * n : -6]
    weights, early = (rest[:-1], rest[-1]) if last else (rest, None)
    out, context_mem, weight_mem, result_mem, context_sem, weight_sem = refs[-6:]
    place, half, col = meta[0], meta[1], meta[2]
    deep = weights[0].shape[1]
    wide = contexts[0].shape[3]
    part = contexts[0].shape[2]
    starts = [0]
    for source in weights[::2]:
        starts.append(starts[-1] + source.shape[0])
    copies = []
    for side in range(2):
        base = lax.bitwise_xor(col, side) * deep
        copies.append([])
        for k, source in enumerate(weights[side::2]):
            copies[side].append(
                pltpu.make_async_copy(
                    source,
                    weight_mem.at[side, pl.ds(starts[k], source.shape[0]), :],
                    weight_sem.at[2 * k + side],
                )
            )
        for g in range(groups):
            for m in range(n):
                first = pl.multiple_of(lax.bitwise_xor(place, m) * wide, 128)
                copies[side].append(
                    pltpu.make_async_copy(
                        contexts[g * n + m].at[side],
                        context_mem.at[side, g, :, :, pl.ds(first, wide)],
                        context_sem.at[(g * n + m) * 2 + side],
                    )
                )
    for copy in copies[0]:
        copy.start()
    for side in range(2):
        for copy in copies[side]:
            copy.wait()
        if side == 0:
            for copy in copies[1]:
                copy.start()
        for g in range(groups):
            rows = slice(starts[-2] if g == 1 else 0, starts[-1])
            product = lax.dot_general(
                weight_mem[side, rows],
                context_mem[side, g].reshape(size * part, deep),
                (((1,), (1,)), ((), ())),
                preferred_element_type=jnp.float32,
            )
            if side == 0:
                result_mem[g, rows] = product
            else:
                result_mem[g, rows] += product
    for k in range(size):
        tokens = slice(k * part, (k + 1) * part)
        if not last:
            out[k] = result_mem[0, :, tokens].astype(jnp.bfloat16)
            continue
        near, far = half, lax.bitwise_xor(half, 1)
        out[2 * k + near] = result_mem[0, : starts[1], tokens].astype(jnp.bfloat16)
        out[2 * k + far] = result_mem[0, starts[1] :, tokens].astype(jnp.bfloat16)
        at = 2 * (low + k)
        out[at + near] = early[k, : starts[1]]
        edge = starts[-2] - starts[1]
        out[at + far, :edge] = early[k, starts[1] :]
        out[at + far, edge:] = result_mem[1, starts[-2] :, tokens].astype(jnp.bfloat16)


def close_kernel(n, activations, arrived, out):
    _, _, part = arrived.shape
    for col in range(2):
        rows = pl.ds(col * part, part)
        whole = jnp.concatenate([arrived[2 * p + col] for p in range(n)], axis=0)
        out[rows, :] = (
            activations[rows, :].astype(jnp.float32) + whole.T.astype(jnp.float32)
        ).astype(jnp.bfloat16)


def split_body(
    activations,
    positions,
    query_weight,
    key_weight,
    value_weight,
    output_weight,
    input_gain,
    query_gain,
    key_gain,
):
    tokens, features = activations.shape
    n = key_weight.shape[1] // HD
    heads = query_weight.shape[1] // key_weight.shape[1]
    reach = WINDOW // tokens
    part = tokens // 2
    half, place, col = lax.axis_index("half"), lax.axis_index("place"), lax.axis_index("cols")
    meta = jnp.stack([place, half, col]).astype(jnp.int32)
    bf16, f32 = jnp.bfloat16, jnp.float32
    shaped = jax.ShapeDtypeStruct

    deep = query_weight.shape[0]
    kv_cut = run(
        functools.partial(cut_kv_kernel, n),
        shaped((deep, n * 2 * HD), bf16),
        [VMEM, VMEM],
        VMEM,
        [],
        0,
        2 * query_weight.size * 2,
    )(key_weight, value_weight)
    cut = run(
        functools.partial(cut_kernel, n),
        [shaped((deep, heads * HD), bf16)] * n,
        [SMEM, VMEM],
        [VMEM] * n,
        [],
        0,
        2 * query_weight.size * 2,
    )(meta, query_weight)
    kv_rows = lax.all_gather(kv_cut, "half", axis=0, tiled=True)

    wide = activations.astype(f32)
    squares = jnp.sum(wide * wide, axis=-1).reshape(2, part)
    squares = (squares + swapped(squares, 0, 1)).reshape(tokens, 1)
    inverse = lax.rsqrt(squares / (2 * features) + 1e-06)
    gain = lax.dynamic_slice_in_dim(input_gain, col * features, features, 0)
    normed = (wide * inverse * gain).astype(bf16)

    z, y, c = n // 2, n // 4, 1
    blocks = {(0, 0): normed}
    blocks[y, 0] = swapped(normed, y, 0)
    blocks[0, 1] = swapped(normed, 0, 1)
    blocks[z, 0] = swapped(normed, z, 0)
    blocks[y, 1] = swapped(blocks[y, 0], 0, 1)
    blocks[z, 1] = swapped(blocks[z, 0], 0, 1)
    blocks[z + y, 0] = swapped(blocks[z, 0], y, 0)
    blocks[z + y, 1] = swapped(blocks[z + y, 0], 0, 1)
    for m, side in list(blocks):
        blocks[m + c, side] = swapped(blocks[m, side], c, 0)
    block_list = [blocks[m, side] for m in range(n) for side in range(2)]

    in_half = lax.dynamic_slice_in_dim(positions, half * n * tokens, n * tokens, 0)
    frequency = 10000.0 ** (-(jnp.arange(HD // 2, dtype=f32) * 2.0 / HD))
    angles = in_half.astype(f32)[:, None] * frequency[None, :]
    cosine, sine = jnp.cos(angles), jnp.sin(angles)
    cosine = jnp.concatenate([cosine, cosine], -1).reshape(n, tokens, HD)
    sine = jnp.concatenate([-sine, sine], -1).reshape(n, tokens, HD)
    index = jnp.arange(positions.shape[0], dtype=jnp.int32)
    starts = jnp.concatenate(
        [jnp.full((reach * tokens,), -(2**30), jnp.int32), index - positions], 0
    )
    docs = lax.dynamic_slice_in_dim(starts, half * n * tokens, (n + reach) * tokens, 0)
    k_doc = docs.reshape(n + reach, 1, tokens)
    q_doc = docs[reach * tokens :].reshape(n, tokens, 1)

    near = [cut[0]] + [swapped(cut[m], m, 0) for m in range(1, n)]
    q_own = run(
        join_kernel,
        shaped((n * deep, heads * HD), bf16),
        [VMEM] * n,
        VMEM,
        [],
        0,
        4 * n * deep * heads * HD,
    )(*near)
    q_rows = lax.all_gather(q_own, "half", axis=0, tiled=True)
    kv_rows, cosine, sine, q_doc = lax.optimization_barrier((kv_rows, cosine, sine, q_doc))
    kv_parts = []
    for m in range(n):
        first = lax.bitwise_xor(place, m) * 2 * HD
        piece = lax.dynamic_slice_in_dim(kv_rows, first, 2 * HD, 1)
        kv_parts.append(piece if m == 0 else swapped(piece, m, 0))

    flops = 2 * n * tokens * 2 * features * (2 + heads) * HD
    kv_own, kv_tail, queries = run(
        functools.partial(project_kernel, n, reach, heads),
        [
            shaped((n, tokens, 2 * HD), bf16),
            shaped((reach, tokens, 2 * HD), bf16),
            shaped((n, heads * tokens, HD), bf16),
        ],
        [SMEM, VMEM, VMEM, VMEM, VMEM] + [ANY] * (3 * n + 1),
        [VMEM, VMEM, VMEM],
        [
            pltpu.VMEM((2, n, tokens, features), bf16),
            pltpu.VMEM((2, features, 2 * HD), bf16),
            pltpu.VMEM((2, features, heads * HD), bf16),
            pltpu.SemaphoreType.DMA((n, 2)),
            pltpu.SemaphoreType.DMA((4 * n,)),
        ],
        flops,
        2 * n * tokens * features * 2,
    )(
        meta,
        cosine,
        sine,
        key_gain.reshape(1, HD),
        query_gain.reshape(1, HD),
        *block_list,
        *kv_parts,
        q_rows,
    )
    kv_back = lax.ppermute(kv_tail, "half", [(0, 1)])

    own_weight, _ = lax.optimization_barrier((output_weight.T, q_own))
    ahead = own_weight.shape[0] * 4 // 7 // 16 * 16
    out_weights = [own_weight, swapped(own_weight, 0, 1)]
    for rows in [own_weight[:ahead], own_weight[ahead:]]:
        both = lax.all_gather(rows, "half", axis=0)
        piece = lax.dynamic_index_in_dim(both, 1 - half, 0, keepdims=False)
        out_weights += [piece, swapped(piece, 0, 1)]

    contexts = []
    spans = [(reach, n - reach), (0, reach)]
    for low, count in spans:
        backs = [kv_back] if low < reach else []
        shape = shaped((count, part, heads * HD), bf16)
        keep, send = run(
            functools.partial(attend_kernel, low, count, reach, heads),
            [shape, shape],
            [SMEM] + [VMEM] * (4 + len(backs)),
            [VMEM, VMEM],
            [],
            8 * count * heads * tokens * (reach + 1) * tokens * HD,
            4 * n * tokens * 2 * HD,
        )(meta, q_doc, k_doc, queries, kv_own, *backs)
        there = swapped(send, 0, 1)
        pair = run(
            pair_kernel,
            shaped((2, count, part, heads * HD), bf16),
            [VMEM, VMEM],
            VMEM,
            [],
            0,
            8 * count * part * heads * HD,
        )(keep, there)
        pairs = {0: pair}
        pairs[z] = swapped(pair, z, 0)
        pairs[y] = swapped(pair, y, 0)
        pairs[z + y] = swapped(pairs[z], y, 0)
        for m in list(pairs):
            pairs[m + c] = swapped(pairs[m], c, 0)
        contexts.append([pairs[m] for m in range(n)])

    out_cols = output_weight.shape[1]
    deep_out = output_weight.shape[0]
    count = reach
    all_rows = sum(w.shape[0] for w in out_weights[::2])
    early_rows = all_rows - out_weights[-1].shape[0]

    def project_out(low, groups, weights, early, shape, rows):
        return run(
            functools.partial(output_kernel, n, low, count),
            shaped(shape, bf16),
            [SMEM] + [ANY] * (len(groups) * n + len(weights)) + [VMEM] * len(early),
            VMEM,
            [
                pltpu.VMEM((2, len(groups), count, part, deep_out), bf16),
                pltpu.VMEM((2, rows, deep_out), bf16),
                pltpu.VMEM((len(groups), rows, count * part), f32),
                pltpu.SemaphoreType.DMA((2 * n * len(groups),)),
                pltpu.SemaphoreType.DMA((len(weights),)),
            ],
            4 * rows * count * part * deep_out,
            4 * rows * deep_out,
        )(meta, *[c for g in groups for c in g], *weights, *early)

    early = project_out(
        None, contexts[:1], out_weights[:-2], [], (count, early_rows, part), early_rows
    )
    result = project_out(
        reach, [contexts[1], contexts[0]], out_weights, [early], (2 * n, out_cols, part), all_rows
    )

    arrived = lax.all_to_all(result, ("place", "cols"), 0, 0, tiled=True)
    return run(
        functools.partial(close_kernel, n),
        shaped((tokens, features), bf16),
        [VMEM, VMEM],
        VMEM,
        [],
        0,
        6 * tokens * features,
    )(activations, arrived)


def solution(mesh):
    sizes = mesh.shape
    if sizes["cols"] == 2 and sizes["sub"] == 1 and sizes["rows"] == 16:
        shape = (sizes["groups"], 2, sizes["rows"] // 2, sizes["cols"], sizes["sub"])
        names = ("groups", "half", "place", "cols", "sub")
        fine, rows = Mesh(mesh.devices.reshape(shape), names), ("half", "place")
    else:
        fine, rows = mesh, ("rows",)
    columns = ("cols", "sub")
    placed = (
        P(("groups", *rows), columns),
        P("groups"),
        P(rows, columns),
        P(rows, columns),
        P(rows, columns),
        P(columns, rows),
        P(),
        P(),
        P(),
    )

    def mapped(body):
        return jax.shard_map(
            body, mesh=fine, in_specs=placed, out_specs=placed[0], check_vma=False
        )

    if fine is mesh:
        return mapped(gathered_body)

    return mapped(split_body)
```
